32 devices in a mesh: dp: 16 (over z, x, core), seq: 2 (over y).
Axes of the slice: x: 2, y: 2, z: 4, core: 2. Of those that a mesh axis runs over, the one named last changes fastest.
Arguments:
- block_input: bfloat16 [16, 2048, 768], P('dp', 'seq'), may hold values from -6 to 6
- cotangent: bfloat16 [16, 2048, 768], P('dp', 'seq'), may hold values from -6 to 6
- in_weight: float32 [768, 3328], P('dp'), may hold values from -0.21875 to 0.21875
- dt_weight: float32 [768, 24], P('dp'), may hold values from -0.21875 to 0.21875
- out_weight: float32 [1536, 768], P('dp'), may hold values from -0.15625 to 0.15625
- norm_gain: float32 [768], replicated, may hold values from 0.5 to 1.5
- conv_weight: float32 [4, 1792], replicated, may hold values from -3 to 3
- conv_bias: float32 [1792], replicated, may hold values from -1.5 to 1.5
- dt_bias: float32 [24], replicated, may hold values from -6.9 to -2.25
- decay_log: float32 [24], replicated, may hold values from 0 to 2.5
- skip_gain: float32 [24], replicated, may hold values from 0.5 to 1.5
- gate_gain: float32 [1536], replicated, may hold values from 0.5 to 1.5
- in_left: float32 [32, 26, 24, 24], P('dp'), as said below
- in_right: float32 [32, 26, 128, 128], P('dp'), as said below
- in_left_root: float32 [32, 26, 24, 24], P('dp'), as said below
- in_right_root: float32 [32, 26, 128, 128], P('dp'), as said below
- dt_left: float32 [32, 24, 24], P('dp'), as said below
- dt_right: float32 [32, 24, 24], P('dp'), as said below
- dt_left_root: float32 [32, 24, 24], P('dp'), as said below
- dt_right_root: float32 [32, 24, 24], P('dp'), as said below
- out_left: float32 [64, 6, 24, 24], P('dp'), as said below
- out_right: float32 [64, 6, 128, 128], P('dp'), as said below
- out_left_root: float32 [64, 6, 24, 24], P('dp'), as said below
- out_right_root: float32 [64, 6, 128, 128], P('dp'), as said below
- vector_moment: float32 [11336], replicated, may hold values from 1638.4 to 65536
Outputs:
- block_output: bfloat16 [16, 2048, 768], P('dp', 'seq')
- input_grad: float32 [16, 2048, 768], P('dp', 'seq')
- in_grad: float32 [768, 3328], P('dp')
- dt_grad: float32 [768, 24], P('dp')
- out_grad: float32 [1536, 768], P('dp')
- in_update: float32 [768, 3328], P('dp')
- dt_update: float32 [768, 24], P('dp')
- out_update: float32 [1536, 768], P('dp')
- in_left_new: float32 [32, 26, 24, 24], P('dp')
- in_right_new: float32 [32, 26, 128, 128], P('dp')
- dt_left_new: float32 [32, 24, 24], P('dp')
- dt_right_new: float32 [32, 24, 24], P('dp')
- out_left_new: float32 [64, 6, 24, 24], P('dp')
- out_right_new: float32 [64, 6, 128, 128], P('dp')
- vector_grad: float32 [11336], replicated
- vector_moment_new: float32 [11336], replicated
- vector_update: float32 [11336], replicated
The draws below stay inside these ranges and needn't reach their ends.
Inputs may be any that keep to these rules, and one draw needn't show every extreme that they name: `in_left`: every block of the statistics and of the given roots is symmetric. `in_right`: every block is symmetric. `in_left_root`: every block is symmetric. `in_right_root`: every block is symmetric. `dt_left`: every block is symmetric. `dt_right`: every block is symmetric. `dt_left_root`: every block is symmetric. `dt_right_root`: every block is symmetric. `out_left`: every block is symmetric. `out_right`: every block is symmetric. `out_left_root`: every block is symmetric. `out_right_root`: every block is symmetric.
All inputs are finite; a program needn't handle non-finite values.
Results may differ from the reference program's by a relative error of at most 0.0033.
The reference program's roundings to bfloat16 on the way count: a program that leaves them out, or rounds other values in their place, can miss the bound.
Values may be sent and summed in bfloat16 or wider, within the bound.
No kernel may reach another device: no remote copies, remote signals or barrier semaphores. Data moves between devices by JAX's collectives and lax.ppermute only.
A program may use at most 256 MiB of HBM per device.

```python
import math
import jax
import jax.numpy as jnp
from jax import lax

D = 768
HEADS = 24
HEADDIM = 64
DSTATE = 128
KCONV = 4
BLOCK_LEN = 256
LENGTH = 2048
ROW_BLOCK = 24
COL_BLOCK = 128
DI = 1536
INCOLS = 3328
CONVCH = 1792
NVEC = 11336
BATCH = 16


def symmetric_draw(key, leading, size, magnitude):
    first_key, second_key = jax.random.split(key)
    full_shape = leading + (size, size)
    rough = jax.random.normal(first_key, full_shape, jnp.float32)
    diagonal = jax.random.uniform(second_key, leading + (size,), jnp.float32, 1.0, 3.0)
    identity = jnp.eye(size, dtype=jnp.float32)
    mirrored = (rough + jnp.swapaxes(rough, -1, -2)) * (0.15 / math.sqrt(size))
    return magnitude * (mirrored * (1.0 - identity) + identity * diagonal[..., None])


def stat_level(columns):
    return 0.05 * BATCH * LENGTH * columns


def head_order(key):
    return jax.random.permutation(jax.random.fold_in(key, 11), HEADS)


def draw_dt_bias(key, part):
    order = head_order(key)
    fraction = jax.random.uniform(jax.random.fold_in(key, 12), (HEADS,), jnp.float32)
    spread = -6.9 + 4.65 * fraction * fraction
    value = jnp.where(order < HEADS // 4, -6.9, spread)
    value = jnp.where(order == HEADS - 1, -2.25, value)
    return value.astype(jnp.float32)


def draw_decay_log(key, part):
    order = head_order(key)
    fraction = jax.random.uniform(jax.random.fold_in(key, 13), (HEADS,), jnp.float32)
    value = jnp.where(order < HEADS // 4, 0.5 * fraction, 2.5 * fraction)
    value = jnp.where(order == 0, 0.0, value)
    value = jnp.where(order == HEADS - 1, 2.5, value)
    return value.astype(jnp.float32)


def draw_in_left(key, part):
    return symmetric_draw(key, (D // ROW_BLOCK, INCOLS // COL_BLOCK), ROW_BLOCK, stat_level(COL_BLOCK))


def draw_in_right(key, part):
    return symmetric_draw(key, (D // ROW_BLOCK, INCOLS // COL_BLOCK), COL_BLOCK, stat_level(ROW_BLOCK))


def draw_in_left_root(key, part):
    return symmetric_draw(key, (D // ROW_BLOCK, INCOLS // COL_BLOCK), ROW_BLOCK, stat_level(COL_BLOCK) ** (-0.25))


def draw_in_right_root(key, part):
    return symmetric_draw(key, (D // ROW_BLOCK, INCOLS // COL_BLOCK), COL_BLOCK, stat_level(ROW_BLOCK) ** (-0.25))


def draw_dt_left(key, part):
    return symmetric_draw(key, (D // ROW_BLOCK,), ROW_BLOCK, stat_level(HEADS))


def draw_dt_right(key, part):
    return symmetric_draw(key, (D // ROW_BLOCK,), HEADS, stat_level(ROW_BLOCK))


def draw_dt_left_root(key, part):
    return symmetric_draw(key, (D // ROW_BLOCK,), ROW_BLOCK, stat_level(HEADS) ** (-0.25))


def draw_dt_right_root(key, part):
    return symmetric_draw(key, (D // ROW_BLOCK,), HEADS, stat_level(ROW_BLOCK) ** (-0.25))


def draw_out_left(key, part):
    return symmetric_draw(key, (DI // ROW_BLOCK, D // COL_BLOCK), ROW_BLOCK, stat_level(COL_BLOCK))


def draw_out_right(key, part):
    return symmetric_draw(key, (DI // ROW_BLOCK, D // COL_BLOCK), COL_BLOCK, stat_level(ROW_BLOCK))


def draw_out_left_root(key, part):
    return symmetric_draw(key, (DI // ROW_BLOCK, D // COL_BLOCK), ROW_BLOCK, stat_level(COL_BLOCK) ** (-0.25))


def draw_out_right_root(key, part):
    return symmetric_draw(key, (DI // ROW_BLOCK, D // COL_BLOCK), COL_BLOCK, stat_level(ROW_BLOCK) ** (-0.25))


def levels(own_key, extent, shards, low, top_value):
    level, own = 1.0, jax.random.fold_in(own_key, 6)
    for position, blocks in shards:
        steps = jnp.exp(jax.random.uniform(jax.random.fold_in(own, position), (blocks,), jnp.float32, low / len(shards), top_value / len(shards)))
        level = level * jnp.repeat(steps, extent[position] // blocks).reshape([-1 if axis == position else 1 for axis in range(len(extent))])
    return level


def scatter_about(rng, shape, scale, reach, cuts=(), kind=jnp.bfloat16):
    values = scale * jax.random.normal(rng, shape, jnp.float32)
    if cuts:
        values = values * levels(rng, shape, cuts, -0.22, 0.18)
    return jnp.clip(values, -reach, reach).astype(kind)


def setup_inputs(seed: int = 0) -> dict:
    seeds = jax.random.split(jax.random.key(seed), 26)
    block_input = scatter_about(seeds[0], (BATCH, LENGTH, D), 1.0, 6.0, ((0, 16), (1, 2)))
    cotangent = scatter_about(seeds[1], (BATCH, LENGTH, D), 1.0, 6.0, ((0, 16), (1, 2)))
    in_weight = scatter_about(seeds[2], (D, INCOLS), D ** -0.5, 0.21875, ((0, 16),), jnp.float32)
    dt_weight = scatter_about(seeds[3], (D, HEADS), D ** -0.5, 0.21875, ((0, 16),), jnp.float32)
    out_weight = scatter_about(seeds[4], (DI, D), DI ** -0.5, 0.15625, ((0, 16),), jnp.float32)
    norm_gain = jnp.clip(1.0 + 0.1 * jax.random.normal(seeds[5], (D,), jnp.float32), 0.5, 1.5)
    conv_weight = scatter_about(seeds[6], (KCONV, CONVCH), KCONV ** -0.5, 3.0, (), jnp.float32)
    conv_bias = scatter_about(seeds[7], (CONVCH,), 0.3, 1.5, (), jnp.float32)
    dt_bias = draw_dt_bias(jax.random.fold_in(seeds[25], 71), 0)
    decay_log = draw_decay_log(jax.random.fold_in(seeds[25], 71), 0)
    skip_gain = jnp.clip(jax.random.uniform(seeds[10], (HEADS,), jnp.float32, 0.5, 1.5), 0.5, 1.5)
    gate_gain = jnp.clip(1.0 + 0.1 * jax.random.normal(seeds[11], (DI,), jnp.float32), 0.5, 1.5)
    in_left = draw_in_left(jax.random.fold_in(seeds[25], 71), 0)
    in_right = draw_in_right(jax.random.fold_in(seeds[25], 71), 0)
    in_left_root = draw_in_left_root(jax.random.fold_in(seeds[25], 71), 0)
    in_right_root = draw_in_right_root(jax.random.fold_in(seeds[25], 71), 0)
    dt_left = draw_dt_left(jax.random.fold_in(seeds[25], 71), 0)
    dt_right = draw_dt_right(jax.random.fold_in(seeds[25], 71), 0)
    dt_left_root = draw_dt_left_root(jax.random.fold_in(seeds[25], 71), 0)
    dt_right_root = draw_dt_right_root(jax.random.fold_in(seeds[25], 71), 0)
    out_left = draw_out_left(jax.random.fold_in(seeds[25], 71), 0)
    out_right = draw_out_right(jax.random.fold_in(seeds[25], 71), 0)
    out_left_root = draw_out_left_root(jax.random.fold_in(seeds[25], 71), 0)
    out_right_root = draw_out_right_root(jax.random.fold_in(seeds[25], 71), 0)
    vector_moment = jnp.clip(jnp.exp(jax.random.uniform(seeds[24], (NVEC,), jnp.float32, math.log(1638.4), math.log(65536.0))), 1638.4, 65536.0)
    return {"block_input": block_input, "cotangent": cotangent, "in_weight": in_weight, "dt_weight": dt_weight, "out_weight": out_weight, "norm_gain": norm_gain, "conv_weight": conv_weight, "conv_bias": conv_bias, "dt_bias": dt_bias, "decay_log": decay_log, "skip_gain": skip_gain, "gate_gain": gate_gain, "in_left": in_left, "in_right": in_right, "in_left_root": in_left_root, "in_right_root": in_right_root, "dt_left": dt_left, "dt_right": dt_right, "dt_left_root": dt_left_root, "dt_right_root": dt_right_root, "out_left": out_left, "out_right": out_right, "out_left_root": out_left_root, "out_right_root": out_right_root, "vector_moment": vector_moment}


EPS = 1e-05
LR = 0.25
LR_VEC = 0.02
HIGH = lax.Precision.HIGHEST

@jax.custom_vjp
def low(v):
    return lax.optimization_barrier(v.astype(jnp.bfloat16)).astype(jnp.float32)

@jax.custom_vjp
def low_back(v):
    return v

def low_keep(v):
    return (low(v), None)

def low_pass(kept, grad):
    return (grad,)

def back_keep(v):
    return (v, None)

def back_low(kept, grad):
    return (low(grad),)
low.defvjp(low_keep, low_pass)
low_back.defvjp(back_keep, back_low)

def causal_conv(signal, kernel, offset):
    length = signal.shape[-2]
    widths = [(0, 0)] * (signal.ndim - 2) + [(KCONV - 1, 0), (0, 0)]
    padded = jnp.pad(signal, widths)
    running = offset + kernel[0] * padded[..., 0:length, :]
    for tap_index in range(1, KCONV):
        running = running + kernel[tap_index] * padded[..., tap_index:tap_index + length, :]
    return jax.nn.silu(running)

def carry_step(carried, scanned):
    new_state, factor = scanned
    return (carried * factor[:, None, None] + new_state, carried)

def state_space(values, step_sizes, decay_rates, inputs_b, inputs_c, skip_gain):
    length, head_count, head_size = values.shape
    block_count = length // BLOCK_LEN
    blocks_x = values.reshape(block_count, BLOCK_LEN, head_count, head_size)
    blocks_dt = step_sizes.reshape(block_count, BLOCK_LEN, head_count)
    blocks_b = inputs_b.reshape(block_count, BLOCK_LEN, -1)
    blocks_c = inputs_c.reshape(block_count, BLOCK_LEN, -1)
    cumulative = jnp.cumsum(blocks_dt * decay_rates, axis=1)
    row_index = lax.broadcasted_iota(jnp.int32, (BLOCK_LEN, BLOCK_LEN), 0)
    earlier = lax.broadcasted_iota(jnp.int32, (BLOCK_LEN, BLOCK_LEN), 1)
    causal = (row_index >= earlier)[None, :, :, None]
    spread = cumulative[:, :, None, :] - cumulative[:, None, :, :]
    kernel = jnp.where(causal, jnp.exp(jnp.where(causal, spread, 0.0)), 0.0)
    scores = jnp.einsum('cqn,csn->cqs', blocks_c, blocks_b, precision=HIGH)
    mixing = scores[..., None] * kernel * blocks_dt[:, None, :, :]
    inner_part = jnp.einsum('cqsh,cshp->cqhp', mixing, blocks_x, precision=HIGH)
    weights = jnp.exp(cumulative[:, -1:, :] - cumulative) * blocks_dt
    fresh_state = jnp.einsum('csn,cshp->chnp', blocks_b, weights[..., None] * blocks_x, precision=HIGH)
    factor = jnp.exp(cumulative[:, -1, :])
    initial = jnp.zeros((head_count, blocks_b.shape[-1], head_size), jnp.float32)
    last_state, entering = lax.scan(jax.checkpoint(carry_step), initial, (fresh_state, factor))
    outer_part = jnp.einsum('cqn,chnp->cqhp', blocks_c, entering, precision=HIGH) * jnp.exp(cumulative)[..., None]
    combined = inner_part + outer_part + skip_gain[None, None, :, None] * blocks_x
    return combined.reshape(length, head_count, head_size)

def norm_piece(incoming, norm_gain):
    inv_rms = lax.rsqrt(lax.optimization_barrier(jnp.mean(incoming * incoming, axis=-1, keepdims=True)) + EPS)
    return incoming * inv_rms * norm_gain

def gate_piece(states, gate_part, gate_gain):
    gated_out = states * jax.nn.silu(gate_part)
    norm_gate = lax.rsqrt(lax.optimization_barrier(jnp.mean(gated_out * gated_out, axis=-1, keepdims=True)) + EPS)
    return gated_out * norm_gate * gate_gain

def kron_update(gradient, left_stat, right_stat, left_root, right_root):
    row_tiles, col_tiles = (left_stat.shape[0], left_stat.shape[1])
    row_size, col_size = (left_stat.shape[-1], right_stat.shape[-1])
    grad_tiles = gradient.reshape(row_tiles, row_size, col_tiles, col_size).transpose(0, 2, 1, 3)
    left_new = 0.5 * left_stat + 0.5 * jnp.einsum('abij,abkj->abik', grad_tiles, grad_tiles, precision=HIGH)
    right_new = 0.5 * right_stat + 0.5 * jnp.einsum('abji,abjk->abik', grad_tiles, grad_tiles, precision=HIGH)
    shaped = jnp.einsum('abij,abjk->abik', left_root, grad_tiles, precision=HIGH)
    shaped = jnp.einsum('abij,abjk->abik', shaped, right_root, precision=HIGH)
    update = (-LR * shaped).transpose(0, 2, 1, 3).reshape(gradient.shape)
    return (update, left_new, right_new)

def vector_step(gradient, moment):
    moment_new = 0.5 * moment + 0.5 * gradient * gradient
    return (-LR_VEC * gradient * lax.rsqrt(moment_new), moment_new)

def layer(incoming, in_weight, dt_weight, out_weight, norm_gain, conv_weight, conv_bias, dt_bias, decay_log, skip_gain, gate_gain):
    normed = low(norm_piece(incoming, norm_gain))
    projected = low_back(jnp.dot(normed, low(in_weight), precision=HIGH))
    dt_raw = low(low_back(jnp.dot(normed, low(dt_weight), precision=HIGH)))
    gate_part = projected[:, :DI]
    mixed_part = low(projected[:, DI:])
    convolved = causal_conv(mixed_part, conv_weight, conv_bias)
    values = convolved[:, :DI].reshape(-1, HEADS, HEADDIM)
    inputs_b = convolved[:, DI:DI + DSTATE]
    inputs_c = convolved[:, DI + DSTATE:]
    step_sizes = jax.nn.softplus(dt_raw + dt_bias)
    decay_rates = -jnp.exp(decay_log)
    states = state_space(values, step_sizes, decay_rates, inputs_b, inputs_c, skip_gain).reshape(-1, DI)
    states = low_back(low(states))
    branch = low(gate_piece(states, gate_part, gate_gain))
    return incoming + jnp.dot(branch, low(out_weight), precision=HIGH)

def reference(block_input, cotangent, in_weight, dt_weight, out_weight, norm_gain, conv_weight, conv_bias, dt_bias, decay_log, skip_gain, gate_gain, in_left, in_right, in_left_root, in_right_root, dt_left, dt_right, dt_left_root, dt_right_root, out_left, out_right, out_left_root, out_right_root, vector_moment):
    parameters = (in_weight, dt_weight, out_weight, norm_gain, conv_weight, conv_bias, dt_bias, decay_log, skip_gain, gate_gain)

    def one_sequence(totals, sequence_pair):
        incoming, upstream = sequence_pair
        output, backward = jax.vjp(layer, incoming.astype(jnp.float32), *parameters)
        gradients = backward(upstream.astype(jnp.float32))
        totals = tuple((running + fresh_grad for running, fresh_grad in zip(totals, gradients[1:])))
        return (totals, (output.astype(jnp.bfloat16), gradients[0]))
    initial = tuple((jnp.zeros_like(param_value) for param_value in parameters))
    totals, outputs = lax.scan(one_sequence, initial, (block_input, cotangent))
    block_output, input_grad = outputs
    in_grad, dt_grad, out_grad = (totals[0], totals[1], totals[2])
    vector_grad = jnp.concatenate([totals[3], totals[9], totals[4].reshape(-1), totals[5], totals[6], totals[7], totals[8]])
    in_update, in_left_new, in_right_new = kron_update(in_grad, in_left, in_right, in_left_root, in_right_root)
    dt_update, dt_left_wide, dt_right_wide = kron_update(dt_grad, dt_left[:, None], dt_right[:, None], dt_left_root[:, None], dt_right_root[:, None])
    out_update, out_left_new, out_right_new = kron_update(out_grad, out_left, out_right, out_left_root, out_right_root)
    vector_update, vector_moment_new = vector_step(vector_grad, vector_moment)
    return (block_output, input_grad, in_grad, dt_grad, out_grad, in_update, dt_update, out_update, in_left_new, in_right_new, dt_left_wide[:, 0], dt_right_wide[:, 0], out_left_new, out_right_new, vector_grad, vector_moment_new, vector_update)
```

```python
import functools

import jax
import jax.numpy as jnp
from jax import lax
from jax.experimental import pallas as pl
from jax.experimental.pallas import tpu as pltpu
from jax.sharding import PartitionSpec as P

D = 768
HEADS = 24
HEADDIM = 64
DSTATE = 128
KCONV = 4
DI = 1536
CONVCH = 1792
INCOLS = 3328

BL = 128
PAIRS = HEADS // 2
ROWS = 16

AXES = ("z", "x", "core")

EPS = 1e-05
LR = 0.25
LR_VEC = 0.02
NEG = -1e30
BF = jnp.bfloat16
F32 = jnp.float32
HIGH = lax.Precision.HIGHEST
NN = (((1,), (0,)), ((), ()))
NT = (((1,), (1,)), ((), ()))
TN = (((0,), (0,)), ((), ()))


def dot(a, b, dims=NN):
    return lax.dot_general(a, b, dims, preferred_element_type=F32)


def split2(v):
    high = v.astype(BF)
    return high, (v - high.astype(F32)).astype(BF)


def dot3(a, b, dims=NN):
    ah, al = split2(a)
    bh, bl = split2(b)
    return dot(ah, bh, dims) + dot(al, bh, dims) + dot(ah, bl, dims)


def pack(v):
    high = v.astype(BF).astype(F32)
    rest = v - high
    mid = rest.astype(BF).astype(F32)
    low = rest - mid
    return (high + pltpu.roll(mid, 32, 1) + pltpu.roll(low, 64, 1)).astype(BF)


def head_lanes(shape):
    return lax.broadcasted_iota(jnp.int32, shape, 1) < HEADS


def prefix(tri, v):
    parts = dot(tri, pack(v))
    total = parts + pltpu.roll(parts, 96, 1) + pltpu.roll(parts, 64, 1)
    return jnp.where(head_lanes(total.shape), total, 0.0)


def expand(v, emat):
    return dot(pack(v), emat)


def head_sum(v, gather):
    high, low = split2(v)
    return dot(high, gather) + dot(low, gather)


def tri_mask(lower):
    rows = lax.broadcasted_iota(jnp.int32, (BL, BL), 0)
    cols = lax.broadcasted_iota(jnp.int32, (BL, BL), 1)
    return (rows >= cols) if lower else (cols >= rows)


def softplus(v):
    return jnp.maximum(v, 0.0) + jnp.log1p(jnp.exp(-jnp.abs(v)))


def sigmoid(v):
    return 1.0 / (1.0 + jnp.exp(-v))


def rates(alog_ref):
    rate = -jnp.exp(alog_ref[0:1, :])
    return jnp.where(head_lanes(rate.shape), rate, 0.0)


def pair_blocks(v):
    left = lax.broadcasted_iota(jnp.int32, v.shape, 1) < HEADDIM
    return jnp.concatenate([jnp.where(left, v, 0.0), jnp.where(left, 0.0, v)], axis=0).astype(BF)


def norm_rows(u, gain):
    inv = lax.rsqrt(jnp.mean(u * u, axis=-1, keepdims=True) + EPS)
    return u * inv * gain


def first_kernel(
    u_ref, halo_ref, gain_ref, wm_ref, wdt_ref, cw_ref, cb_ref, dtb_ref, alog_ref, emat_ref,
    normed_ref, mixed_ref, pre_ref, z_ref, state_ref, total_ref,
    tail, full,
):
    step_index = pl.program_id(1)
    tile = u_ref.shape[1]
    gain = gain_ref[0:1, :]

    @pl.when(step_index == 0)
    def _():
        near = norm_rows(halo_ref[0].astype(F32), gain).astype(BF)
        tail[...] = dot(near, wm_ref[...]).astype(BF).astype(F32)
        state_ref[...] = jnp.zeros_like(state_ref)
        total_ref[...] = jnp.zeros_like(total_ref)

    normed = norm_rows(u_ref[0].astype(F32), gain).astype(BF)
    normed_ref[0] = normed
    mixed_low = dot(normed, wm_ref[...]).astype(BF)
    mixed_ref[0] = mixed_low
    mixed = mixed_low.astype(F32)
    z = dot(normed, wdt_ref[...]).astype(BF).astype(F32) + dtb_ref[0:1, :]
    z_ref[0] = z
    full[0:8, :] = tail[...]
    full[8:, :] = mixed
    tail[...] = mixed[tile - 8 :, :]
    pre = cb_ref[0:1, :] + cw_ref[KCONV - 1 : KCONV, :] * mixed
    for tap in range(KCONV - 1):
        pre = pre + cw_ref[tap : tap + 1, :] * full[5 + tap : 5 + tap + tile, :]
    pre_ref[0] = pre
    conv = pre * sigmoid(pre)
    step_all = softplus(z)
    rate = rates(alog_ref)
    tri = jnp.where(tri_mask(True), 1.0, 0.0).astype(BF)
    emat = emat_ref[...]
    for part in range(tile // BL):
        rows = slice(part * BL, (part + 1) * BL)
        step = step_all[rows]
        cum = prefix(tri, step * rate)
        last = cum[BL - 1 : BL, :]
        weights = expand(jnp.exp(last - cum) * step, emat)
        decay = expand(
            jnp.where(head_lanes((8, 128)), jnp.broadcast_to(jnp.exp(last), (8, 128)), 0.0), emat
        )[0:1, :]
        inputs_b = conv[rows, DI : DI + DSTATE]
        fresh = dot3(inputs_b.T, weights * conv[rows, :DI])
        state_ref[0] = state_ref[0] * decay + fresh
        total_ref[0] = total_ref[0] + jnp.broadcast_to(last, (8, 128))


def second_kernel(
    pre_ref, z_ref, gate_ref, bgrad_ref, u_ref, enter_ref, wo_ref, skip_ref, ggain_ref, alog_ref,
    emat_ref, gmat_ref,
    out_ref, branch_ref, dy_ref, ggrad_ref, state_ref, rdot_ref, dstate_ref, gain_acc, skip_acc,
    state, running, xs, ys, es,
):
    step_index = pl.program_id(1)
    tile = pre_ref.shape[1]
    parts = tile // BL

    @pl.when(step_index == 0)
    def _():
        state[...] = enter_ref[0]
        running[...] = jnp.ones_like(running)
        dstate_ref[...] = jnp.zeros_like(dstate_ref)

    @pl.when((step_index == 0) & (pl.program_id(0) == 0))
    def _():
        gain_acc[...] = jnp.zeros_like(gain_acc)
        skip_acc[...] = jnp.zeros_like(skip_acc)

    rate = rates(alog_ref)
    mask = tri_mask(True)
    tri = jnp.where(mask, 1.0, 0.0).astype(BF)
    emat = emat_ref[...]
    cts = []
    for part in range(parts):
        rows = slice(part * BL, (part + 1) * BL)
        pre = pre_ref[0, rows, :]
        conv = pre * sigmoid(pre)
        x = conv[:, :DI]
        inputs_b = conv[:, DI : DI + DSTATE]
        inputs_c = conv[:, DI + DSTATE :]
        step = softplus(z_ref[0, rows, :])
        cum = prefix(tri, step * rate)
        cum_t = cum.T
        last = cum[BL - 1 : BL, :]
        lanes = head_lanes(cum.shape)
        wide = expand(
            jnp.concatenate(
                [step, jnp.where(lanes, jnp.exp(cum), 0.0), jnp.exp(last - cum) * step], axis=0
            ),
            emat,
        )
        grown = wide[BL : 2 * BL]
        decay = grown[BL - 1 : BL, :]
        scaled = wide[:BL] * x
        scores = dot3(inputs_c, inputs_b, NT)
        held = state[...]
        state_ref[0, part] = held
        outer = grown * dot3(inputs_c, held)
        state[...] = held * decay + dot3(inputs_b.T, wide[2 * BL :] * x)
        for pair in range(PAIRS):
            cols = slice(pair * 128, (pair + 1) * 128)
            mixing = []
            for h in (2 * pair, 2 * pair + 1):
                spread = jnp.where(mask, cum[:, h : h + 1] - cum_t[h : h + 1, :], NEG)
                mixing.append(scores * jnp.exp(spread))
            mh, ml = split2(jnp.concatenate(mixing, axis=1))
            piece = scaled[:, cols]
            high = piece.astype(BF).astype(F32)
            rh, rl = pair_blocks(high), pair_blocks(piece - high)
            inner = dot(mh, rh) + dot(ml, rh) + dot(mh, rl)
            ys[rows, cols] = inner + outer[:, cols]
        xs[rows, :] = x
        es[rows, :] = grown * running[0:1, :]
        running[...] = running[...] * decay
        cts.append(inputs_c.T)

    gain = ggain_ref[0:1, :]
    skip = skip_ref[0:1, :]

    def rows_step(r, carry):
        rows = pl.ds(pl.multiple_of(r * ROWS, ROWS), ROWS)
        x = xs[rows, :]
        yhat = ys[rows, :]
        states = (yhat + skip * x).astype(BF).astype(F32)
        gate = gate_ref[rows, :]
        sg = sigmoid(gate)
        sl = gate * sg
        gated = states * sl
        inv = lax.rsqrt(jnp.mean(gated * gated, axis=-1, keepdims=True) + EPS)
        norm = gated * inv
        branch_ref[rows, :] = (norm * gain).astype(BF)
        bg = bgrad_ref[rows, :]
        tg = bg * gain
        gain_acc[...] += bg * norm
        dot_row = jnp.mean(tg * norm, axis=-1, keepdims=True)
        dgated = inv * (tg - norm * dot_row)
        dy_low = (dgated * sl).astype(BF)
        dy_ref[rows, :] = dy_low
        ggrad_ref[rows, :] = (dgated * states * (sg * (1.0 + gate * (1.0 - sg)))).astype(BF)
        dy = dy_low.astype(F32)
        skip_acc[...] += dy * x
        ys[rows, :] = dy * yhat
        es[rows, :] = es[rows, :] * dy
        return carry

    lax.fori_loop(0, tile // ROWS, rows_step, 0)
    out_ref[0] = (u_ref[0].astype(F32) + dot(branch_ref[...], wo_ref[...])).astype(BF)
    rdot_ref[0] = head_sum(ys[...], gmat_ref[...])
    for part in range(parts):
        rows = slice(part * BL, (part + 1) * BL)
        dstate_ref[0] = dstate_ref[0] + dot3(cts[part], es[rows, :])


def third_kernel(
    pre_ref, mixed_ref, z_ref, dy_ref, state_ref, rdot_ref, leave_ref, cw_ref, skip_ref, alog_ref,
    emat_ref, gmat_ref,
    mgrad_ref, dz_ref, last_ref, first_ref, cw_acc, cb_acc, dtb_acc, rate_acc,
    dstate, tail, full,
):
    step_index = pl.program_id(1)

    @pl.when(step_index == 0)
    def _():
        dstate[...] = leave_ref[0]
        tail[...] = jnp.zeros_like(tail)

    @pl.when((step_index == 0) & (pl.program_id(0) == 0))
    def _():
        for ref in (cw_acc, cb_acc, dtb_acc, rate_acc):
            ref[...] = jnp.zeros_like(ref)

    rate = rates(alog_ref)
    mask = tri_mask(False)
    low_tri = jnp.where(tri_mask(True), 1.0, 0.0).astype(BF)
    high_tri = jnp.where(mask, 1.0, 0.0).astype(BF)
    emat = emat_ref[...]
    gmat = gmat_ref[...]
    skip = skip_ref[0:1, :]
    pre = pre_ref[0]
    sg = sigmoid(pre)
    conv = pre * sg
    x = conv[:, :DI]
    inputs_b = conv[:, DI : DI + DSTATE]
    inputs_c = conv[:, DI + DSTATE :]
    z = z_ref[0]
    step = softplus(z)
    cum = prefix(low_tri, step * rate)
    cum_t = cum.T
    last = cum[BL - 1 : BL, :]
    lanes = head_lanes(cum.shape)
    wide = expand(
        jnp.concatenate(
            [
                step,
                jnp.where(lanes, jnp.exp(cum), 0.0),
                jnp.where(lanes, jnp.exp(last - cum), 0.0),
            ],
            axis=0,
        ),
        emat,
    )
    dt_wide, grown, shrink = wide[:BL], wide[BL : 2 * BL], wide[2 * BL :]
    decay = grown[BL - 1 : BL, :]
    scaled = dt_wide * x
    dy = dy_ref[...].astype(F32)
    held = state_ref[0, 0]
    ds = dstate[...]
    scores_t = dot3(inputs_b, inputs_c, NT)
    dscaled_state = shrink * dot3(inputs_b, ds)
    dscores_t = jnp.zeros((BL, BL), F32)
    pieces = []
    for pair in range(PAIRS):
        cols = slice(pair * 128, (pair + 1) * 128)
        kernels = []
        for h in (2 * pair, 2 * pair + 1):
            spread = jnp.where(mask, cum_t[h : h + 1, :] - cum[:, h : h + 1], NEG)
            kernels.append(jnp.exp(spread))
        mh, ml = split2(jnp.concatenate([scores_t * k for k in kernels], axis=1))
        dyb = pair_blocks(dy[:, cols])
        pieces.append(dot(mh, dyb) + dot(ml, dyb))
        sh, sl = split2(scaled[:, cols])
        dmix = dot(sh, dyb, NT) + dot(sl, dyb, NT)
        dscores_t = dscores_t + dmix[:, :BL] * kernels[0] + dmix[:, BL:] * kernels[1]
    dscaled = jnp.concatenate(pieces, axis=1) + dscaled_state
    dx = dt_wide * dscaled + skip * dy
    grown_dy = grown * dy
    ends = jnp.sum(scaled * dscaled_state, axis=0, keepdims=True) + decay * jnp.sum(
        held * ds, axis=0, keepdims=True
    )
    sums = head_sum(
        jnp.concatenate([x * dscaled, jnp.broadcast_to(ends, (8, DI))], axis=0), gmat
    )
    direct = sums[:BL]
    is_last = lax.broadcasted_iota(jnp.int32, (BL, 128), 0) == BL - 1
    dcum = rdot_ref[0] - step * direct + jnp.where(is_last, sums[BL : BL + 1, :], 0.0)
    dcum = jnp.where(lanes, dcum, 0.0)
    drate = prefix(high_tri, dcum)
    dz = (rate * drate + direct) * sigmoid(z)
    dz_ref[0] = dz.astype(BF)
    dtb_acc[...] += jnp.sum(dz.reshape(BL // 8, 8, 128), axis=0)
    rate_acc[...] += jnp.sum((step * drate).reshape(BL // 8, 8, 128), axis=0)
    db = dot3(dscores_t, inputs_c) + dot3(shrink * scaled, ds, NT)
    dc = dot3(dscores_t.T, inputs_b) + dot3(grown_dy, held, NT)
    dstate[...] = decay * ds + dot3(inputs_c.T, grown_dy)
    dpre = jnp.concatenate([dx, db, dc], axis=1) * (sg * (1.0 + pre * (1.0 - sg)))
    full[0:BL, :] = dpre
    full[BL:, :] = tail[...]
    tail[...] = dpre[0:8, :]
    first_ref[0] = dpre[0:8, :]
    mixed = mixed_ref[0].astype(F32)
    cb_acc[...] += jnp.sum(dpre.reshape(BL // 8, 8, CONVCH), axis=0)
    mgrad = jnp.zeros_like(dpre)
    for tap in range(KCONV):
        moved = full[KCONV - 1 - tap : KCONV - 1 - tap + BL, :]
        mgrad = mgrad + cw_ref[tap : tap + 1, :] * moved
        cw_acc[tap] += jnp.sum((moved * mixed).reshape(BL // 8, 8, CONVCH), axis=0)
    mgrad_ref[0] = mgrad.astype(BF)

    @pl.when(step_index == 0)
    def _():
        last_ref[0] = mgrad[BL - 8 :, :]


PARAMS = dict(vmem_limit_bytes=60 * 1024 * 1024)


def whole(shape):
    zeros = (0,) * len(shape)
    return pl.BlockSpec(shape, lambda b, i: zeros)


def run_first(u, halo, gain, wm, wdt, cw, cb, dtb, alog, emat):
    seqs, length, _ = u.shape
    tile = min(256, length)
    grid = (seqs, length // tile)
    tok = lambda width: pl.BlockSpec((1, tile, width), lambda b, i: (b, i, 0))
    per = lambda *shape: pl.BlockSpec((1,) + shape, lambda b, i: (b,) + (0,) * len(shape))
    return pl.pallas_call(
        first_kernel,
        grid=grid,
        in_specs=[
            tok(D), per(8, D), whole(gain.shape), whole(wm.shape), whole(wdt.shape),
            whole(cw.shape), whole(cb.shape), whole(dtb.shape), whole(alog.shape), whole(emat.shape),
        ],
        out_specs=[
            tok(D), tok(CONVCH), tok(CONVCH), tok(128), per(DSTATE, DI), per(8, 128),
        ],
        out_shape=[
            jax.ShapeDtypeStruct((seqs, length, D), BF),
            jax.ShapeDtypeStruct((seqs, length, CONVCH), BF),
            jax.ShapeDtypeStruct((seqs, length, CONVCH), F32),
            jax.ShapeDtypeStruct((seqs, length, 128), F32),
            jax.ShapeDtypeStruct((seqs, DSTATE, DI), F32),
            jax.ShapeDtypeStruct((seqs, 8, 128), F32),
        ],
        scratch_shapes=[pltpu.VMEM((8, CONVCH), F32), pltpu.VMEM((tile + 8, CONVCH), F32)],
        compiler_params=pltpu.CompilerParams(**PARAMS),
        name="first",
    )(u, halo, gain, wm, wdt, cw, cb, dtb, alog, emat)


def run_second(pre, z, gate, bgrad, u, enter, wo, skip, ggain, alog, emat, gmat):
    seqs, length, _ = u.shape
    tile = min(256, length)
    steps = length // tile
    parts = tile // BL
    grid = (seqs, steps)
    tok = lambda width: pl.BlockSpec((1, tile, width), lambda b, i: (b, i, 0))
    flat = lambda width: pl.BlockSpec((tile, width), lambda b, i: (b * steps + i, 0))
    per = lambda *shape: pl.BlockSpec((1,) + shape, lambda b, i: (b,) + (0,) * len(shape))
    rows = seqs * length
    return pl.pallas_call(
        second_kernel,
        grid=grid,
        in_specs=[
            tok(CONVCH), tok(128), flat(DI), flat(DI), tok(D), per(DSTATE, DI), whole(wo.shape),
            whole(skip.shape), whole(ggain.shape), whole(alog.shape), whole(emat.shape),
            whole(gmat.shape),
        ],
        out_specs=[
            tok(D), flat(DI), flat(DI), flat(DI),
            pl.BlockSpec((1, parts, DSTATE, DI), lambda b, i: (b, i, 0, 0)),
            tok(128), per(DSTATE, DI), whole((ROWS, DI)), whole((ROWS, DI)),
        ],
        out_shape=[
            jax.ShapeDtypeStruct((seqs, length, D), BF),
            jax.ShapeDtypeStruct((rows, DI), BF),
            jax.ShapeDtypeStruct((rows, DI), BF),
            jax.ShapeDtypeStruct((rows, DI), BF),
            jax.ShapeDtypeStruct((seqs, length // BL, DSTATE, DI), F32),
            jax.ShapeDtypeStruct((seqs, length, 128), F32),
            jax.ShapeDtypeStruct((seqs, DSTATE, DI), F32),
            jax.ShapeDtypeStruct((ROWS, DI), F32),
            jax.ShapeDtypeStruct((ROWS, DI), F32),
        ],
        scratch_shapes=[
            pltpu.VMEM((DSTATE, DI), F32), pltpu.VMEM((8, DI), F32), pltpu.VMEM((tile, DI), F32),
            pltpu.VMEM((tile, DI), F32), pltpu.VMEM((tile, DI), F32),
        ],
        compiler_params=pltpu.CompilerParams(**PARAMS),
        name="second",
    )(pre, z, gate, bgrad, u, enter, wo, skip, ggain, alog, emat, gmat)


def run_third(pre, mixed, z, dy, states, rdot, leave, cw, skip, alog, emat, gmat):
    seqs, length, _ = pre.shape
    steps = length // BL
    grid = (seqs, steps)
    tok = lambda width: pl.BlockSpec((1, BL, width), lambda b, i: (b, steps - 1 - i, 0))
    per = lambda *shape: pl.BlockSpec((1,) + shape, lambda b, i: (b,) + (0,) * len(shape))
    return pl.pallas_call(
        third_kernel,
        grid=grid,
        in_specs=[
            tok(CONVCH), tok(CONVCH), tok(128),
            pl.BlockSpec((BL, DI), lambda b, i: (b * steps + steps - 1 - i, 0)),
            pl.BlockSpec((1, 1, DSTATE, DI), lambda b, i: (b, steps - 1 - i, 0, 0)),
            tok(128), per(DSTATE, DI), whole(cw.shape), whole(skip.shape), whole(alog.shape),
            whole(emat.shape), whole(gmat.shape),
        ],
        out_specs=[
            tok(CONVCH), tok(128), per(8, CONVCH), per(8, CONVCH), whole((KCONV, 8, CONVCH)),
            whole((8, CONVCH)), whole((8, 128)), whole((8, 128)),
        ],
        out_shape=[
            jax.ShapeDtypeStruct((seqs, length, CONVCH), BF),
            jax.ShapeDtypeStruct((seqs, length, 128), BF),
            jax.ShapeDtypeStruct((seqs, 8, CONVCH), F32),
            jax.ShapeDtypeStruct((seqs, 8, CONVCH), F32),
            jax.ShapeDtypeStruct((KCONV, 8, CONVCH), F32),
            jax.ShapeDtypeStruct((8, CONVCH), F32),
            jax.ShapeDtypeStruct((8, 128), F32),
            jax.ShapeDtypeStruct((8, 128), F32),
        ],
        scratch_shapes=[
            pltpu.VMEM((DSTATE, DI), F32), pltpu.VMEM((8, CONVCH), F32),
            pltpu.VMEM((BL + 8, CONVCH), F32),
        ],
        compiler_params=pltpu.CompilerParams(**PARAMS),
        name="third",
    )(pre, mixed, z, dy, states, rdot, leave, cw, skip, alog, emat, gmat)


def norm_piece(incoming, norm_gain):
    inv_rms = lax.rsqrt(jnp.mean(incoming * incoming, axis=-1, keepdims=True) + EPS)
    return incoming * inv_rms * norm_gain


def kron_update(gradient, left_stat, right_stat, left_root, right_root):
    row_tiles, col_tiles = (left_stat.shape[0], left_stat.shape[1])
    row_size, col_size = (left_stat.shape[-1], right_stat.shape[-1])
    grad_tiles = gradient.reshape(row_tiles, row_size, col_tiles, col_size).transpose(0, 2, 1, 3)
    left_new = 0.5 * left_stat + 0.5 * jnp.einsum(
        "abij,abkj->abik", grad_tiles, grad_tiles, precision=HIGH
    )
    right_new = 0.5 * right_stat + 0.5 * jnp.einsum(
        "abji,abjk->abik", grad_tiles, grad_tiles, precision=HIGH
    )
    shaped = jnp.einsum("abij,abjk->abik", left_root, grad_tiles, precision=HIGH)
    shaped = jnp.einsum("abij,abjk->abik", shaped, right_root, precision=HIGH)
    update = (-LR * shaped).transpose(0, 2, 1, 3).reshape(gradient.shape)
    return (update, left_new, right_new)


def swapped(v, axis, size, offset):
    return lax.ppermute(v, axis, [(i, (i + offset) % size) for i in range(size)])


def pick(v, index):
    return lax.dynamic_index_in_dim(v, index, 0, keepdims=False)


def scatter_stage(v, axis, kind=BF):
    size = lax.axis_size(axis)
    here = lax.axis_index(axis)
    total = pick(v, here)
    for offset in range(1, size):
        sent = pick(v, lax.rem(here + offset, size)).astype(kind)
        total = total + swapped(sent, axis, size, offset).astype(F32)
    return total


def gather_stage(v, axis):
    size = lax.axis_size(axis)
    here = lax.axis_index(axis)
    out = jnp.zeros((size,) + v.shape, v.dtype)
    out = lax.dynamic_update_index_in_dim(out, v, here, 0)
    for offset in range(1, size):
        got = swapped(v, axis, size, offset)
        out = lax.dynamic_update_index_in_dim(out, got, lax.rem(here - offset + size, size), 0)
    return out


def core_sum(partial):
    z, x, core = (lax.axis_size(a) for a in ("z", "x", "core"))
    rows, cols = partial.shape
    blocks = partial.reshape(z, x, core, rows // (z * x * core), cols)
    return scatter_stage(jnp.moveaxis(blocks, 2, 0), "core", F32)


def across(v):
    return scatter_stage(scatter_stage(jnp.moveaxis(v, 1, 0), "x"), "z")


def reduce_plain(v):
    owned = across(v)
    total = owned
    size = lax.axis_size("seq")
    if size > 2:
        return lax.psum(owned, "seq")
    for offset in range(1, size):
        total = total + swapped(owned, "seq", size, offset)
    return total


def reduce_split(v):
    size = lax.axis_size("seq")
    z, x, rows, cols = v.shape
    if cols % (128 * size):
        return reduce_plain(v)
    v = jnp.moveaxis(v.reshape(z, x, rows, size, cols // size), 3, 0)
    owned = across(scatter_stage(v, "seq"))
    return jnp.moveaxis(gather_stage(owned, "seq"), 0, 1).reshape(rows, cols)


def row8(v, width=None):
    v = v.reshape(1, -1)
    if width is not None:
        v = jnp.pad(v, ((0, 0), (0, width - v.shape[1])))
    return jnp.broadcast_to(v, (8, v.shape[1]))


def body(
    block_input,
    cotangent,
    in_weight,
    dt_weight,
    out_weight,
    norm_gain,
    conv_weight,
    conv_bias,
    dt_bias,
    decay_log,
    skip_gain,
    gate_gain,
    in_left,
    in_right,
    in_left_root,
    in_right_root,
    dt_left,
    dt_right,
    dt_left_root,
    dt_right_root,
    out_left,
    out_right,
    out_left_root,
    out_right_root,
    vector_moment,
):
    seq_count, local_len, _ = block_input.shape
    seq_devices = lax.axis_size("seq")
    row_count = seq_count * local_len
    up = [(i, i + 1) for i in range(seq_devices - 1)]
    down = [(i + 1, i) for i in range(seq_devices - 1)]

    in_low = in_weight.astype(BF)
    dt_low = jnp.pad(dt_weight.astype(BF), ((0, 0), (0, 128 - HEADS)))
    main = lax.all_gather(
        jnp.concatenate([in_low[:, DI:], dt_low], axis=1), AXES, axis=0, tiled=True
    )
    wg = lax.all_gather(in_low[:, :DI], AXES, axis=0, tiled=True)
    wo = lax.all_gather(out_weight.astype(BF), AXES, axis=0, tiled=True)
    wm, wdt = main[:, :CONVCH], main[:, CONVCH:]
    halo = lax.ppermute(block_input[:, local_len - 8 :, :], "seq", up)

    part = jnp.arange(128)
    channel = jnp.arange(DI)
    emat = (
        ((part[:, None] % 32) == (channel[None, :] // HEADDIM)) & (part[:, None] < 96)
    ).astype(BF)
    gmat = ((channel[:, None] // HEADDIM) == part[None, :]).astype(BF)
    skip_wide = row8(jnp.repeat(skip_gain, HEADDIM))
    alog = row8(decay_log, 128)
    dtb = row8(jnp.concatenate([dt_bias, jnp.full((128 - HEADS,), -1e4, F32)]))
    cw8 = jnp.pad(conv_weight, ((0, 4), (0, 0)))

    normed, mixed, pre, z, local_state, total = run_first(
        block_input, halo, row8(norm_gain), wm, wdt, cw8, row8(conv_bias), dtb, alog, emat
    )
    span = jnp.repeat(jnp.exp(total[:, 0:1, :HEADS]), HEADDIM, axis=2)
    enter = lax.ppermute(local_state, "seq", up)
    for _ in range(seq_devices - 2):
        enter = lax.ppermute(local_state + span * enter, "seq", up)

    normed_rows = normed.reshape(row_count, D)
    upstream = cotangent.reshape(row_count, D)
    gate_part = dot(normed_rows, wg)
    branch_grad = dot(upstream, wo, NT)
    (
        block_output, branch, states_grad, gate_grad, states, rdot, local_dstate, gain_acc, skip_acc,
    ) = run_second(
        pre, z, gate_part, branch_grad, block_input, enter, wo, skip_wide, row8(gate_gain), alog,
        emat, gmat,
    )
    leave = lax.ppermute(local_dstate, "seq", down)
    for _ in range(seq_devices - 2):
        leave = lax.ppermute(local_dstate + span * leave, "seq", down)

    out_grad = reduce_split(core_sum(dot(branch, upstream, TN)))
    gate_sum = reduce_plain(core_sum(dot(normed_rows, gate_grad, TN)))

    mgrad, dz, last8, first8, cw_acc, cb_acc, dtb_acc, rate_acc = run_third(
        pre, mixed, z, states_grad, states, rdot, leave, cw8, skip_wide, alog, emat, gmat
    )
    near = lax.ppermute(first8, "seq", down)
    ends = mixed[:, local_len - 8 :, :].astype(F32)
    extra = jnp.stack(
        [
            sum(conv_weight[k] * near[:, j - k, :] for k in range(j + 1))
            for j in range(KCONV - 1)
        ],
        axis=1,
    )
    last8 = last8 + jnp.pad(extra, ((0, 0), (8 - (KCONV - 1), 0), (0, 0)))
    mgrad = lax.dynamic_update_slice(mgrad, last8.astype(BF), (0, local_len - 8, 0))
    cw_extra = jnp.stack(
        [
            sum(
                (near[:, j - k, :] * ends[:, 8 - (KCONV - 1) + j, :] for j in range(k, KCONV - 1)),
                jnp.zeros((seq_count, CONVCH), F32),
            ).sum(0)
            for k in range(KCONV)
        ]
    )
    conv_weight_grad = cw_acc.sum(1) + cw_extra
    conv_bias_grad = cb_acc.sum(0)

    mgrad_rows = mgrad.reshape(row_count, CONVCH)
    dz_rows = dz.reshape(row_count, 128)
    mixed_local = jnp.concatenate(
        [
            dot(normed_rows, mgrad_rows, TN),
            dot(normed_rows, dz_rows, TN),
        ],
        axis=1,
    )
    mixed_chip = core_sum(mixed_local)
    third_cols = mixed_chip.shape[3] // 3
    mixed_sum = jnp.concatenate(
        [
            reduce_plain(mixed_chip[..., :third_cols]),
            reduce_split(mixed_chip[..., third_cols:]),
        ],
        axis=1,
    )
    normed_grad = (
        dot(gate_grad, wg, NT) + dot(mgrad_rows, wm, NT) + dot(dz_rows, wdt, NT)
    )
    incoming = block_input.reshape(row_count, D).astype(F32)
    _, norm_back = jax.vjp(norm_piece, incoming, norm_gain)
    input_part, norm_gain_grad = norm_back(normed_grad)
    input_grad = (input_part + upstream.astype(F32)).reshape(block_input.shape)

    vector_local = jnp.concatenate(
        [
            norm_gain_grad,
            gain_acc.sum(0),
            conv_weight_grad.reshape(-1),
            conv_bias_grad,
            dtb_acc.sum(0)[:HEADS],
            -jnp.exp(decay_log) * rate_acc.sum(0)[:HEADS],
            skip_acc.sum(0).reshape(HEADS, HEADDIM).sum(1),
        ]
    )
    vector_grad = lax.psum(vector_local, AXES + ("seq",))

    in_grad = jnp.concatenate([gate_sum, mixed_sum[:, :CONVCH]], axis=1)
    dt_grad = mixed_sum[:, CONVCH : CONVCH + HEADS]

    in_update, in_left_new, in_right_new = kron_update(
        in_grad, in_left, in_right, in_left_root, in_right_root
    )
    dt_update, dt_left_wide, dt_right_wide = kron_update(
        dt_grad, dt_left[:, None], dt_right[:, None], dt_left_root[:, None], dt_right_root[:, None]
    )
    out_update, out_left_new, out_right_new = kron_update(
        out_grad, out_left, out_right, out_left_root, out_right_root
    )
    vector_moment_new = 0.5 * vector_moment + 0.5 * vector_grad * vector_grad
    vector_update = -LR_VEC * vector_grad * lax.rsqrt(vector_moment_new)
    return (
        block_output,
        input_grad,
        in_grad,
        dt_grad,
        out_grad,
        in_update,
        dt_update,
        out_update,
        in_left_new,
        in_right_new,
        dt_left_wide[:, 0],
        dt_right_wide[:, 0],
        out_left_new,
        out_right_new,
        vector_grad,
        vector_moment_new,
        vector_update,
    )


def solution(mesh):
    dp, seq = mesh.shape["dp"], mesh.shape["seq"]
    split = (4, dp // 8, 2)
    torus = jax.sharding.Mesh(mesh.devices.reshape(split + (seq,)), AXES + ("seq",))
    tokens = P(AXES, "seq", None)
    rows = P(AXES, None)
    tri = P(AXES, None, None)
    quad = P(AXES, None, None, None)
    placed = (
        (tokens, tokens, rows, rows, rows) + (P(),) * 7 + (quad,) * 4 + (tri,) * 4 + (quad,) * 4 + (P(),)
    )
    return jax.shard_map(
        body,
        mesh=torus,
        in_specs=placed,
        out_specs=(tokens, tokens)
        + (rows,) * 6
        + (quad, quad, tri, tri, quad, quad)
        + (P(), P(), P()),
        check_vma=False,
    )
```

```python
import functools

import jax
import jax.numpy as jnp
from jax import lax
from jax.experimental import pallas as pl
from jax.experimental.pallas import tpu as pltpu
from jax.sharding import PartitionSpec as P


D = 768
HEADS = 24
HEADDIM = 64
DSTATE = 128
KCONV = 4
DI = 1536
CONVCH = 1792

BL = 128
PAIRS = HEADS // 2
ROWS = 16

AXES = ("z", "x", "core")

EPS = 1e-05
LR = 0.25
LR_VEC = 0.02
NEG = -1e30
BF = jnp.bfloat16
F32 = jnp.float32
NN = (((1,), (0,)), ((), ()))
NT = (((1,), (1,)), ((), ()))
TN = (((0,), (0,)), ((), ()))


def dot(a, b, dims=NN):
    return lax.dot_general(a, b, dims, preferred_element_type=F32)


def split2(v):
    high = v.astype(BF)
    return high, (v - high.astype(F32)).astype(BF)


def dot3(a, b, dims=NN):
    ah, al = split2(a)
    bh, bl = split2(b)
    return dot(ah, bh, dims) + dot(al, bh, dims) + dot(ah, bl, dims)


def pack(v):
    high = v.astype(BF).astype(F32)
    rest = v - high
    mid = rest.astype(BF).astype(F32)
    low = rest - mid
    return (high + pltpu.roll(mid, 32, 1) + pltpu.roll(low, 64, 1)).astype(BF)


def head_lanes(shape):
    return lax.broadcasted_iota(jnp.int32, shape, 1) < HEADS


def prefix(tri, v):
    parts = dot(tri, pack(v))
    total = parts + pltpu.roll(parts, 96, 1) + pltpu.roll(parts, 64, 1)
    return jnp.where(head_lanes(total.shape), total, 0.0)


def expand(v, emat):
    return dot(pack(v), emat)


def head_sum(v, gather):
    high, low = split2(v)
    return dot(high, gather) + dot(low, gather)


def tri_mask(lower):
    rows = lax.broadcasted_iota(jnp.int32, (BL, BL), 0)
    cols = lax.broadcasted_iota(jnp.int32, (BL, BL), 1)
    return (rows >= cols) if lower else (cols >= rows)


def softplus(v):
    return jnp.maximum(v, 0.0) + jnp.log1p(jnp.exp(-jnp.abs(v)))


def sigmoid(v):
    return 1.0 / (1.0 + jnp.exp(-v))


def rates(alog_ref):
    rate = -jnp.exp(alog_ref[0:1, :])
    return jnp.where(head_lanes(rate.shape), rate, 0.0)


def pair_blocks(v):
    left = lax.broadcasted_iota(jnp.int32, v.shape, 1) < HEADDIM
    return jnp.concatenate([jnp.where(left, v, 0.0), jnp.where(left, 0.0, v)], axis=0).astype(BF)


def norm_rows(u, gain):
    inv = lax.rsqrt(jnp.mean(u * u, axis=-1, keepdims=True) + EPS)
    return u * inv * gain


def first_kernel(
    u_ref, halo_ref, gain_ref, wm_ref, wdt_ref, cw_ref, cb_ref, dtb_ref, alog_ref, emat_ref,
    normed_ref, mixed_ref, pre_ref, z_ref, state_ref, total_ref,
    tail, full,
):
    step_index = pl.program_id(1)
    tile = u_ref.shape[1]
    gain = gain_ref[0:1, :]

    @pl.when(step_index == 0)
    def _():
        near = norm_rows(halo_ref[0].astype(F32), gain).astype(BF)
        tail[...] = dot(near, wm_ref[...]).astype(BF).astype(F32)
        state_ref[...] = jnp.zeros_like(state_ref)
        total_ref[...] = jnp.zeros_like(total_ref)

    normed = norm_rows(u_ref[0].astype(F32), gain).astype(BF)
    normed_ref[0] = normed
    mixed_low = dot(normed, wm_ref[...]).astype(BF)
    mixed_ref[0] = mixed_low
    mixed = mixed_low.astype(F32)
    z = dot(normed, wdt_ref[...]).astype(BF).astype(F32) + dtb_ref[0:1, :]
    z_ref[0] = z
    full[0:8, :] = tail[...]
    full[8:, :] = mixed
    tail[...] = mixed[tile - 8 :, :]
    pre = cb_ref[0:1, :] + cw_ref[KCONV - 1 : KCONV, :] * mixed
    for tap in range(KCONV - 1):
        pre = pre + cw_ref[tap : tap + 1, :] * full[5 + tap : 5 + tap + tile, :]
    pre_ref[0] = pre
    conv = pre * sigmoid(pre)
    step_all = softplus(z)
    rate = rates(alog_ref)
    tri = jnp.where(tri_mask(True), 1.0, 0.0).astype(BF)
    emat = emat_ref[...]
    for part in range(tile // BL):
        rows = slice(part * BL, (part + 1) * BL)
        step = step_all[rows]
        cum = prefix(tri, step * rate)
        last = cum[BL - 1 : BL, :]
        weights = expand(jnp.exp(last - cum) * step, emat)
        decay = expand(
            jnp.where(head_lanes((8, 128)), jnp.broadcast_to(jnp.exp(last), (8, 128)), 0.0), emat
        )[0:1, :]
        inputs_b = conv[rows, DI : DI + DSTATE]
        fresh = dot3(inputs_b.T, weights * conv[rows, :DI])
        state_ref[0] = state_ref[0] * decay + fresh
        total_ref[0] = total_ref[0] + jnp.broadcast_to(last, (8, 128))


def second_kernel(
    pre_ref, z_ref, gate_ref, bgrad_ref, u_ref, enter_ref, wo_ref, skip_ref, ggain_ref, alog_ref,
    emat_ref, gmat_ref,
    out_ref, branch_ref, dy_ref, ggrad_ref, state_ref, rdot_ref, dstate_ref, gain_acc, skip_acc,
    state, running, xs, ys, es,
):
    step_index = pl.program_id(1)
    tile = pre_ref.shape[1]
    parts = tile // BL

    @pl.when(step_index == 0)
    def _():
        state[...] = enter_ref[0]
        running[...] = jnp.ones_like(running)
        dstate_ref[...] = jnp.zeros_like(dstate_ref)

    @pl.when((step_index == 0) & (pl.program_id(0) == 0))
    def _():
        gain_acc[...] = jnp.zeros_like(gain_acc)
        skip_acc[...] = jnp.zeros_like(skip_acc)

    rate = rates(alog_ref)
    mask = tri_mask(True)
    tri = jnp.where(mask, 1.0, 0.0).astype(BF)
    emat = emat_ref[...]
    cts = []
    for part in range(parts):
        rows = slice(part * BL, (part + 1) * BL)
        pre = pre_ref[0, rows, :]
        conv = pre * sigmoid(pre)
        x = conv[:, :DI]
        inputs_b = conv[:, DI : DI + DSTATE]
        inputs_c = conv[:, DI + DSTATE :]
        step = softplus(z_ref[0, rows, :])
        cum = prefix(tri, step * rate)
        cum_t = cum.T
        last = cum[BL - 1 : BL, :]
        lanes = head_lanes(cum.shape)
        wide = expand(
            jnp.concatenate(
                [step, jnp.where(lanes, jnp.exp(cum), 0.0), jnp.exp(last - cum) * step], axis=0
            ),
            emat,
        )
        grown = wide[BL : 2 * BL]
        decay = grown[BL - 1 : BL, :]
        scaled = wide[:BL] * x
        scores = dot3(inputs_c, inputs_b, NT)
        held = state[...]
        state_ref[0, part] = held
        outer = grown * dot3(inputs_c, held)
        state[...] = held * decay + dot3(inputs_b.T, wide[2 * BL :] * x)
        for pair in range(PAIRS):
            cols = slice(pair * 128, (pair + 1) * 128)
            mixing = []
            for h in (2 * pair, 2 * pair + 1):
                spread = jnp.where(mask, cum[:, h : h + 1] - cum_t[h : h + 1, :], NEG)
                mixing.append(scores * jnp.exp(spread))
            mh, ml = split2(jnp.concatenate(mixing, axis=1))
            piece = scaled[:, cols]
            high = piece.astype(BF).astype(F32)
            rh, rl = pair_blocks(high), pair_blocks(piece - high)
            inner = dot(mh, rh) + dot(ml, rh) + dot(mh, rl)
            ys[rows, cols] = inner + outer[:, cols]
        xs[rows, :] = x
        es[rows, :] = grown * running[0:1, :]
        running[...] = running[...] * decay
        cts.append(inputs_c.T)

    gain = ggain_ref[0:1, :]
    skip = skip_ref[0:1, :]

    def rows_step(r, carry):
        rows = pl.ds(pl.multiple_of(r * ROWS, ROWS), ROWS)
        x = xs[rows, :]
        yhat = ys[rows, :]
        states = (yhat + skip * x).astype(BF).astype(F32)
        gate = gate_ref[rows, :]
        sg = sigmoid(gate)
        sl = gate * sg
        gated = states * sl
        inv = lax.rsqrt(jnp.mean(gated * gated, axis=-1, keepdims=True) + EPS)
        norm = gated * inv
        branch_ref[rows, :] = (norm * gain).astype(BF)
        bg = bgrad_ref[rows, :]
        tg = bg * gain
        gain_acc[...] += bg * norm
        dot_row = jnp.mean(tg * norm, axis=-1, keepdims=True)
        dgated = inv * (tg - norm * dot_row)
        dy_low = (dgated * sl).astype(BF)
        dy_ref[rows, :] = dy_low
        ggrad_ref[rows, :] = (dgated * states * (sg * (1.0 + gate * (1.0 - sg)))).astype(BF)
        dy = dy_low.astype(F32)
        skip_acc[...] += dy * x
        ys[rows, :] = dy * yhat
        es[rows, :] = es[rows, :] * dy
        return carry

    lax.fori_loop(0, tile // ROWS, rows_step, 0)
    out_ref[0] = (u_ref[0].astype(F32) + dot(branch_ref[...], wo_ref[...])).astype(BF)
    rdot_ref[0] = head_sum(ys[...], gmat_ref[...])
    for part in range(parts):
        rows = slice(part * BL, (part + 1) * BL)
        dstate_ref[0] = dstate_ref[0] + dot3(cts[part], es[rows, :])


def third_kernel(
    pre_ref, mixed_ref, z_ref, dy_ref, state_ref, rdot_ref, leave_ref, cw_ref, skip_ref, alog_ref,
    emat_ref, gmat_ref,
    mgrad_ref, dz_ref, last_ref, first_ref, cw_acc, cb_acc, dtb_acc, rate_acc,
    dstate, tail, full,
):
    step_index = pl.program_id(1)

    @pl.when(step_index == 0)
    def _():
        dstate[...] = leave_ref[0]
        tail[...] = jnp.zeros_like(tail)

    @pl.when((step_index == 0) & (pl.program_id(0) == 0))
    def _():
        for ref in (cw_acc, cb_acc, dtb_acc, rate_acc):
            ref[...] = jnp.zeros_like(ref)

    rate = rates(alog_ref)
    mask = tri_mask(False)
    low_tri = jnp.where(tri_mask(True), 1.0, 0.0).astype(BF)
    high_tri = jnp.where(mask, 1.0, 0.0).astype(BF)
    emat = emat_ref[...]
    gmat = gmat_ref[...]
    skip = skip_ref[0:1, :]
    pre = pre_ref[0]
    sg = sigmoid(pre)
    conv = pre * sg
    x = conv[:, :DI]
    inputs_b = conv[:, DI : DI + DSTATE]
    inputs_c = conv[:, DI + DSTATE :]
    z = z_ref[0]
    step = softplus(z)
    cum = prefix(low_tri, step * rate)
    cum_t = cum.T
    last = cum[BL - 1 : BL, :]
    lanes = head_lanes(cum.shape)
    wide = expand(
        jnp.concatenate(
            [
                step,
                jnp.where(lanes, jnp.exp(cum), 0.0),
                jnp.where(lanes, jnp.exp(last - cum), 0.0),
            ],
            axis=0,
        ),
        emat,
    )
    dt_wide, grown, shrink = wide[:BL], wide[BL : 2 * BL], wide[2 * BL :]
    decay = grown[BL - 1 : BL, :]
    scaled = dt_wide * x
    dy = dy_ref[...].astype(F32)
    held = state_ref[0, 0]
    ds = dstate[...]
    scores_t = dot3(inputs_b, inputs_c, NT)
    dscaled_state = shrink * dot3(inputs_b, ds)
    dscores_t = jnp.zeros((BL, BL), F32)
    pieces = []
    for pair in range(PAIRS):
        cols = slice(pair * 128, (pair + 1) * 128)
        kernels = []
        for h in (2 * pair, 2 * pair + 1):
            spread = jnp.where(mask, cum_t[h : h + 1, :] - cum[:, h : h + 1], NEG)
            kernels.append(jnp.exp(spread))
        mh, ml = split2(jnp.concatenate([scores_t * k for k in kernels], axis=1))
        dyb = pair_blocks(dy[:, cols])
        pieces.append(dot(mh, dyb) + dot(ml, dyb))
        sh, sl = split2(scaled[:, cols])
        dmix = dot(sh, dyb, NT) + dot(sl, dyb, NT)
        dscores_t = dscores_t + dmix[:, :BL] * kernels[0] + dmix[:, BL:] * kernels[1]
    dscaled = jnp.concatenate(pieces, axis=1) + dscaled_state
    dx = dt_wide * dscaled + skip * dy
    grown_dy = grown * dy
    ends = jnp.sum(scaled * dscaled_state, axis=0, keepdims=True) + decay * jnp.sum(
        held * ds, axis=0, keepdims=True
    )
    sums = head_sum(
        jnp.concatenate([x * dscaled, jnp.broadcast_to(ends, (8, DI))], axis=0), gmat
    )
    direct = sums[:BL]
    is_last = lax.broadcasted_iota(jnp.int32, (BL, 128), 0) == BL - 1
    dcum = rdot_ref[0] - step * direct + jnp.where(is_last, sums[BL : BL + 1, :], 0.0)
    dcum = jnp.where(lanes, dcum, 0.0)
    drate = prefix(high_tri, dcum)
    dz = (rate * drate + direct) * sigmoid(z)
    dz_ref[0] = dz.astype(BF)
    dtb_acc[...] += jnp.sum(dz.reshape(BL // 8, 8, 128), axis=0)
    rate_acc[...] += jnp.sum((step * drate).reshape(BL // 8, 8, 128), axis=0)
    db = dot3(dscores_t, inputs_c) + dot3(shrink * scaled, ds, NT)
    dc = dot3(dscores_t.T, inputs_b) + dot3(grown_dy, held, NT)
    dstate[...] = decay * ds + dot3(inputs_c.T, grown_dy)
    dpre = jnp.concatenate([dx, db, dc], axis=1) * (sg * (1.0 + pre * (1.0 - sg)))
    full[0:BL, :] = dpre
    full[BL:, :] = tail[...]
    tail[...] = dpre[0:8, :]
    first_ref[0] = dpre[0:8, :]
    mixed = mixed_ref[0].astype(F32)
    cb_acc[...] += jnp.sum(dpre.reshape(BL // 8, 8, CONVCH), axis=0)
    mgrad = jnp.zeros_like(dpre)
    for tap in range(KCONV):
        moved = full[KCONV - 1 - tap : KCONV - 1 - tap + BL, :]
        mgrad = mgrad + cw_ref[tap : tap + 1, :] * moved
        cw_acc[tap] += jnp.sum((moved * mixed).reshape(BL // 8, 8, CONVCH), axis=0)
    mgrad_ref[0] = mgrad.astype(BF)

    @pl.when(step_index == 0)
    def _():
        last_ref[0] = mgrad[BL - 8 :, :]


PARAMS = dict(vmem_limit_bytes=60 * 1024 * 1024)


def whole(shape):
    zeros = (0,) * len(shape)
    return pl.BlockSpec(shape, lambda b, i: zeros)


def run_first(u, halo, gain, wm, wdt, cw, cb, dtb, alog, emat):
    seqs, length, _ = u.shape
    tile = min(256, length)
    grid = (seqs, length // tile)
    tok = lambda width: pl.BlockSpec((1, tile, width), lambda b, i: (b, i, 0))
    per = lambda *shape: pl.BlockSpec((1,) + shape, lambda b, i: (b,) + (0,) * len(shape))
    return pl.pallas_call(
        first_kernel,
        grid=grid,
        in_specs=[
            tok(D), per(8, D), whole(gain.shape), whole(wm.shape), whole(wdt.shape),
            whole(cw.shape), whole(cb.shape), whole(dtb.shape), whole(alog.shape), whole(emat.shape),
        ],
        out_specs=[
            tok(D), tok(CONVCH), tok(CONVCH), tok(128), per(DSTATE, DI), per(8, 128),
        ],
        out_shape=[
            jax.ShapeDtypeStruct((seqs, length, D), BF),
            jax.ShapeDtypeStruct((seqs, length, CONVCH), BF),
            jax.ShapeDtypeStruct((seqs, length, CONVCH), F32),
            jax.ShapeDtypeStruct((seqs, length, 128), F32),
            jax.ShapeDtypeStruct((seqs, DSTATE, DI), F32),
            jax.ShapeDtypeStruct((seqs, 8, 128), F32),
        ],
        scratch_shapes=[pltpu.VMEM((8, CONVCH), F32), pltpu.VMEM((tile + 8, CONVCH), F32)],
        compiler_params=pltpu.CompilerParams(**PARAMS),
        name="first",
    )(u, halo, gain, wm, wdt, cw, cb, dtb, alog, emat)


def run_second(pre, z, gate, bgrad, u, enter, wo, skip, ggain, alog, emat, gmat):
    seqs, length, _ = u.shape
    tile = min(256, length)
    steps = length // tile
    parts = tile // BL
    grid = (seqs, steps)
    tok = lambda width: pl.BlockSpec((1, tile, width), lambda b, i: (b, i, 0))
    flat = lambda width: pl.BlockSpec((tile, width), lambda b, i: (b * steps + i, 0))
    per = lambda *shape: pl.BlockSpec((1,) + shape, lambda b, i: (b,) + (0,) * len(shape))
    rows = seqs * length
    return pl.pallas_call(
        second_kernel,
        grid=grid,
        in_specs=[
            tok(CONVCH), tok(128), flat(DI), flat(DI), tok(D), per(DSTATE, DI), whole(wo.shape),
            whole(skip.shape), whole(ggain.shape), whole(alog.shape), whole(emat.shape),
            whole(gmat.shape),
        ],
        out_specs=[
            tok(D), flat(DI), flat(DI), flat(DI),
            pl.BlockSpec((1, parts, DSTATE, DI), lambda b, i: (b, i, 0, 0)),
            tok(128), per(DSTATE, DI), whole((ROWS, DI)), whole((ROWS, DI)),
        ],
        out_shape=[
            jax.ShapeDtypeStruct((seqs, length, D), BF),
            jax.ShapeDtypeStruct((rows, DI), BF),
            jax.ShapeDtypeStruct((rows, DI), BF),
            jax.ShapeDtypeStruct((rows, DI), BF),
            jax.ShapeDtypeStruct((seqs, length // BL, DSTATE, DI), F32),
            jax.ShapeDtypeStruct((seqs, length, 128), F32),
            jax.ShapeDtypeStruct((seqs, DSTATE, DI), F32),
            jax.ShapeDtypeStruct((ROWS, DI), F32),
            jax.ShapeDtypeStruct((ROWS, DI), F32),
        ],
        scratch_shapes=[
            pltpu.VMEM((DSTATE, DI), F32), pltpu.VMEM((8, DI), F32), pltpu.VMEM((tile, DI), F32),
            pltpu.VMEM((tile, DI), F32), pltpu.VMEM((tile, DI), F32),
        ],
        compiler_params=pltpu.CompilerParams(**PARAMS),
        name="second",
    )(pre, z, gate, bgrad, u, enter, wo, skip, ggain, alog, emat, gmat)


def run_third(pre, mixed, z, dy, states, rdot, leave, cw, skip, alog, emat, gmat):
    seqs, length, _ = pre.shape
    steps = length // BL
    grid = (seqs, steps)
    tok = lambda width: pl.BlockSpec((1, BL, width), lambda b, i: (b, steps - 1 - i, 0))
    per = lambda *shape: pl.BlockSpec((1,) + shape, lambda b, i: (b,) + (0,) * len(shape))
    return pl.pallas_call(
        third_kernel,
        grid=grid,
        in_specs=[
            tok(CONVCH), tok(CONVCH), tok(128),
            pl.BlockSpec((BL, DI), lambda b, i: (b * steps + steps - 1 - i, 0)),
            pl.BlockSpec((1, 1, DSTATE, DI), lambda b, i: (b, steps - 1 - i, 0, 0)),
            tok(128), per(DSTATE, DI), whole(cw.shape), whole(skip.shape), whole(alog.shape),
            whole(emat.shape), whole(gmat.shape),
        ],
        out_specs=[
            tok(CONVCH), tok(128), per(8, CONVCH), per(8, CONVCH), whole((KCONV, 8, CONVCH)),
            whole((8, CONVCH)), whole((8, 128)), whole((8, 128)),
        ],
        out_shape=[
            jax.ShapeDtypeStruct((seqs, length, CONVCH), BF),
            jax.ShapeDtypeStruct((seqs, length, 128), BF),
            jax.ShapeDtypeStruct((seqs, 8, CONVCH), F32),
            jax.ShapeDtypeStruct((seqs, 8, CONVCH), F32),
            jax.ShapeDtypeStruct((KCONV, 8, CONVCH), F32),
            jax.ShapeDtypeStruct((8, CONVCH), F32),
            jax.ShapeDtypeStruct((8, 128), F32),
            jax.ShapeDtypeStruct((8, 128), F32),
        ],
        scratch_shapes=[
            pltpu.VMEM((DSTATE, DI), F32), pltpu.VMEM((8, CONVCH), F32),
            pltpu.VMEM((BL + 8, CONVCH), F32),
        ],
        compiler_params=pltpu.CompilerParams(**PARAMS),
        name="third",
    )(pre, mixed, z, dy, states, rdot, leave, cw, skip, alog, emat, gmat)


def norm_piece(incoming, norm_gain):
    inv_rms = lax.rsqrt(jnp.mean(incoming * incoming, axis=-1, keepdims=True) + EPS)
    return incoming * inv_rms * norm_gain


def kron_update(gradient, left_stat, right_stat, left_root, right_root):
    row_tiles, col_tiles = (left_stat.shape[0], left_stat.shape[1])
    row_size, col_size = (left_stat.shape[-1], right_stat.shape[-1])
    grad_tiles = gradient.reshape(row_tiles, row_size, col_tiles, col_size).transpose(0, 2, 1, 3)
    left_new = 0.5 * left_stat + 0.5 * jnp.einsum(
        "abij,abkj->abik", grad_tiles, grad_tiles, precision=lax.Precision.HIGH
    )
    right_new = 0.5 * right_stat + 0.5 * jnp.einsum(
        "abji,abjk->abik", grad_tiles, grad_tiles, precision=lax.Precision.HIGH
    )
    shaped = jnp.einsum("abij,abjk->abik", left_root, grad_tiles, precision=lax.Precision.HIGH)
    shaped = jnp.einsum("abij,abjk->abik", shaped, right_root, precision=lax.Precision.HIGH)
    update = (-LR * shaped).transpose(0, 2, 1, 3).reshape(gradient.shape)
    return (update, left_new, right_new)


def swapped(v, axis, size, offset):
    return lax.ppermute(v, axis, [(i, (i + offset) % size) for i in range(size)])


def pick(v, index):
    return lax.dynamic_index_in_dim(v, index, 0, keepdims=False)


def scatter_stage(v, axis, kind=BF):
    size = lax.axis_size(axis)
    here = lax.axis_index(axis)
    total = pick(v, here)
    for offset in range(1, size):
        sent = pick(v, lax.rem(here + offset, size)).astype(kind)
        total = total + swapped(sent, axis, size, offset).astype(F32)
    return total


def gather_stage(v, axis):
    size = lax.axis_size(axis)
    here = lax.axis_index(axis)
    out = jnp.zeros((size,) + v.shape, v.dtype)
    out = lax.dynamic_update_index_in_dim(out, v, here, 0)
    for offset in range(1, size):
        got = swapped(v, axis, size, offset)
        out = lax.dynamic_update_index_in_dim(out, got, lax.rem(here - offset + size, size), 0)
    return out


def core_sum(partial):
    z, x, core = (lax.axis_size(a) for a in ("z", "x", "core"))
    rows, cols = partial.shape
    blocks = partial.reshape(z, x, core, rows // (z * x * core), cols)
    return scatter_stage(jnp.moveaxis(blocks, 2, 0), "core", F32)


def across(v):
    return scatter_stage(scatter_stage(jnp.moveaxis(v, 1, 0), "x"), "z")


def reduce_plain(v):
    owned = across(v)
    total = owned
    size = lax.axis_size("seq")
    if size > 2:
        return lax.psum(owned, "seq")
    for offset in range(1, size):
        total = total + swapped(owned, "seq", size, offset)
    return total


def reduce_split(v):
    size = lax.axis_size("seq")
    z, x, rows, cols = v.shape
    if cols % (128 * size):
        return reduce_plain(v)
    v = jnp.moveaxis(v.reshape(z, x, rows, size, cols // size), 3, 0)
    owned = across(scatter_stage(v, "seq"))
    return jnp.moveaxis(gather_stage(owned, "seq"), 0, 1).reshape(rows, cols)


def xor_sum(v, axis):
    size = lax.axis_size(axis)
    bit = 1
    while bit < size:
        v = v + lax.ppermute(v, axis, [(i, i ^ bit) for i in range(size)])
        bit *= 2
    return v


def fold_kernel(kinds, widths, idx, *refs):
    refs = list(refs)
    counts = {"split": (2, 4), "xz": (2, 2), "yx": (2, 2), "z": (2, 1), "plain": (2, 2), "halves": (2, 2)}
    n_in = sum(counts[k][0] for k in kinds)
    ins, outs = refs[:n_in], refs[n_in:]
    at = pl.program_id(0)
    z, x, y = idx[0], idx[1], idx[3]
    for kind, (low, width, half) in zip(kinds, widths):
        a, b = ins[0], ins[1]
        ins = ins[2:]
        mine, outs = outs[: counts[kind][1]], outs[counts[kind][1] :]
        if kind in ("split", "plain"):
            keep, send = mine[0], mine[1]
            cols = slice(low, low + width)
            keep[0] = a[0, x, 0, :, cols] + b[0, x, :, cols]
            send[0] = (a[0, 1 - x, 0, :, cols] + b[0, 1 - x, :, cols]).astype(BF)
        if kind in ("split", "halves"):
            keep, send = mine[-2], mine[-1]
            base = low + (width if kind == "split" else 0)
            own = pl.ds(pl.multiple_of(base + y * half, 128), half)
            other = pl.ds(pl.multiple_of(base + (1 - y) * half, 128), half)
            for i in range(2):
                keep[0, i] = a[0, i, 0, :, own] + b[0, i, :, own]
                send[0, i] = (a[0, i, 0, :, other] + b[0, i, :, other]).astype(BF)
        if kind == "xz":
            own, send = mine
            total = a[0] + b[0].astype(F32)
            send[0] = total.astype(BF)

            @pl.when(at == z)
            def _(own=own, total=total):
                own[...] = total

        if kind == "yx":
            keep, send = mine
            keep[0] = a[0, x] + b[0, x].astype(F32)
            send[0] = (a[0, 1 - x] + b[0, 1 - x].astype(F32)).astype(BF)
        if kind == "z":
            out = mine[0]

            @pl.when(at == 0)
            def _(out=out, a=a):
                out[...] = a[...]

            @pl.when(at != z)
            def _(out=out, b=b):
                out[...] += b[0].astype(F32)


def fold(idx, jobs):
    ins, in_specs, outs, out_specs = [], [], [], []

    def step(*shape):
        zeros = (0,) * len(shape)
        return pl.BlockSpec((1,) + shape, lambda i, idx: (i,) + zeros)

    def add_out(lead, rows, width, kind, spec=None):
        outs.append(jax.ShapeDtypeStruct(lead + (rows, width), kind))
        out_specs.append(spec or step(*(lead[1:] + (rows, width))))

    for kind, first, second, low, width, half in jobs:
        rows, cols = first.shape[-2:]
        ins += [first, second]
        if kind in ("split", "plain", "halves"):
            in_specs.append(
                pl.BlockSpec((1, 2, 1, rows, cols), lambda i, idx: (i, 0, idx[2], 0, 0))
            )
            in_specs.append(step(2, rows, cols))
            if kind in ("split", "plain"):
                add_out((4,), rows, width, F32)
                add_out((4,), rows, width, BF)
            if kind in ("split", "halves"):
                add_out((4, 2), rows, half, F32)
                add_out((4, 2), rows, half, BF)
        if kind == "xz":
            in_specs += [step(rows, cols)] * 2
            add_out((), rows, cols, F32, pl.BlockSpec((rows, cols), lambda i, idx: (0, 0)))
            add_out((4,), rows, cols, BF)
        if kind == "yx":
            in_specs += [step(2, rows, cols)] * 2
            add_out((4,), rows, cols, F32)
            add_out((4,), rows, cols, BF)
        if kind == "z":
            in_specs += [pl.BlockSpec((rows, cols), lambda i, idx: (0, 0)), step(rows, cols)]
            add_out((), rows, cols, F32, pl.BlockSpec((rows, cols), lambda i, idx: (0, 0)))
    return pl.pallas_call(
        functools.partial(fold_kernel, [j[0] for j in jobs], [j[3:] for j in jobs]),
        grid_spec=pltpu.PrefetchScalarGridSpec(
            num_scalar_prefetch=1, grid=(4,), in_specs=in_specs, out_specs=out_specs
        ),
        out_shape=outs,
        compiler_params=pltpu.CompilerParams(**PARAMS),
        name="fold",
    )(idx, *ins)


def core_exchange(partial, core):
    rows, cols = partial.shape
    blocks = partial.reshape(4, 2, 2, rows // 16, cols)
    sent = lax.dynamic_index_in_dim(blocks, 1 - core, 2, keepdims=False)
    return blocks, swapped(sent, "core", 2, 1)


def z_blocks(send):
    return lax.all_to_all(send, "z", split_axis=0, concat_axis=0, tiled=True)


def z_permutes(own, send, z):
    total = own
    for offset in range(1, 4):
        total = total + swapped(pick(send, lax.rem(z + offset, 4)), "z", 4, offset).astype(F32)
    return total


def around(v, axis):
    size = lax.axis_size(axis)
    return jnp.stack([v] + [swapped(v, axis, size, offset) for offset in range(1, size)])


def assemble_kernel(idx, near_ref, far_ref, out_ref, sems, *, order):
    sizes = {"z": 4, "x": 2, "seq": 2}
    here = {"z": idx[0], "x": idx[1], "core": idx[2], "seq": idx[3]}
    copies = []
    for a in range(near_ref.shape[0]):
        for b in range(near_ref.shape[1]):
            for c in range(near_ref.shape[2]):
                at = dict(
                    (axis, lax.rem(here[axis] - back + sizes[axis], sizes[axis]))
                    for axis, back in zip(order[::-1], (a, b, c))
                )
                for ref, core in ((near_ref, here["core"]), (far_ref, 1 - here["core"])):
                    block = ((at["z"] * 2 + at["x"]) * 2 + core) * 2 + at["seq"]
                    copies.append(
                        pltpu.make_async_copy(
                            ref.at[a, b, c], out_ref.at[block], sems.at[len(copies)]
                        )
                    )
    for copy in copies:
        copy.start()
    for copy in copies:
        copy.wait()


def assemble(idx, near, far, order):
    rows, cols = near.shape[-2:]
    out = pl.pallas_call(
        functools.partial(assemble_kernel, order=order),
        grid_spec=pltpu.PrefetchScalarGridSpec(
            num_scalar_prefetch=1,
            grid=(1,),
            in_specs=[pl.BlockSpec(memory_space=pl.ANY)] * 2,
            out_specs=pl.BlockSpec(memory_space=pl.ANY),
            scratch_shapes=[pltpu.SemaphoreType.DMA((32,))],
        ),
        out_shape=jax.ShapeDtypeStruct((32, rows, cols), near.dtype),
        name="assemble",
    )(idx, near, far)
    return out.reshape(32 * rows, cols)


def row8(v, width=None):
    v = v.reshape(1, -1)
    if width is not None:
        v = jnp.pad(v, ((0, 0), (0, width - v.shape[1])))
    return jnp.broadcast_to(v, (8, v.shape[1]))


def body(
    block_input,
    cotangent,
    in_weight,
    dt_weight,
    out_weight,
    norm_gain,
    conv_weight,
    conv_bias,
    dt_bias,
    decay_log,
    skip_gain,
    gate_gain,
    in_left,
    in_right,
    in_left_root,
    in_right_root,
    dt_left,
    dt_right,
    dt_left_root,
    dt_right_root,
    out_left,
    out_right,
    out_left_root,
    out_right_root,
    vector_moment,
):
    seq_count, local_len, _ = block_input.shape
    seq_devices = lax.axis_size("seq")
    row_count = seq_count * local_len
    up = [(i, i + 1) for i in range(seq_devices - 1)]
    down = [(i + 1, i) for i in range(seq_devices - 1)]

    in_low = in_weight.astype(BF)
    dt_low = jnp.pad(dt_weight.astype(BF), ((0, 0), (0, 128 - HEADS)))
    main = lax.all_gather(
        jnp.concatenate([in_low[:, DI:], dt_low], axis=1), AXES, axis=0, tiled=True
    )
    torus_sizes = tuple(lax.axis_size(a) for a in ("z", "x", "core", "seq"))
    direct = torus_sizes == (4, 2, 2, 2)
    idx = jnp.stack([lax.axis_index(a) for a in ("z", "x", "core", "seq")]).astype(jnp.int32)
    gate_low, out_low = in_low[:, :DI], out_weight.astype(BF)
    if direct:
        order = ("z", "x", "seq")
        gate_near = pick(gate_low.reshape(2, -1, DI), idx[3])
        out_near = pick(out_low.reshape(2, -1, D), idx[3])
        gate_near = around(around(gate_near, "z"), "x")
        out_near = around(around(out_near, "z"), "x")
        main, _, _ = lax.optimization_barrier((main, gate_near, out_near))
        gate_near = around(gate_near, "seq")
        out_near = around(out_near, "seq")
    else:
        wg = lax.all_gather(gate_low, AXES, axis=0, tiled=True)
        wo = lax.all_gather(out_low, AXES, axis=0, tiled=True)
    wm, wdt = main[:, :CONVCH], main[:, CONVCH:]
    halo = lax.ppermute(block_input[:, local_len - 8 :, :], "seq", up)

    part = jnp.arange(128)
    channel = jnp.arange(DI)
    emat = (
        ((part[:, None] % 32) == (channel[None, :] // HEADDIM)) & (part[:, None] < 96)
    ).astype(BF)
    gmat = ((channel[:, None] // HEADDIM) == part[None, :]).astype(BF)
    skip_wide = row8(jnp.repeat(skip_gain, HEADDIM))
    alog = row8(decay_log, 128)
    dtb = row8(jnp.concatenate([dt_bias, jnp.full((128 - HEADS,), -1e4, F32)]))
    cw8 = jnp.pad(conv_weight, ((0, 4), (0, 0)))

    normed, mixed, pre, z, local_state, total = run_first(
        block_input, halo, row8(norm_gain), wm, wdt, cw8, row8(conv_bias), dtb, alog, emat
    )
    span = jnp.repeat(jnp.exp(total[:, 0:1, :HEADS]), HEADDIM, axis=2)
    enter = lax.ppermute(local_state, "seq", up)
    for _ in range(seq_devices - 2):
        enter = lax.ppermute(local_state + span * enter, "seq", up)

    if direct:
        out_far = swapped(out_near, "core", 2, 1)
        gate_far = swapped(gate_near, "core", 2, 1)
        wo = assemble(idx, out_near, out_far, order)
        wg = assemble(idx, gate_near, gate_far, order)
    normed_rows = normed.reshape(row_count, D)
    upstream = cotangent.reshape(row_count, D)
    gate_part = dot(normed_rows, wg)
    branch_grad = dot(upstream, wo, NT)
    (
        block_output, branch, states_grad, gate_grad, states, rdot, local_dstate, gain_acc, skip_acc,
    ) = run_second(
        pre, z, gate_part, branch_grad, block_input, enter, wo, skip_wide, row8(gate_gain), alog,
        emat, gmat,
    )
    leave = lax.ppermute(local_dstate, "seq", down)
    for _ in range(seq_devices - 2):
        leave = lax.ppermute(local_dstate + span * leave, "seq", down)

    out_partial = dot(branch, upstream, TN)
    gate_partial = dot(normed_rows, gate_grad, TN)
    if direct:
        out_half = D // 2
        gate_blocks, gate_got = core_exchange(gate_partial, idx[2])
        out_blocks, out_got = core_exchange(out_partial, idx[2])
        gate_keep, gate_send, out_keep, out_send = fold(
            idx,
            [
                ("plain", gate_blocks, gate_got, 0, DI, 0),
                ("halves", out_blocks, out_got, 0, 0, out_half),
            ],
        )
        states_grad, gate_send, out_send = lax.optimization_barrier(
            (states_grad, gate_send, out_send)
        )
        gate_got = swapped(gate_send, "x", 2, 1)
        out_got = swapped(out_send, "seq", 2, 1)

    mgrad, dz, last8, first8, cw_acc, cb_acc, dtb_acc, rate_acc = run_third(
        pre, mixed, z, states_grad, states, rdot, leave, cw8, skip_wide, alog, emat, gmat
    )
    if direct:
        gate_own, gate_send, out_keep, out_send = fold(
            idx,
            [
                ("xz", gate_keep, gate_got, 0, 0, 0),
                ("yx", out_keep, out_got, 0, 0, 0),
            ],
        )
        mgrad, _, _ = lax.optimization_barrier((mgrad, gate_send, out_send))
        out_got = swapped(out_send, "x", 2, 1)
        gate_own = z_permutes(gate_own, gate_send, idx[0])
    else:
        gate_sum = reduce_plain(core_sum(gate_partial))
        out_grad = reduce_split(core_sum(out_partial))
    near = lax.ppermute(first8, "seq", down)
    ends = mixed[:, local_len - 8 :, :].astype(F32)
    extra = jnp.stack(
        [
            sum(conv_weight[k] * near[:, j - k, :] for k in range(j + 1))
            for j in range(KCONV - 1)
        ],
        axis=1,
    )
    last8 = last8 + jnp.pad(extra, ((0, 0), (8 - (KCONV - 1), 0), (0, 0)))
    mgrad = lax.dynamic_update_slice(mgrad, last8.astype(BF), (0, local_len - 8, 0))
    cw_extra = jnp.stack(
        [
            sum(
                (near[:, j - k, :] * ends[:, 8 - (KCONV - 1) + j, :] for j in range(k, KCONV - 1)),
                jnp.zeros((seq_count, CONVCH), F32),
            ).sum(0)
            for k in range(KCONV)
        ]
    )
    conv_weight_grad = cw_acc.sum(1) + cw_extra
    conv_bias_grad = cb_acc.sum(0)

    mgrad_rows = mgrad.reshape(row_count, CONVCH)
    dz_rows = dz.reshape(row_count, 128)
    mixed_local = jnp.concatenate(
        [
            dot(normed_rows, mgrad_rows, TN),
            dot(normed_rows, dz_rows, TN),
        ],
        axis=1,
    )
    normed_grad = (
        dot(gate_grad, wg, NT) + dot(mgrad_rows, wm, NT) + dot(dz_rows, wdt, NT)
    )
    incoming = block_input.reshape(row_count, D).astype(F32)
    _, norm_back = jax.vjp(norm_piece, incoming, norm_gain)
    input_part, norm_gain_grad = norm_back(normed_grad)
    input_grad = (input_part + upstream.astype(F32)).reshape(block_input.shape)

    vector_local = jnp.concatenate(
        [
            norm_gain_grad,
            gain_acc.sum(0),
            conv_weight_grad.reshape(-1),
            conv_bias_grad,
            dtb_acc.sum(0)[:HEADS],
            -jnp.exp(decay_log) * rate_acc.sum(0)[:HEADS],
            skip_acc.sum(0).reshape(HEADS, HEADDIM).sum(1),
        ]
    )
    if direct:
        side = (CONVCH + 128) // 3
        blocks, got = core_exchange(mixed_local, idx[2])
        plain_keep, plain_send, half_keep, half_send = fold(
            idx, [("split", blocks, got, 0, side, side)]
        )
        out_got, vector_local, _, _ = lax.optimization_barrier(
            (out_got, vector_local, plain_send, half_send)
        )
        half_got = swapped(half_send, "seq", 2, 1)
        plain_got = swapped(plain_send, "x", 2, 1)
        out_own, out_send = fold(idx, [("xz", out_keep, out_got, 0, 0, 0)])
        gate_sum = gate_own + swapped(gate_own, "seq", 2, 1)
        out_own = z_permutes(out_own, out_send, idx[0])
        out_grad = jnp.moveaxis(gather_stage(out_own, "seq"), 0, 1).reshape(-1, D)
        plain_own, plain_send, half_keep, half_send = fold(
            idx,
            [
                ("xz", plain_keep, plain_got, 0, 0, 0),
                ("yx", half_keep, half_got, 0, 0, 0),
            ],
        )
        half_got = swapped(half_send, "x", 2, 1)
        plain_got = z_blocks(plain_send)
        plain_own, half_own, half_send = fold(
            idx,
            [
                ("z", plain_own, plain_got, 0, 0, 0),
                ("xz", half_keep, half_got, 0, 0, 0),
            ],
        )
        plain_got = swapped(plain_own, "seq", 2, 1)
        half_got = z_blocks(half_send)
        (half_own,) = fold(idx, [("z", half_own, half_got, 0, 0, 0)])
        halves = gather_stage(half_own, "seq")
        mixed_sum = jnp.concatenate([plain_own + plain_got, halves[0], halves[1]], axis=1)
    else:
        mixed_chip = core_sum(mixed_local)
        third_cols = mixed_chip.shape[3] // 3
        mixed_sum = jnp.concatenate(
            [
                reduce_plain(mixed_chip[..., :third_cols]),
                reduce_split(mixed_chip[..., third_cols:]),
            ],
            axis=1,
        )

    vector_rows = jnp.pad(vector_local, (0, -vector_local.shape[0] % 1024)).reshape(-1, 128)
    for axis in ("core", "seq", "x", "z"):
        vector_rows = xor_sum(vector_rows, axis)
    vector_grad = vector_rows.reshape(-1)[: vector_local.shape[0]]

    in_grad = jnp.concatenate([gate_sum, mixed_sum[:, :CONVCH]], axis=1)
    dt_grad = mixed_sum[:, CONVCH : CONVCH + HEADS]

    in_update, in_left_new, in_right_new = kron_update(
        in_grad, in_left, in_right, in_left_root, in_right_root
    )
    dt_update, dt_left_wide, dt_right_wide = kron_update(
        dt_grad, dt_left[:, None], dt_right[:, None], dt_left_root[:, None], dt_right_root[:, None]
    )
    out_update, out_left_new, out_right_new = kron_update(
        out_grad, out_left, out_right, out_left_root, out_right_root
    )
    vector_moment_new = 0.5 * vector_moment + 0.5 * vector_grad * vector_grad
    vector_update = -LR_VEC * vector_grad * lax.rsqrt(vector_moment_new)
    return (
        block_output,
        input_grad,
        in_grad,
        dt_grad,
        out_grad,
        in_update,
        dt_update,
        out_update,
        in_left_new,
        in_right_new,
        dt_left_wide[:, 0],
        dt_right_wide[:, 0],
        out_left_new,
        out_right_new,
        vector_grad,
        vector_moment_new,
        vector_update,
    )


def solution(mesh):
    dp, seq = mesh.shape["dp"], mesh.shape["seq"]
    split = (4, dp // 8, 2)
    torus = jax.sharding.Mesh(mesh.devices.reshape(split + (seq,)), AXES + ("seq",))
    tokens = P(AXES, "seq", None)
    rows = P(AXES, None)
    tri = P(AXES, None, None)
    quad = P(AXES, None, None, None)
    placed = (
        (tokens, tokens, rows, rows, rows) + (P(),) * 7 + (quad,) * 4 + (tri,) * 4 + (quad,) * 4 + (P(),)
    )

    return jax.shard_map(
        body,
        mesh=torus,
        in_specs=placed,
        out_specs=(tokens, tokens)
        + (rows,) * 6
        + (quad, quad, tri, tri, quad, quad)
        + (P(), P(), P()),
        check_vma=False,
    )
```

```python
import functools

import jax
import jax.numpy as jnp
from jax import lax
from jax.experimental import pallas as pl
from jax.experimental.pallas import tpu as pltpu
from jax.sharding import PartitionSpec as P


D = 768
HEADS = 24
HEADDIM = 64
DSTATE = 128
KCONV = 4
DI = 1536
CONVCH = 1792
WIDE = CONVCH + 128

BL = 128
PAIRS = HEADS // 2
ROWS = 16

AXES = ("z", "x", "core")

EPS = 1e-05
LR = 0.25
LR_VEC = 0.02
NEG = -1e30
BF = jnp.bfloat16
F32 = jnp.float32
NN = (((1,), (0,)), ((), ()))
NT = (((1,), (1,)), ((), ()))
TN = (((0,), (0,)), ((), ()))


def dot(a, b, dims=NN):
    return lax.dot_general(a, b, dims, preferred_element_type=F32)


def split2(v):
    high = v.astype(BF)
    return high, (v - high.astype(F32)).astype(BF)


def dot3(a, b, dims=NN):
    ah, al = split2(a)
    bh, bl = split2(b)
    return dot(ah, bh, dims) + dot(al, bh, dims) + dot(ah, bl, dims)


def pack(v):
    high = v.astype(BF).astype(F32)
    rest = v - high
    mid = rest.astype(BF).astype(F32)
    low = rest - mid
    return (high + pltpu.roll(mid, 32, 1) + pltpu.roll(low, 64, 1)).astype(BF)


def head_lanes(shape):
    return lax.broadcasted_iota(jnp.int32, shape, 1) < HEADS


def prefix(tri, v):
    parts = dot(tri, pack(v))
    total = parts + pltpu.roll(parts, 96, 1) + pltpu.roll(parts, 64, 1)
    return jnp.where(head_lanes(total.shape), total, 0.0)


def expand(v, emat):
    return dot(pack(v), emat)


def head_sum(v, gather):
    high, low = split2(v)
    return dot(high, gather) + dot(low, gather)


def tri_mask(lower):
    rows = lax.broadcasted_iota(jnp.int32, (BL, BL), 0)
    cols = lax.broadcasted_iota(jnp.int32, (BL, BL), 1)
    return (rows >= cols) if lower else (cols >= rows)


def softplus(v):
    return jnp.maximum(v, 0.0) + jnp.log1p(jnp.exp(-jnp.abs(v)))


def sigmoid(v):
    return 1.0 / (1.0 + jnp.exp(-v))


def rates(alog_ref):
    rate = -jnp.exp(alog_ref[0:1, :])
    return jnp.where(head_lanes(rate.shape), rate, 0.0)


def pair_blocks(v):
    left = lax.broadcasted_iota(jnp.int32, v.shape, 1) < HEADDIM
    return jnp.concatenate([jnp.where(left, v, 0.0), jnp.where(left, 0.0, v)], axis=0).astype(BF)


def norm_rows(u, gain):
    inv = lax.rsqrt(jnp.mean(u * u, axis=-1, keepdims=True) + EPS)
    return u * inv * gain


def first_kernel(
    u_ref, halo_ref, gain_ref, w_ref, cw_ref, cb_ref, dtb_ref, alog_ref, emat_ref,
    normed_ref, mixed_ref, pre_ref, z_ref, state_ref, total_ref,
    tail, full,
):
    step_index = pl.program_id(1)
    tile = u_ref.shape[1]
    gain = gain_ref[0:1, :]

    @pl.when(step_index == 0)
    def _():
        near = norm_rows(halo_ref[0].astype(F32), gain).astype(BF)
        tail[...] = dot(near, w_ref[:, :CONVCH]).astype(BF).astype(F32)
        state_ref[...] = jnp.zeros_like(state_ref)
        total_ref[...] = jnp.zeros_like(total_ref)

    normed = norm_rows(u_ref[0].astype(F32), gain).astype(BF)
    normed_ref[0] = normed
    projected = dot(normed, w_ref[...])
    mixed_low = projected[:, :CONVCH].astype(BF)
    mixed_ref[0] = mixed_low
    mixed = mixed_low.astype(F32)
    z = projected[:, CONVCH:].astype(BF).astype(F32) + dtb_ref[0:1, :]
    z_ref[0] = z
    full[0:8, :] = tail[...]
    full[8:, :] = mixed
    tail[...] = mixed[tile - 8 :, :]
    pre = cb_ref[0:1, :] + cw_ref[KCONV - 1 : KCONV, :] * mixed
    for tap in range(KCONV - 1):
        pre = pre + cw_ref[tap : tap + 1, :] * full[5 + tap : 5 + tap + tile, :]
    pre_ref[0] = pre
    conv = pre * sigmoid(pre)
    step_all = softplus(z)
    rate = rates(alog_ref)
    tri = jnp.where(tri_mask(True), 1.0, 0.0).astype(BF)
    emat = emat_ref[...]
    for part in range(tile // BL):
        rows = slice(part * BL, (part + 1) * BL)
        step = step_all[rows]
        cum = prefix(tri, step * rate)
        last = cum[BL - 1 : BL, :]
        weights = expand(jnp.exp(last - cum) * step, emat)
        decay = expand(
            jnp.where(head_lanes((8, 128)), jnp.broadcast_to(jnp.exp(last), (8, 128)), 0.0), emat
        )[0:1, :]
        inputs_b = conv[rows, DI : DI + DSTATE]
        fresh = dot3(inputs_b.T, weights * conv[rows, :DI])
        state_ref[0] = state_ref[0] * decay + fresh
        total_ref[0] = total_ref[0] + jnp.broadcast_to(last, (8, 128))


def second_kernel(
    pre_ref, z_ref, gate_ref, bgrad_ref, u_ref, enter_ref, wo_ref, skip_ref, ggain_ref, alog_ref,
    emat_ref, gmat_ref,
    out_ref, branch_ref, dy_ref, ggrad_ref, state_ref, rdot_ref, dstate_ref, sums_ref,
    gain_acc, skip_acc, state, running, xs, ys, es,
):
    step_index = pl.program_id(1)
    tile = pre_ref.shape[1]
    parts = tile // BL

    @pl.when(step_index == 0)
    def _():
        state[...] = enter_ref[0]
        running[...] = jnp.ones_like(running)
        dstate_ref[...] = jnp.zeros_like(dstate_ref)

    @pl.when((step_index == 0) & (pl.program_id(0) == 0))
    def _():
        gain_acc[...] = jnp.zeros_like(gain_acc)
        skip_acc[...] = jnp.zeros_like(skip_acc)

    rate = rates(alog_ref)
    mask = tri_mask(True)
    tri = jnp.where(mask, 1.0, 0.0).astype(BF)
    emat = emat_ref[...]
    cts = []
    for part in range(parts):
        rows = slice(part * BL, (part + 1) * BL)
        pre = pre_ref[0, rows, :]
        conv = pre * sigmoid(pre)
        x = conv[:, :DI]
        inputs_b = conv[:, DI : DI + DSTATE]
        inputs_c = conv[:, DI + DSTATE :]
        step = softplus(z_ref[0, rows, :])
        cum = prefix(tri, step * rate)
        cum_t = cum.T
        last = cum[BL - 1 : BL, :]
        lanes = head_lanes(cum.shape)
        wide = expand(
            jnp.concatenate(
                [step, jnp.where(lanes, jnp.exp(cum), 0.0), jnp.exp(last - cum) * step], axis=0
            ),
            emat,
        )
        grown = wide[BL : 2 * BL]
        decay = grown[BL - 1 : BL, :]
        scaled = wide[:BL] * x
        scores = dot3(inputs_c, inputs_b, NT)
        held = state[...]
        state_ref[0, part] = held
        outer = grown * dot3(inputs_c, held)
        state[...] = held * decay + dot3(inputs_b.T, wide[2 * BL :] * x)
        for pair in range(PAIRS):
            cols = slice(pair * 128, (pair + 1) * 128)
            mixing = []
            for h in (2 * pair, 2 * pair + 1):
                spread = jnp.where(mask, cum[:, h : h + 1] - cum_t[h : h + 1, :], NEG)
                mixing.append(scores * jnp.exp(spread))
            mh, ml = split2(jnp.concatenate(mixing, axis=1))
            piece = scaled[:, cols]
            high = piece.astype(BF).astype(F32)
            rh, rl = pair_blocks(high), pair_blocks(piece - high)
            inner = dot(mh, rh) + dot(ml, rh) + dot(mh, rl)
            ys[rows, cols] = inner + outer[:, cols]
        xs[rows, :] = x
        es[rows, :] = grown * running[0:1, :]
        running[...] = running[...] * decay
        cts.append(inputs_c.T)

    gain = ggain_ref[0:1, :]
    skip = skip_ref[0:1, :]

    def rows_step(r, carry):
        rows = pl.ds(pl.multiple_of(r * ROWS, ROWS), ROWS)
        x = xs[rows, :]
        yhat = ys[rows, :]
        states = (yhat + skip * x).astype(BF).astype(F32)
        gate = gate_ref[rows, :]
        sg = sigmoid(gate)
        sl = gate * sg
        gated = states * sl
        inv = lax.rsqrt(jnp.mean(gated * gated, axis=-1, keepdims=True) + EPS)
        norm = gated * inv
        branch_ref[rows, :] = (norm * gain).astype(BF)
        bg = bgrad_ref[rows, :]
        tg = bg * gain
        gain_acc[...] += bg * norm
        dot_row = jnp.mean(tg * norm, axis=-1, keepdims=True)
        dgated = inv * (tg - norm * dot_row)
        dy_low = (dgated * sl).astype(BF)
        dy_ref[rows, :] = dy_low
        ggrad_ref[rows, :] = (dgated * states * (sg * (1.0 + gate * (1.0 - sg)))).astype(BF)
        dy = dy_low.astype(F32)
        skip_acc[...] += dy * x
        ys[rows, :] = dy * yhat
        es[rows, :] = es[rows, :] * dy
        return carry

    lax.fori_loop(0, tile // ROWS, rows_step, 0)
    out_ref[0] = (u_ref[0].astype(F32) + dot(branch_ref[...], wo_ref[...])).astype(BF)
    rdot_ref[0] = head_sum(ys[...], gmat_ref[...])
    for part in range(parts):
        rows = slice(part * BL, (part + 1) * BL)
        dstate_ref[0] = dstate_ref[0] + dot3(cts[part], es[rows, :])

    @pl.when((step_index == pl.num_programs(1) - 1) & (pl.program_id(0) == pl.num_programs(0) - 1))
    def _():
        sums_ref[0:1, :] = jnp.sum(gain_acc[...], axis=0, keepdims=True)
        sums_ref[1:2, :] = jnp.sum(skip_acc[...], axis=0, keepdims=True)


def third_kernel(
    pre_ref, mixed_ref, z_ref, dy_ref, state_ref, rdot_ref, leave_ref, cw_ref, skip_ref, alog_ref,
    emat_ref, gmat_ref,
    mgrad_ref, last_ref, first_ref, sums_ref,
    cw_acc, cb_acc, dtb_acc, rate_acc, dstate, tail, full,
):
    step_index = pl.program_id(1)

    @pl.when(step_index == 0)
    def _():
        dstate[...] = leave_ref[0]
        tail[...] = jnp.zeros_like(tail)

    @pl.when((step_index == 0) & (pl.program_id(0) == 0))
    def _():
        for ref in (cw_acc, cb_acc, dtb_acc, rate_acc):
            ref[...] = jnp.zeros_like(ref)

    rate = rates(alog_ref)
    mask = tri_mask(False)
    low_tri = jnp.where(tri_mask(True), 1.0, 0.0).astype(BF)
    high_tri = jnp.where(mask, 1.0, 0.0).astype(BF)
    emat = emat_ref[...]
    gmat = gmat_ref[...]
    skip = skip_ref[0:1, :]
    pre = pre_ref[0]
    sg = sigmoid(pre)
    conv = pre * sg
    x = conv[:, :DI]
    inputs_b = conv[:, DI : DI + DSTATE]
    inputs_c = conv[:, DI + DSTATE :]
    z = z_ref[0]
    step = softplus(z)
    cum = prefix(low_tri, step * rate)
    cum_t = cum.T
    last = cum[BL - 1 : BL, :]
    lanes = head_lanes(cum.shape)
    wide = expand(
        jnp.concatenate(
            [
                step,
                jnp.where(lanes, jnp.exp(cum), 0.0),
                jnp.where(lanes, jnp.exp(last - cum), 0.0),
            ],
            axis=0,
        ),
        emat,
    )
    dt_wide, grown, shrink = wide[:BL], wide[BL : 2 * BL], wide[2 * BL :]
    decay = grown[BL - 1 : BL, :]
    scaled = dt_wide * x
    dy = dy_ref[...].astype(F32)
    held = state_ref[0, 0]
    ds = dstate[...]
    scores_t = dot3(inputs_b, inputs_c, NT)
    dscaled_state = shrink * dot3(inputs_b, ds)
    dscores_t = jnp.zeros((BL, BL), F32)
    pieces = []
    for pair in range(PAIRS):
        cols = slice(pair * 128, (pair + 1) * 128)
        kernels = []
        for h in (2 * pair, 2 * pair + 1):
            spread = jnp.where(mask, cum_t[h : h + 1, :] - cum[:, h : h + 1], NEG)
            kernels.append(jnp.exp(spread))
        mh, ml = split2(jnp.concatenate([scores_t * k for k in kernels], axis=1))
        dyb = pair_blocks(dy[:, cols])
        pieces.append(dot(mh, dyb) + dot(ml, dyb))
        sh, sl = split2(scaled[:, cols])
        dmix = dot(sh, dyb, NT) + dot(sl, dyb, NT)
        dscores_t = dscores_t + dmix[:, :BL] * kernels[0] + dmix[:, BL:] * kernels[1]
    dscaled = jnp.concatenate(pieces, axis=1) + dscaled_state
    dx = dt_wide * dscaled + skip * dy
    grown_dy = grown * dy
    ends = jnp.sum(scaled * dscaled_state, axis=0, keepdims=True) + decay * jnp.sum(
        held * ds, axis=0, keepdims=True
    )
    sums = head_sum(
        jnp.concatenate([x * dscaled, jnp.broadcast_to(ends, (8, DI))], axis=0), gmat
    )
    direct = sums[:BL]
    is_last = lax.broadcasted_iota(jnp.int32, (BL, 128), 0) == BL - 1
    dcum = rdot_ref[0] - step * direct + jnp.where(is_last, sums[BL : BL + 1, :], 0.0)
    dcum = jnp.where(lanes, dcum, 0.0)
    drate = prefix(high_tri, dcum)
    dz = (rate * drate + direct) * sigmoid(z)
    mgrad_ref[0, :, CONVCH:] = dz.astype(BF)
    dtb_acc[...] += jnp.sum(dz.reshape(BL // 8, 8, 128), axis=0)
    rate_acc[...] += jnp.sum((step * drate).reshape(BL // 8, 8, 128), axis=0)
    db = dot3(dscores_t, inputs_c) + dot3(shrink * scaled, ds, NT)
    dc = dot3(dscores_t.T, inputs_b) + dot3(grown_dy, held, NT)
    dstate[...] = decay * ds + dot3(inputs_c.T, grown_dy)
    dpre = jnp.concatenate([dx, db, dc], axis=1) * (sg * (1.0 + pre * (1.0 - sg)))
    full[0:BL, :] = dpre
    full[BL:, :] = tail[...]
    tail[...] = dpre[0:8, :]
    first_ref[0] = dpre[0:8, :]
    mixed = mixed_ref[0].astype(F32)
    cb_acc[...] += jnp.sum(dpre.reshape(BL // 8, 8, CONVCH), axis=0)
    mgrad = jnp.zeros_like(dpre)
    for tap in range(KCONV):
        moved = full[KCONV - 1 - tap : KCONV - 1 - tap + BL, :]
        mgrad = mgrad + cw_ref[tap : tap + 1, :] * moved
        cw_acc[tap] += jnp.sum((moved * mixed).reshape(BL // 8, 8, CONVCH), axis=0)
    mgrad_ref[0, :, :CONVCH] = mgrad.astype(BF)

    @pl.when(step_index == 0)
    def _():
        last_ref[0] = mgrad[BL - 8 :, :]

    @pl.when((step_index == pl.num_programs(1) - 1) & (pl.program_id(0) == pl.num_programs(0) - 1))
    def _():
        for tap in range(KCONV):
            sums_ref[tap : tap + 1, :] = jnp.sum(cw_acc[tap], axis=0, keepdims=True)
        sums_ref[4:5, :] = jnp.sum(cb_acc[...], axis=0, keepdims=True)
        sums_ref[5:6, :128] = jnp.sum(dtb_acc[...], axis=0, keepdims=True)
        sums_ref[6:7, :128] = jnp.sum(rate_acc[...], axis=0, keepdims=True)


def patch_kernel(mgrad_ref, mixed_ref, last_ref, near_ref, cw_ref, out_ref, extra_ref):
    @pl.when(pl.program_id(0) == 0)
    def _():
        extra_ref[...] = jnp.zeros_like(extra_ref)

    rows = [last_ref[0, i : i + 1, :] for i in range(8)]
    near = [near_ref[0, i : i + 1, :] for i in range(KCONV - 1)]
    held = mixed_ref[0].astype(F32)
    first = 8 - (KCONV - 1)
    for k in range(KCONV - 1):
        for j in range(k, KCONV - 1):
            rows[first + j] = rows[first + j] + cw_ref[k : k + 1, :] * near[j - k]
            extra_ref[k : k + 1, :] += near[j - k] * held[8 + first + j : 9 + first + j, :]
    old = mgrad_ref[0].astype(F32)
    patched = jnp.concatenate([old[:8, :CONVCH], jnp.concatenate(rows, axis=0)], axis=0)
    out_ref[0, :, :CONVCH] = patched.astype(BF)
    out_ref[0, :, CONVCH:] = mgrad_ref[0, :, CONVCH:]


PARAMS = dict(vmem_limit_bytes=60 * 1024 * 1024)


def whole(shape):
    zeros = (0,) * len(shape)
    return pl.BlockSpec(shape, lambda b, i: zeros)


def run_first(u, halo, gain, w, cw, cb, dtb, alog, emat):
    seqs, length, _ = u.shape
    tile = min(256, length)
    grid = (seqs, length // tile)
    tok = lambda width: pl.BlockSpec((1, tile, width), lambda b, i: (b, i, 0))
    per = lambda *shape: pl.BlockSpec((1,) + shape, lambda b, i: (b,) + (0,) * len(shape))
    return pl.pallas_call(
        first_kernel,
        grid=grid,
        in_specs=[
            tok(D), per(8, D), whole(gain.shape), whole(w.shape),
            whole(cw.shape), whole(cb.shape), whole(dtb.shape), whole(alog.shape), whole(emat.shape),
        ],
        out_specs=[
            tok(D), tok(CONVCH), tok(CONVCH), tok(128), per(DSTATE, DI), per(8, 128),
        ],
        out_shape=[
            jax.ShapeDtypeStruct((seqs, length, D), BF),
            jax.ShapeDtypeStruct((seqs, length, CONVCH), BF),
            jax.ShapeDtypeStruct((seqs, length, CONVCH), F32),
            jax.ShapeDtypeStruct((seqs, length, 128), F32),
            jax.ShapeDtypeStruct((seqs, DSTATE, DI), F32),
            jax.ShapeDtypeStruct((seqs, 8, 128), F32),
        ],
        scratch_shapes=[pltpu.VMEM((8, CONVCH), F32), pltpu.VMEM((tile + 8, CONVCH), F32)],
        compiler_params=pltpu.CompilerParams(**PARAMS),
        name="first",
    )(u, halo, gain, w, cw, cb, dtb, alog, emat)


def run_second(pre, z, gate, bgrad, u, enter, wo, skip, ggain, alog, emat, gmat):
    seqs, length, _ = u.shape
    tile = min(256, length)
    steps = length // tile
    parts = tile // BL
    grid = (seqs, steps)
    tok = lambda width: pl.BlockSpec((1, tile, width), lambda b, i: (b, i, 0))
    flat = lambda width: pl.BlockSpec((tile, width), lambda b, i: (b * steps + i, 0))
    per = lambda *shape: pl.BlockSpec((1,) + shape, lambda b, i: (b,) + (0,) * len(shape))
    rows = seqs * length
    return pl.pallas_call(
        second_kernel,
        grid=grid,
        in_specs=[
            tok(CONVCH), tok(128), flat(DI), flat(DI), tok(D), per(DSTATE, DI), whole(wo.shape),
            whole(skip.shape), whole(ggain.shape), whole(alog.shape), whole(emat.shape),
            whole(gmat.shape),
        ],
        out_specs=[
            tok(D), flat(DI), flat(DI), flat(DI),
            pl.BlockSpec((1, parts, DSTATE, DI), lambda b, i: (b, i, 0, 0)),
            tok(128), per(DSTATE, DI), whole((8, DI)),
        ],
        out_shape=[
            jax.ShapeDtypeStruct((seqs, length, D), BF),
            jax.ShapeDtypeStruct((rows, DI), BF),
            jax.ShapeDtypeStruct((rows, DI), BF),
            jax.ShapeDtypeStruct((rows, DI), BF),
            jax.ShapeDtypeStruct((seqs, length // BL, DSTATE, DI), F32),
            jax.ShapeDtypeStruct((seqs, length, 128), F32),
            jax.ShapeDtypeStruct((seqs, DSTATE, DI), F32),
            jax.ShapeDtypeStruct((8, DI), F32),
        ],
        scratch_shapes=[
            pltpu.VMEM((ROWS, DI), F32), pltpu.VMEM((ROWS, DI), F32),
            pltpu.VMEM((DSTATE, DI), F32), pltpu.VMEM((8, DI), F32), pltpu.VMEM((tile, DI), F32),
            pltpu.VMEM((tile, DI), F32), pltpu.VMEM((tile, DI), F32),
        ],
        compiler_params=pltpu.CompilerParams(**PARAMS),
        name="second",
    )(pre, z, gate, bgrad, u, enter, wo, skip, ggain, alog, emat, gmat)


def run_third(pre, mixed, z, dy, states, rdot, leave, cw, skip, alog, emat, gmat):
    seqs, length, _ = pre.shape
    steps = length // BL
    grid = (seqs, steps)
    tok = lambda width: pl.BlockSpec((1, BL, width), lambda b, i: (b, steps - 1 - i, 0))
    per = lambda *shape: pl.BlockSpec((1,) + shape, lambda b, i: (b,) + (0,) * len(shape))
    return pl.pallas_call(
        third_kernel,
        grid=grid,
        in_specs=[
            tok(CONVCH), tok(CONVCH), tok(128),
            pl.BlockSpec((BL, DI), lambda b, i: (b * steps + steps - 1 - i, 0)),
            pl.BlockSpec((1, 1, DSTATE, DI), lambda b, i: (b, steps - 1 - i, 0, 0)),
            tok(128), per(DSTATE, DI), whole(cw.shape), whole(skip.shape), whole(alog.shape),
            whole(emat.shape), whole(gmat.shape),
        ],
        out_specs=[
            tok(WIDE), per(8, CONVCH), per(8, CONVCH), whole((8, CONVCH)),
        ],
        out_shape=[
            jax.ShapeDtypeStruct((seqs, length, WIDE), BF),
            jax.ShapeDtypeStruct((seqs, 8, CONVCH), F32),
            jax.ShapeDtypeStruct((seqs, 8, CONVCH), F32),
            jax.ShapeDtypeStruct((8, CONVCH), F32),
        ],
        scratch_shapes=[
            pltpu.VMEM((KCONV, 8, CONVCH), F32), pltpu.VMEM((8, CONVCH), F32),
            pltpu.VMEM((8, 128), F32), pltpu.VMEM((8, 128), F32),
            pltpu.VMEM((DSTATE, DI), F32), pltpu.VMEM((8, CONVCH), F32),
            pltpu.VMEM((BL + 8, CONVCH), F32),
        ],
        compiler_params=pltpu.CompilerParams(**PARAMS),
        name="third",
    )(pre, mixed, z, dy, states, rdot, leave, cw, skip, alog, emat, gmat)


def run_patch(mgrad, mixed, last8, near, cw):
    seqs, length, _ = mgrad.shape
    end = length // 16 - 1
    tok = lambda width: pl.BlockSpec((1, 16, width), lambda b: (b, end, 0))
    per = pl.BlockSpec((1, 8, CONVCH), lambda b: (b, 0, 0))
    row = pl.BlockSpec((8, CONVCH), lambda b: (0, 0))
    return pl.pallas_call(
        patch_kernel,
        grid=(seqs,),
        in_specs=[tok(WIDE), tok(CONVCH), per, per, row],
        out_specs=[tok(WIDE), row],
        out_shape=[
            jax.ShapeDtypeStruct(mgrad.shape, BF),
            jax.ShapeDtypeStruct((8, CONVCH), F32),
        ],
        input_output_aliases={0: 0},
        name="patch",
    )(mgrad, mixed, last8, near, cw)


def norm_piece(incoming, norm_gain):
    inv_rms = lax.rsqrt(jnp.mean(incoming * incoming, axis=-1, keepdims=True) + EPS)
    return incoming * inv_rms * norm_gain


def kron_update(gradient, left_stat, right_stat, left_root, right_root):
    row_tiles, col_tiles = (left_stat.shape[0], left_stat.shape[1])
    row_size, col_size = (left_stat.shape[-1], right_stat.shape[-1])
    grad_tiles = gradient.reshape(row_tiles, row_size, col_tiles, col_size).transpose(0, 2, 1, 3)
    left_new = 0.5 * left_stat + 0.5 * jnp.einsum(
        "abij,abkj->abik", grad_tiles, grad_tiles, precision=lax.Precision.HIGH
    )
    right_new = 0.5 * right_stat + 0.5 * jnp.einsum(
        "abji,abjk->abik", grad_tiles, grad_tiles, precision=lax.Precision.HIGH
    )
    shaped = jnp.einsum("abij,abjk->abik", left_root, grad_tiles, precision=lax.Precision.HIGH)
    shaped = jnp.einsum("abij,abjk->abik", shaped, right_root, precision=lax.Precision.HIGH)
    update = (-LR * shaped).transpose(0, 2, 1, 3).reshape(gradient.shape)
    return (update, left_new, right_new)


def swapped(v, axis, size, offset):
    return lax.ppermute(v, axis, [(i, (i + offset) % size) for i in range(size)])


def pick(v, index):
    return lax.dynamic_index_in_dim(v, index, 0, keepdims=False)


def scatter_stage(v, axis, kind=BF):
    size = lax.axis_size(axis)
    here = lax.axis_index(axis)
    total = pick(v, here)
    for offset in range(1, size):
        sent = pick(v, lax.rem(here + offset, size)).astype(kind)
        total = total + swapped(sent, axis, size, offset).astype(F32)
    return total


def gather_stage(v, axis):
    size = lax.axis_size(axis)
    here = lax.axis_index(axis)
    out = jnp.zeros((size,) + v.shape, v.dtype)
    out = lax.dynamic_update_index_in_dim(out, v, here, 0)
    for offset in range(1, size):
        got = swapped(v, axis, size, offset)
        out = lax.dynamic_update_index_in_dim(out, got, lax.rem(here - offset + size, size), 0)
    return out


def core_sum(partial):
    z, x, core = (lax.axis_size(a) for a in ("z", "x", "core"))
    rows, cols = partial.shape
    blocks = partial.reshape(z, x, core, rows // (z * x * core), cols)
    return scatter_stage(jnp.moveaxis(blocks, 2, 0), "core", F32)


def across(v):
    return scatter_stage(scatter_stage(jnp.moveaxis(v, 1, 0), "x"), "z")


def reduce_plain(v):
    owned = across(v)
    total = owned
    size = lax.axis_size("seq")
    if size > 2:
        return lax.psum(owned, "seq")
    for offset in range(1, size):
        total = total + swapped(owned, "seq", size, offset)
    return total


def reduce_split(v):
    size = lax.axis_size("seq")
    z, x, rows, cols = v.shape
    if cols % (128 * size):
        return reduce_plain(v)
    v = jnp.moveaxis(v.reshape(z, x, rows, size, cols // size), 3, 0)
    owned = across(scatter_stage(v, "seq"))
    return jnp.moveaxis(gather_stage(owned, "seq"), 0, 1).reshape(rows, cols)


def xor_sum(v, axis):
    size = lax.axis_size(axis)
    bit = 1
    while bit < size:
        v = v + lax.ppermute(v, axis, [(i, i ^ bit) for i in range(size)])
        bit *= 2
    return v


def chip_kernel(idx, *refs):
    send_ref, own_ref = refs[-2:]
    pieces = []
    for part_ref, got_ref in zip(refs[:-2:2], refs[1:-2:2]):
        total = part_ref[0, 0] + got_ref[0]
        width = own_ref.shape[1]
        rows = total.shape[0] * total.shape[1] // width
        pieces += [
            total[i * rows : (i + 1) * rows] for i in range(total.shape[0] // rows)
        ]
    mine = pl.program_id(0) == idx[0] * 2 + idx[1]
    row = 0
    col = 0
    for piece in pieces:
        rows, cols = piece.shape
        at = (slice(row, row + rows), slice(col, col + cols))
        send_ref[(0,) + at] = piece.astype(BF)

        @pl.when(mine)
        def _(at=at, piece=piece):
            own_ref[at] = piece

        col += cols
        if col == own_ref.shape[1]:
            row, col = row + rows, 0


def chip_sum(idx, pairs):
    in_specs, ins, total, width = [], [], 0, 0
    for blocks, got in pairs:
        _, _, rows, cols = blocks.shape
        width = max(width, cols)
        total += rows * cols
        ins += [blocks, got]
        in_specs += [
            pl.BlockSpec((1, 1, rows, cols), lambda i, idx: (i, idx[2], 0, 0)),
            pl.BlockSpec((1, rows, cols), lambda i, idx: (i, 0, 0)),
        ]
    rows = total // width
    return pl.pallas_call(
        chip_kernel,
        grid_spec=pltpu.PrefetchScalarGridSpec(
            num_scalar_prefetch=1,
            grid=(8,),
            in_specs=in_specs,
            out_specs=[
                pl.BlockSpec((1, rows, width), lambda i, idx: (i, 0, 0)),
                pl.BlockSpec((rows, width), lambda i, idx: (0, 0)),
            ],
        ),
        out_shape=[
            jax.ShapeDtypeStruct((8, rows, width), BF),
            jax.ShapeDtypeStruct((rows, width), F32),
        ],
        compiler_params=pltpu.CompilerParams(**PARAMS),
        name="chip_sum",
    )(idx, *ins)


def owner_kernel(idx, own_ref, got_ref, out_ref):
    mine = idx[0] * 2 + idx[1]
    total = own_ref[...]
    for i in range(8):
        total = total + jnp.where(mine == i, 0.0, got_ref[i].astype(F32))
    out_ref[...] = total


def owner_sum(idx, own, got):
    rows, width = own.shape
    tile = 16
    return pl.pallas_call(
        owner_kernel,
        grid_spec=pltpu.PrefetchScalarGridSpec(
            num_scalar_prefetch=1,
            grid=(rows // tile,),
            in_specs=[
                pl.BlockSpec((tile, width), lambda i, idx: (i, 0)),
                pl.BlockSpec((8, tile, width), lambda i, idx: (0, i, 0)),
            ],
            out_specs=pl.BlockSpec((tile, width), lambda i, idx: (i, 0)),
        ),
        out_shape=jax.ShapeDtypeStruct((rows, width), F32),
        name="owner_sum",
    )(idx, own, got)


def core_exchange(partial, core):
    rows, cols = partial.shape
    blocks = partial.reshape(8, 2, rows // 16, cols)
    sent = lax.dynamic_index_in_dim(blocks, 1 - core, 1, keepdims=False)
    return blocks, swapped(sent, "core", 2, 1)


def around(v, axis):
    size = lax.axis_size(axis)
    return jnp.stack([v] + [swapped(v, axis, size, offset) for offset in range(1, size)])


def assemble_kernel(idx, near_ref, far_ref, out_ref, *, order):
    sizes = {"z": 4, "x": 2, "seq": 2}
    here = {"z": idx[0], "x": idx[1], "core": idx[2], "seq": idx[3]}
    for a in range(near_ref.shape[0]):
        for b in range(near_ref.shape[1]):
            for c in range(near_ref.shape[2]):
                at = dict(
                    (axis, lax.rem(here[axis] - back + sizes[axis], sizes[axis]))
                    for axis, back in zip(order[::-1], (a, b, c))
                )
                for ref, core in ((near_ref, here["core"]), (far_ref, 1 - here["core"])):
                    block = ((at["z"] * 2 + at["x"]) * 2 + core) * 2 + at["seq"]
                    out_ref[block] = ref[a, b, c]


def assemble(idx, near, far, order):
    rows, cols = near.shape[-2:]
    out = pl.pallas_call(
        functools.partial(assemble_kernel, order=order),
        grid_spec=pltpu.PrefetchScalarGridSpec(
            num_scalar_prefetch=1,
            grid=(1,),
            in_specs=[pl.BlockSpec(near.shape, lambda i, idx: (0,) * 5)] * 2,
            out_specs=pl.BlockSpec((32, rows, cols), lambda i, idx: (0, 0, 0)),
        ),
        out_shape=jax.ShapeDtypeStruct((32, rows, cols), near.dtype),
        compiler_params=pltpu.CompilerParams(**PARAMS),
        name="assemble",
    )(idx, near, far)
    return out.reshape(32 * rows, cols)


def row8(v, width=None):
    v = v.reshape(1, -1)
    if width is not None:
        v = jnp.pad(v, ((0, 0), (0, width - v.shape[1])))
    return jnp.broadcast_to(v, (8, v.shape[1]))


def body(
    block_input,
    cotangent,
    in_weight,
    dt_weight,
    out_weight,
    norm_gain,
    conv_weight,
    conv_bias,
    dt_bias,
    decay_log,
    skip_gain,
    gate_gain,
    in_left,
    in_right,
    in_left_root,
    in_right_root,
    dt_left,
    dt_right,
    dt_left_root,
    dt_right_root,
    out_left,
    out_right,
    out_left_root,
    out_right_root,
    vector_moment,
):
    seq_count, local_len, _ = block_input.shape
    seq_devices = lax.axis_size("seq")
    row_count = seq_count * local_len
    up = [(i, i + 1) for i in range(seq_devices - 1)]
    down = [(i + 1, i) for i in range(seq_devices - 1)]

    in_low = in_weight.astype(BF)
    dt_low = jnp.pad(dt_weight.astype(BF), ((0, 0), (0, 128 - HEADS)))
    main = lax.all_gather(
        jnp.concatenate([in_low[:, DI:], dt_low], axis=1), AXES, axis=0, tiled=True
    )
    torus_sizes = tuple(lax.axis_size(a) for a in ("z", "x", "core", "seq"))
    direct = torus_sizes == (4, 2, 2, 2)
    idx = jnp.stack([lax.axis_index(a) for a in ("z", "x", "core", "seq")]).astype(jnp.int32)
    gate_low, out_low = in_low[:, :DI], out_weight.astype(BF)
    if direct:
        order = ("z", "x", "seq")
        gate_near = pick(gate_low.reshape(2, -1, DI), idx[3])
        out_near = pick(out_low.reshape(2, -1, D), idx[3])
        gate_near = around(around(gate_near, "z"), "x")
        out_near = around(around(out_near, "z"), "x")
        main, _, _ = lax.optimization_barrier((main, gate_near, out_near))
        gate_near = around(gate_near, "seq")
        out_near = around(out_near, "seq")
    else:
        wg = lax.all_gather(gate_low, AXES, axis=0, tiled=True)
        wo = lax.all_gather(out_low, AXES, axis=0, tiled=True)
    halo = lax.ppermute(block_input[:, local_len - 8 :, :], "seq", up)

    part = jnp.arange(128)
    channel = jnp.arange(DI)
    emat = (
        ((part[:, None] % 32) == (channel[None, :] // HEADDIM)) & (part[:, None] < 96)
    ).astype(BF)
    gmat = ((channel[:, None] // HEADDIM) == part[None, :]).astype(BF)
    skip_wide = row8(jnp.repeat(skip_gain, HEADDIM))
    alog = row8(decay_log, 128)
    dtb = row8(jnp.concatenate([dt_bias, jnp.full((128 - HEADS,), -1e4, F32)]))
    cw8 = jnp.pad(conv_weight, ((0, 4), (0, 0)))

    normed, mixed, pre, z, local_state, total = run_first(
        block_input, halo, row8(norm_gain), main, cw8, row8(conv_bias), dtb, alog, emat
    )
    span = jnp.repeat(jnp.exp(total[:, 0:1, :HEADS]), HEADDIM, axis=2)
    enter = lax.ppermute(local_state, "seq", up)
    for _ in range(seq_devices - 2):
        enter = lax.ppermute(local_state + span * enter, "seq", up)

    if direct:
        out_far = swapped(out_near, "core", 2, 1)
        gate_far = swapped(gate_near, "core", 2, 1)
        wo = assemble(idx, out_near, out_far, order)
        wg = assemble(idx, gate_near, gate_far, order)
    normed_rows = normed.reshape(row_count, D)
    upstream = cotangent.reshape(row_count, D)
    gate_part = dot(normed_rows, wg)
    branch_grad = dot(upstream, wo, NT)
    (
        block_output, branch, states_grad, gate_grad, states, rdot, local_dstate, row_sums,
    ) = run_second(
        pre, z, gate_part, branch_grad, block_input, enter, wo, skip_wide, row8(gate_gain), alog,
        emat, gmat,
    )
    leave = lax.ppermute(local_dstate, "seq", down)
    for _ in range(seq_devices - 2):
        leave = lax.ppermute(local_dstate + span * leave, "seq", down)

    out_partial = dot(branch, upstream, TN)
    gate_partial = dot(normed_rows, gate_grad, TN)
    if direct:
        early, early_own = chip_sum(
            idx, [core_exchange(gate_partial, idx[2]), core_exchange(out_partial, idx[2])]
        )
        states_grad, early = lax.optimization_barrier((states_grad, early))
        early = lax.all_to_all(early, ("z", "x"), split_axis=0, concat_axis=0, tiled=True)

    mgrad, last8, first8, column_sums = run_third(
        pre, mixed, z, states_grad, states, rdot, leave, cw8, skip_wide, alog, emat, gmat
    )
    near = lax.ppermute(first8, "seq", down)
    mgrad, extra = run_patch(mgrad, mixed, last8, near, cw8)
    conv_weight_grad = (column_sums + extra)[:KCONV]
    conv_bias_grad = column_sums[KCONV]

    mgrad_rows = mgrad.reshape(row_count, WIDE)
    mixed_local = dot(normed_rows, mgrad_rows, TN)
    normed_grad = (
        dot(gate_grad, wg, NT) + dot(mgrad_rows, main, NT)
    )
    incoming = block_input.reshape(row_count, D).astype(F32)
    _, norm_back = jax.vjp(norm_piece, incoming, norm_gain)
    input_part, norm_gain_grad = norm_back(normed_grad)
    input_grad = (input_part + upstream.astype(F32)).reshape(block_input.shape)

    vector_local = jnp.concatenate(
        [
            norm_gain_grad,
            row_sums[0],
            conv_weight_grad.reshape(-1),
            conv_bias_grad,
            column_sums[5, :HEADS],
            -jnp.exp(decay_log) * column_sums[6, :HEADS],
            row_sums[1].reshape(HEADS, HEADDIM).sum(1),
        ]
    )
    if direct:
        late, late_own = chip_sum(idx, [core_exchange(mixed_local, idx[2])])
        vector_local, early, late = lax.optimization_barrier((vector_local, early, late))
        late = lax.all_to_all(late, ("z", "x"), split_axis=0, concat_axis=0, tiled=True)
        early_own = owner_sum(idx, early_own, early)
        early_own = early_own + swapped(early_own, "seq", 2, 1)
        share = D // 16
        gate_sum = early_own[:share]
        out_grad = jnp.concatenate([early_own[share:, :D], early_own[share:, D:]], axis=0)
        late_own = owner_sum(idx, late_own, late)
        mixed_sum = late_own + swapped(late_own, "seq", 2, 1)
    else:
        gate_sum = reduce_plain(core_sum(gate_partial))
        out_grad = reduce_split(core_sum(out_partial))
        mixed_sum = reduce_plain(core_sum(mixed_local))
    vector_rows = jnp.pad(vector_local, (0, -vector_local.shape[0] % 1024)).reshape(-1, 128)
    for axis in ("core", "seq", "x", "z"):
        vector_rows = xor_sum(vector_rows, axis)
    vector_grad = vector_rows.reshape(-1)[: vector_local.shape[0]]

    in_grad = jnp.concatenate([gate_sum, mixed_sum[:, :CONVCH]], axis=1)
    dt_grad = mixed_sum[:, CONVCH : CONVCH + HEADS]

    in_update, in_left_new, in_right_new = kron_update(
        in_grad, in_left, in_right, in_left_root, in_right_root
    )
    dt_update, dt_left_wide, dt_right_wide = kron_update(
        dt_grad, dt_left[:, None], dt_right[:, None], dt_left_root[:, None], dt_right_root[:, None]
    )
    out_update, out_left_new, out_right_new = kron_update(
        out_grad, out_left, out_right, out_left_root, out_right_root
    )
    vector_moment_new = 0.5 * vector_moment + 0.5 * vector_grad * vector_grad
    vector_update = -LR_VEC * vector_grad * lax.rsqrt(vector_moment_new)
    return (
        block_output,
        input_grad,
        in_grad,
        dt_grad,
        out_grad,
        in_update,
        dt_update,
        out_update,
        in_left_new,
        in_right_new,
        dt_left_wide[:, 0],
        dt_right_wide[:, 0],
        out_left_new,
        out_right_new,
        vector_grad,
        vector_moment_new,
        vector_update,
    )


def solution(mesh):
    dp, seq = mesh.shape["dp"], mesh.shape["seq"]
    split = (4, dp // 8, 2)
    torus = jax.sharding.Mesh(mesh.devices.reshape(split + (seq,)), AXES + ("seq",))
    tokens = P(AXES, "seq", None)
    rows = P(AXES, None)
    tri = P(AXES, None, None)
    quad = P(AXES, None, None, None)
    placed = (
        (tokens, tokens, rows, rows, rows) + (P(),) * 7 + (quad,) * 4 + (tri,) * 4 + (quad,) * 4 + (P(),)
    )

    return jax.shard_map(
        body,
        mesh=torus,
        in_specs=placed,
        out_specs=(tokens, tokens)
        + (rows,) * 6
        + (quad, quad, tri, tri, quad, quad)
        + (P(), P(), P()),
        check_vma=False,
    )
```

```python
import functools

import jax
import jax.numpy as jnp
from jax import lax
from jax.experimental import pallas as pl
from jax.experimental.pallas import tpu as pltpu
from jax.sharding import PartitionSpec as P


D = 768
HEADS = 24
HEADDIM = 64
DSTATE = 128
KCONV = 4
DI = 1536
CONVCH = 1792
WIDE = CONVCH + 128

BL = 128
PAIRS = HEADS // 2

AXES = ("z", "x", "core")

EPS = 1e-05
LR = 0.25
LR_VEC = 0.02
NEG = -1e30
BF = jnp.bfloat16
F32 = jnp.float32
NN = (((1,), (0,)), ((), ()))
NT = (((1,), (1,)), ((), ()))
TN = (((0,), (0,)), ((), ()))


def dot(a, b, dims=NN):
    return lax.dot_general(a, b, dims, preferred_element_type=F32)


def split2(v):
    high = v.astype(BF)
    return high, (v - high.astype(F32)).astype(BF)


def dot3(a, b, dims=NN):
    ah, al = split2(a)
    bh, bl = split2(b)
    return dot(ah, bh, dims) + dot(al, bh, dims) + dot(ah, bl, dims)


def pack(v):
    high = v.astype(BF).astype(F32)
    rest = v - high
    mid = rest.astype(BF).astype(F32)
    low = rest - mid
    return (high + pltpu.roll(mid, 32, 1) + pltpu.roll(low, 64, 1)).astype(BF)


def head_lanes(shape):
    return lax.broadcasted_iota(jnp.int32, shape, 1) < HEADS


def prefix(tri, v):
    parts = dot(tri, pack(v))
    total = parts + pltpu.roll(parts, 96, 1) + pltpu.roll(parts, 64, 1)
    return jnp.where(head_lanes(total.shape), total, 0.0)


def expand(v, emat):
    return dot(pack(v), emat)


def head_sum(v, gather):
    high, low = split2(v)
    return dot(high, gather) + dot(low, gather)


def tri_mask(lower):
    rows = lax.broadcasted_iota(jnp.int32, (BL, BL), 0)
    cols = lax.broadcasted_iota(jnp.int32, (BL, BL), 1)
    return (rows >= cols) if lower else (cols >= rows)


def softplus(v):
    return jnp.maximum(v, 0.0) + jnp.log1p(jnp.exp(-jnp.abs(v)))


def sigmoid(v):
    return 1.0 / (1.0 + jnp.exp(-v))


def rates(alog_ref):
    rate = -jnp.exp(alog_ref[0:1, :])
    return jnp.where(head_lanes(rate.shape), rate, 0.0)


def pair_blocks(v):
    left = lax.broadcasted_iota(jnp.int32, v.shape, 1) < HEADDIM
    return jnp.concatenate([jnp.where(left, v, 0.0), jnp.where(left, 0.0, v)], axis=0).astype(BF)


def norm_rows(u, gain):
    inv = lax.rsqrt(jnp.mean(u * u, axis=-1, keepdims=True) + EPS)
    return u * inv * gain


def first_kernel(
    u_ref, halo_ref, gain_ref, w_ref, cw_ref, cb_ref, dtb_ref, alog_ref, emat_ref,
    normed_ref, mixed_ref, pre_ref, z_ref, state_ref, total_ref,
    tail, full,
):
    step_index = pl.program_id(1)
    tile = u_ref.shape[1]
    gain = gain_ref[0:1, :]

    @pl.when(step_index == 0)
    def _():
        near = norm_rows(halo_ref[0].astype(F32), gain).astype(BF)
        tail[...] = dot(near, w_ref[:, :CONVCH]).astype(BF).astype(F32)
        state_ref[...] = jnp.zeros_like(state_ref)
        total_ref[...] = jnp.zeros_like(total_ref)

    normed = norm_rows(u_ref[0].astype(F32), gain).astype(BF)
    normed_ref[0] = normed
    projected = dot(normed, w_ref[...])
    mixed_low = projected[:, :CONVCH].astype(BF)
    mixed_ref[0] = mixed_low
    mixed = mixed_low.astype(F32)
    z = projected[:, CONVCH:].astype(BF).astype(F32) + dtb_ref[0:1, :]
    z_ref[0] = z
    for low in range(0, CONVCH, 256):
        cols = slice(low, low + 256)
        own = mixed[:, cols]
        joined = jnp.concatenate([tail[:, cols], own], axis=0)
        pre = cb_ref[0:1, cols] + cw_ref[KCONV - 1 : KCONV, cols] * own
        for tap in range(KCONV - 1):
            moved = pltpu.roll(joined, KCONV - 1 - tap, 0)[8:, :]
            pre = pre + cw_ref[tap : tap + 1, cols] * moved
        pre_ref[0, :, cols] = pre
        full[:, cols] = pre * sigmoid(pre)
    tail[...] = mixed[tile - 8 :, :]
    step_all = softplus(z)
    rate = rates(alog_ref)
    tri = jnp.where(tri_mask(True), 1.0, 0.0).astype(BF)
    emat = emat_ref[...]
    for part in range(tile // BL):
        rows = slice(part * BL, (part + 1) * BL)
        step = step_all[rows]
        cum = prefix(tri, step * rate)
        last = cum[BL - 1 : BL, :]
        weights = expand(jnp.exp(last - cum) * step, emat)
        decay = expand(
            jnp.where(head_lanes((8, 128)), jnp.broadcast_to(jnp.exp(last), (8, 128)), 0.0), emat
        )[0:1, :]
        inputs_b = full[rows, DI : DI + DSTATE]
        fresh = dot3(inputs_b.T, weights * full[rows, :DI])
        state_ref[0] = state_ref[0] * decay + fresh
        total_ref[0] = total_ref[0] + jnp.broadcast_to(last, (8, 128))


def dot_wide(ahl, ah, bh, bl):
    return dot(ahl, jnp.concatenate([bh, bh], axis=0)) + dot(ah, bl)


def dot3_split(a, b, dims):
    (ah, al), (bh, bl) = a, b
    return dot(ah, bh, dims) + dot(al, bh, dims) + dot(ah, bl, dims)


def wide_split(v):
    high, low = split2(v)
    return jnp.concatenate([high, low], axis=1), high


def rows8(v):
    return jnp.sum(v.reshape(v.shape[0] // 8, 8, v.shape[1]), axis=0)


def pair_values(pair, cum, cum_t, step, mask, left, transposed):
    kernels, columns = [], []
    for h in (2 * pair, 2 * pair + 1):
        column = jnp.broadcast_to(cum[:, h : h + 1], (BL, BL))
        row = cum_t[h : h + 1, :]
        spread = (row - column) if transposed else (column - row)
        kernels.append(jnp.exp(jnp.where(mask, spread, NEG)))
        columns.append(column)
    chosen = jnp.where(left, columns[0], columns[1])
    steps = jnp.where(left, step[:, 2 * pair : 2 * pair + 1], step[:, 2 * pair + 1 : 2 * pair + 2])
    return kernels, chosen, steps


def lane_sum(v):
    return jnp.sum(v, axis=1, keepdims=True)


def second_kernel(
    pre_ref, z_ref, gate_ref, bgrad_ref, u_ref, enter_ref, wo_ref, skip_ref, ggain_ref, alog_ref,
    gmat_ref,
    out_ref, branch_ref, dy_ref, ggrad_ref, state_ref, rdot_ref, dstate_ref, sums_ref,
    gain_acc, skip_acc, state, running, ys, es,
):
    step_index = pl.program_id(1)
    tile = pre_ref.shape[1]

    @pl.when(step_index == 0)
    def _():
        state[...] = enter_ref[0]
        running[...] = jnp.ones_like(running)
        dstate_ref[...] = jnp.zeros_like(dstate_ref)

    @pl.when((step_index == 0) & (pl.program_id(0) == 0))
    def _():
        gain_acc[...] = jnp.zeros_like(gain_acc)
        skip_acc[...] = jnp.zeros_like(skip_acc)

    rate = rates(alog_ref)

    def block(part, carry):
        rows = pl.ds(pl.multiple_of(part * BL, BL), BL)
        mask = tri_mask(True)
        left = lax.broadcasted_iota(jnp.int32, (BL, BL), 1) < HEADDIM
        tri = jnp.where(mask, 1.0, 0.0).astype(BF)
        pre = pre_ref[0, rows, DI:]
        conv = pre * sigmoid(pre)
        inputs_b, inputs_c = conv[:, :DSTATE], conv[:, DSTATE:]
        step = softplus(z_ref[0, rows, :])
        cum = prefix(tri, step * rate)
        cum_t = cum.T
        scores = dot3(inputs_c, inputs_b, NT)
        c_wide, c_high = wide_split(inputs_c)
        bt_wide, bt_high = wide_split(inputs_b.T)
        ct_wide, ct_high = wide_split(inputs_c.T)
        squares = jnp.zeros((BL, 128), F32)
        products = jnp.zeros((BL, 128), F32)
        for quad in range(PAIRS // 2):
            cols = slice(quad * 256, (quad + 1) * 256)
            inner, grown, weighted, xs = [], [], [], []
            for pair in (2 * quad, 2 * quad + 1):
                kernels, chosen, steps = pair_values(pair, cum, cum_t, step, mask, left, False)
                own = pre_ref[0, rows, pair * 128 : (pair + 1) * 128]
                x = own * sigmoid(own)
                scaled = steps * x
                mh, ml = split2(jnp.concatenate([scores * k for k in kernels], axis=1))
                high = scaled.astype(BF).astype(F32)
                rh, rl = pair_blocks(high), pair_blocks(scaled - high)
                inner.append(dot(mh, rh) + dot(ml, rh) + dot(mh, rl))
                grown.append(jnp.exp(chosen))
                weighted.append(jnp.exp(chosen[BL - 1 : BL, :] - chosen) * scaled)
                xs.append(x)
            inner, grown, weighted, x = (
                jnp.concatenate(v, axis=1) for v in (inner, grown, weighted, xs)
            )
            held = state[:, cols]
            state_ref[0, part, :, cols] = held
            yhat = inner + grown * dot_wide(c_wide, c_high, *split2(held))
            state[:, cols] = held * grown[BL - 1 : BL, :] + dot_wide(
                bt_wide, bt_high, *split2(weighted)
            )
            ys[:, cols] = yhat
            es[:, cols] = grown
            states = (yhat + skip_ref[0:1, cols] * x).astype(BF).astype(F32)
            gate = gate_ref[rows, cols]
            gated = states * (gate * sigmoid(gate))
            product = gated * (bgrad_ref[rows, cols] * ggain_ref[0:1, cols])
            squared = gated * gated
            squares = squares + squared[:, :128] + squared[:, 128:]
            products = products + product[:, :128] + product[:, 128:]
        inv = lax.rsqrt(lane_sum(squares) * (1.0 / DI) + EPS)
        pull = jnp.broadcast_to(inv * inv * lane_sum(products) * (1.0 / DI), (BL, 128))
        inv = jnp.broadcast_to(inv, (BL, 128))
        rdot = jnp.zeros((BL, 128), F32)
        for quad in range(PAIRS // 2):
            cols = slice(quad * 256, (quad + 1) * 256)
            scaled_dy, dot_terms = [], []
            for pair in (2 * quad, 2 * quad + 1):
                own_cols = slice(pair * 128, (pair + 1) * 128)
                own = pre_ref[0, rows, own_cols]
                x = own * sigmoid(own)
                yhat = ys[:, own_cols]
                states = (yhat + skip_ref[0:1, own_cols] * x).astype(BF).astype(F32)
                gate = gate_ref[rows, own_cols]
                sg = sigmoid(gate)
                sl = gate * sg
                gated = states * sl
                gain = ggain_ref[0:1, own_cols]
                upstream = bgrad_ref[rows, own_cols]
                norm = gated * inv
                branch_ref[rows, own_cols] = (norm * gain).astype(BF)
                gain_acc[:, own_cols] += rows8(upstream * norm)
                dgated = inv * (upstream * gain - gated * pull)
                dy_low = (dgated * sl).astype(BF)
                dy_ref[rows, own_cols] = dy_low
                ggrad_ref[rows, own_cols] = (dgated * states * (sg + sl * (1.0 - sg))).astype(BF)
                dy = dy_low.astype(F32)
                skip_acc[:, own_cols] += rows8(dy * x)
                dot_terms.append(dy * yhat)
                scaled_dy.append(es[:, own_cols] * running[0:1, own_cols] * dy)
            rdot = rdot + head_sum(jnp.concatenate(dot_terms, axis=1), gmat_ref[cols, :])
            dstate_ref[0, :, cols] += dot_wide(
                ct_wide, ct_high, *split2(jnp.concatenate(scaled_dy, axis=1))
            )
            running[:, cols] = running[:, cols] * es[BL - 1 : BL, cols]
        rdot_ref[0, rows, :] = rdot
        return carry

    lax.fori_loop(0, tile // BL, block, 0)
    out_ref[0] = (u_ref[0].astype(F32) + dot(branch_ref[...], wo_ref[...])).astype(BF)

    @pl.when((step_index == pl.num_programs(1) - 1) & (pl.program_id(0) == pl.num_programs(0) - 1))
    def _():
        sums_ref[0:1, :] = jnp.sum(gain_acc[...], axis=0, keepdims=True)
        sums_ref[1:2, :] = jnp.sum(skip_acc[...], axis=0, keepdims=True)


def third_kernel(
    pre_ref, mixed_ref, z_ref, dy_ref, state_ref, rdot_ref, leave_ref, cw_ref, skip_ref, alog_ref,
    gmat_ref,
    mgrad_ref, last_ref, first_ref, sums_ref,
    cw_acc, cb_acc, dtb_acc, rate_acc, dstate, tail,
):
    step_index = pl.program_id(1)

    @pl.when(step_index == 0)
    def _():
        dstate[...] = leave_ref[0]
        tail[...] = jnp.zeros_like(tail)

    @pl.when((step_index == 0) & (pl.program_id(0) == 0))
    def _():
        for ref in (cw_acc, cb_acc, dtb_acc, rate_acc):
            ref[...] = jnp.zeros_like(ref)

    rate = rates(alog_ref)
    mask = tri_mask(False)
    left = lax.broadcasted_iota(jnp.int32, (BL, BL), 1) < HEADDIM
    low_tri = jnp.where(tri_mask(True), 1.0, 0.0).astype(BF)
    high_tri = jnp.where(mask, 1.0, 0.0).astype(BF)
    wide_pre = pre_ref[0, :, DI:]
    wide_sg = sigmoid(wide_pre)
    conv = wide_pre * wide_sg
    inputs_b, inputs_c = conv[:, :DSTATE], conv[:, DSTATE:]
    z = z_ref[0]
    step = softplus(z)
    cum = prefix(low_tri, step * rate)
    cum_t = cum.T
    lanes = head_lanes(cum.shape)
    scores_t = dot3(inputs_b, inputs_c, NT)
    b_wide, b_high = wide_split(inputs_b)
    ct_wide, ct_high = wide_split(inputs_c.T)
    dscores_t = jnp.zeros((BL, BL), F32)
    db = jnp.zeros((BL, DSTATE), F32)
    dc = jnp.zeros((BL, DSTATE), F32)
    sums = jnp.zeros((BL + 8, 128), F32)

    def back_conv(cols, dpre):
        joined = jnp.concatenate([dpre, tail[:, cols]], axis=0)
        tail[:, cols] = dpre[0:8, :]
        mixed = mixed_ref[0, :, cols].astype(F32)
        cb_acc[:, cols] += rows8(dpre)
        mgrad = cw_ref[KCONV - 1 : KCONV, cols] * dpre
        cw_acc[KCONV - 1, :, cols] += rows8(dpre * mixed)
        for tap in range(KCONV - 1):
            moved = pltpu.roll(joined, BL + 8 - (KCONV - 1 - tap), 0)[:BL, :]
            mgrad = mgrad + cw_ref[tap : tap + 1, cols] * moved
            cw_acc[tap, :, cols] += rows8(moved * mixed)
        mgrad_ref[0, :, cols] = mgrad.astype(BF)
        last_ref[0, :, cols] = jnp.where(step_index == 0, mgrad[BL - 8 :, :], last_ref[0, :, cols])

    for quad in range(PAIRS // 2):
        cols = slice(quad * 256, (quad + 1) * 256)
        inner, grown, shrink, scaled, xs, steps_wide, slopes = [], [], [], [], [], [], []
        dy = dy_ref[:, cols].astype(F32)
        for half, pair in enumerate((2 * quad, 2 * quad + 1)):
            kernels, chosen, steps = pair_values(pair, cum, cum_t, step, mask, left, True)
            own = pre_ref[0, :, pair * 128 : (pair + 1) * 128]
            sg = sigmoid(own)
            x = own * sg
            slopes.append(sg + x * (1.0 - sg))
            xd = steps * x
            mh, ml = split2(jnp.concatenate([scores_t * k for k in kernels], axis=1))
            dyb = pair_blocks(dy[:, half * 128 : (half + 1) * 128])
            inner.append(dot(mh, dyb) + dot(ml, dyb))
            sh, sl = split2(xd)
            dmix = dot(sh, dyb, NT) + dot(sl, dyb, NT)
            dscores_t = dscores_t + dmix[:, :BL] * kernels[0] + dmix[:, BL:] * kernels[1]
            grown.append(jnp.exp(chosen))
            shrink.append(jnp.exp(chosen[BL - 1 : BL, :] - chosen))
            scaled.append(xd)
            xs.append(x)
            steps_wide.append(steps)
        inner, grown, shrink, scaled, x, steps_wide, slopes = (
            jnp.concatenate(v, axis=1) for v in (inner, grown, shrink, scaled, xs, steps_wide, slopes)
        )
        held = state_ref[0, 0, :, cols]
        ds = dstate[:, cols]
        held_parts, ds_parts = split2(held), split2(ds)
        decay = grown[BL - 1 : BL, :]
        dscaled_state = shrink * dot_wide(b_wide, b_high, *ds_parts)
        dscaled = inner + dscaled_state
        ends = jnp.sum(scaled * dscaled_state, axis=0, keepdims=True) + decay * jnp.sum(
            held * ds, axis=0, keepdims=True
        )
        sums = sums + head_sum(
            jnp.concatenate([x * dscaled, jnp.broadcast_to(ends, (8, 256))], axis=0),
            gmat_ref[cols, :],
        )
        grown_parts = split2(grown * dy)
        dc = dc + dot3_split(grown_parts, held_parts, NT)
        db = db + dot3_split(split2(shrink * scaled), ds_parts, NT)
        dstate[:, cols] = decay * ds + dot_wide(ct_wide, ct_high, *grown_parts)
        back_conv(cols, (steps_wide * dscaled + skip_ref[0:1, cols] * dy) * slopes)

    direct = sums[:BL]
    is_last = lax.broadcasted_iota(jnp.int32, (BL, 128), 0) == BL - 1
    dcum = rdot_ref[0] - step * direct + jnp.where(is_last, sums[BL : BL + 1, :], 0.0)
    dcum = jnp.where(lanes, dcum, 0.0)
    drate = prefix(high_tri, dcum)
    dz = (rate * drate + direct) * sigmoid(z)
    mgrad_ref[0, :, CONVCH:] = dz.astype(BF)
    dtb_acc[...] += rows8(dz)
    rate_acc[...] += rows8(step * drate)
    db = db + dot3(dscores_t, inputs_c)
    dc = dc + dot3(dscores_t.T, inputs_b)
    back_conv(
        slice(DI, CONVCH),
        jnp.concatenate([db, dc], axis=1) * (wide_sg + conv * (1.0 - wide_sg)),
    )
    first_ref[0] = tail[...]

    @pl.when((step_index == pl.num_programs(1) - 1) & (pl.program_id(0) == pl.num_programs(0) - 1))
    def _():
        for tap in range(KCONV):
            sums_ref[tap : tap + 1, :] = jnp.sum(cw_acc[tap], axis=0, keepdims=True)
        sums_ref[4:5, :] = jnp.sum(cb_acc[...], axis=0, keepdims=True)
        sums_ref[5:6, :128] = jnp.sum(dtb_acc[...], axis=0, keepdims=True)
        sums_ref[6:7, :128] = jnp.sum(rate_acc[...], axis=0, keepdims=True)


def patch_kernel(mgrad_ref, mixed_ref, last_ref, near_ref, cw_ref, out_ref, extra_ref):
    @pl.when(pl.program_id(0) == 0)
    def _():
        extra_ref[...] = jnp.zeros_like(extra_ref)

    rows = [last_ref[0, i : i + 1, :] for i in range(8)]
    near = [near_ref[0, i : i + 1, :] for i in range(KCONV - 1)]
    held = mixed_ref[0].astype(F32)
    first = 8 - (KCONV - 1)
    for k in range(KCONV - 1):
        for j in range(k, KCONV - 1):
            rows[first + j] = rows[first + j] + cw_ref[k : k + 1, :] * near[j - k]
            extra_ref[k : k + 1, :] += near[j - k] * held[8 + first + j : 9 + first + j, :]
    old = mgrad_ref[0].astype(F32)
    patched = jnp.concatenate([old[:8, :CONVCH], jnp.concatenate(rows, axis=0)], axis=0)
    out_ref[0, :, :CONVCH] = patched.astype(BF)
    out_ref[0, :, CONVCH:] = mgrad_ref[0, :, CONVCH:]


PARAMS = dict(vmem_limit_bytes=60 * 1024 * 1024)


def whole(shape):
    zeros = (0,) * len(shape)
    return pl.BlockSpec(shape, lambda b, i: zeros)


def run_first(u, halo, gain, w, cw, cb, dtb, alog, emat):
    seqs, length, _ = u.shape
    tile = min(256, length)
    grid = (seqs, length // tile)
    tok = lambda width: pl.BlockSpec((1, tile, width), lambda b, i: (b, i, 0))
    per = lambda *shape: pl.BlockSpec((1,) + shape, lambda b, i: (b,) + (0,) * len(shape))
    return pl.pallas_call(
        first_kernel,
        grid=grid,
        in_specs=[
            tok(D), per(8, D), whole(gain.shape), whole(w.shape),
            whole(cw.shape), whole(cb.shape), whole(dtb.shape), whole(alog.shape), whole(emat.shape),
        ],
        out_specs=[
            tok(D), tok(CONVCH), tok(CONVCH), tok(128), per(DSTATE, DI), per(8, 128),
        ],
        out_shape=[
            jax.ShapeDtypeStruct((seqs, length, D), BF),
            jax.ShapeDtypeStruct((seqs, length, CONVCH), BF),
            jax.ShapeDtypeStruct((seqs, length, CONVCH), F32),
            jax.ShapeDtypeStruct((seqs, length, 128), F32),
            jax.ShapeDtypeStruct((seqs, DSTATE, DI), F32),
            jax.ShapeDtypeStruct((seqs, 8, 128), F32),
        ],
        scratch_shapes=[pltpu.VMEM((8, CONVCH), F32), pltpu.VMEM((tile, CONVCH), F32)],
        compiler_params=pltpu.CompilerParams(**PARAMS),
        name="first",
    )(u, halo, gain, w, cw, cb, dtb, alog, emat)


def run_second(pre, z, gate, bgrad, u, enter, wo, skip, ggain, alog, gmat):
    seqs, length, _ = u.shape
    tile = min(256, length)
    steps = length // tile
    parts = tile // BL
    grid = (seqs, steps)
    tok = lambda width: pl.BlockSpec((1, tile, width), lambda b, i: (b, i, 0))
    flat = lambda width: pl.BlockSpec((tile, width), lambda b, i: (b * steps + i, 0))
    per = lambda *shape: pl.BlockSpec((1,) + shape, lambda b, i: (b,) + (0,) * len(shape))
    rows = seqs * length
    return pl.pallas_call(
        second_kernel,
        grid=grid,
        in_specs=[
            tok(CONVCH), tok(128), flat(DI), flat(DI), tok(D), per(DSTATE, DI), whole(wo.shape),
            whole(skip.shape), whole(ggain.shape), whole(alog.shape), whole(gmat.shape),
        ],
        out_specs=[
            tok(D), flat(DI), flat(DI), flat(DI),
            pl.BlockSpec((1, parts, DSTATE, DI), lambda b, i: (b, i, 0, 0)),
            tok(128), per(DSTATE, DI), whole((8, DI)),
        ],
        out_shape=[
            jax.ShapeDtypeStruct((seqs, length, D), BF),
            jax.ShapeDtypeStruct((rows, DI), BF),
            jax.ShapeDtypeStruct((rows, DI), BF),
            jax.ShapeDtypeStruct((rows, DI), BF),
            jax.ShapeDtypeStruct((seqs, length // BL, DSTATE, DI), F32),
            jax.ShapeDtypeStruct((seqs, length, 128), F32),
            jax.ShapeDtypeStruct((seqs, DSTATE, DI), F32),
            jax.ShapeDtypeStruct((8, DI), F32),
        ],
        scratch_shapes=[
            pltpu.VMEM((8, DI), F32), pltpu.VMEM((8, DI), F32), pltpu.VMEM((DSTATE, DI), F32),
            pltpu.VMEM((8, DI), F32), pltpu.VMEM((BL, DI), F32), pltpu.VMEM((BL, DI), F32),
        ],
        compiler_params=pltpu.CompilerParams(**PARAMS),
        name="second",
    )(pre, z, gate, bgrad, u, enter, wo, skip, ggain, alog, gmat)


def run_third(pre, mixed, z, dy, states, rdot, leave, cw, skip, alog, gmat):
    seqs, length, _ = pre.shape
    steps = length // BL
    grid = (seqs, steps)
    tok = lambda width: pl.BlockSpec((1, BL, width), lambda b, i: (b, steps - 1 - i, 0))
    per = lambda *shape: pl.BlockSpec((1,) + shape, lambda b, i: (b,) + (0,) * len(shape))
    return pl.pallas_call(
        third_kernel,
        grid=grid,
        in_specs=[
            tok(CONVCH), tok(CONVCH), tok(128),
            pl.BlockSpec((BL, DI), lambda b, i: (b * steps + steps - 1 - i, 0)),
            pl.BlockSpec((1, 1, DSTATE, DI), lambda b, i: (b, steps - 1 - i, 0, 0)),
            tok(128), per(DSTATE, DI), whole(cw.shape), whole(skip.shape), whole(alog.shape),
            whole(gmat.shape),
        ],
        out_specs=[
            tok(WIDE), per(8, CONVCH), per(8, CONVCH), whole((8, CONVCH)),
        ],
        out_shape=[
            jax.ShapeDtypeStruct((seqs, length, WIDE), BF),
            jax.ShapeDtypeStruct((seqs, 8, CONVCH), F32),
            jax.ShapeDtypeStruct((seqs, 8, CONVCH), F32),
            jax.ShapeDtypeStruct((8, CONVCH), F32),
        ],
        scratch_shapes=[
            pltpu.VMEM((KCONV, 8, CONVCH), F32), pltpu.VMEM((8, CONVCH), F32),
            pltpu.VMEM((8, 128), F32), pltpu.VMEM((8, 128), F32),
            pltpu.VMEM((DSTATE, DI), F32), pltpu.VMEM((8, CONVCH), F32),
        ],
        compiler_params=pltpu.CompilerParams(**PARAMS),
        name="third",
    )(pre, mixed, z, dy, states, rdot, leave, cw, skip, alog, gmat)


def run_patch(mgrad, mixed, last8, near, cw):
    seqs, length, _ = mgrad.shape
    end = length // 16 - 1
    tok = lambda width: pl.BlockSpec((1, 16, width), lambda b: (b, end, 0))
    per = pl.BlockSpec((1, 8, CONVCH), lambda b: (b, 0, 0))
    row = pl.BlockSpec((8, CONVCH), lambda b: (0, 0))
    return pl.pallas_call(
        patch_kernel,
        grid=(seqs,),
        in_specs=[tok(WIDE), tok(CONVCH), per, per, row],
        out_specs=[tok(WIDE), row],
        out_shape=[
            jax.ShapeDtypeStruct(mgrad.shape, BF),
            jax.ShapeDtypeStruct((8, CONVCH), F32),
        ],
        input_output_aliases={0: 0},
        name="patch",
    )(mgrad, mixed, last8, near, cw)


def norm_piece(incoming, norm_gain):
    inv_rms = lax.rsqrt(jnp.mean(incoming * incoming, axis=-1, keepdims=True) + EPS)
    return incoming * inv_rms * norm_gain


def kron_update(gradient, left_stat, right_stat, left_root, right_root):
    row_tiles, col_tiles = (left_stat.shape[0], left_stat.shape[1])
    row_size, col_size = (left_stat.shape[-1], right_stat.shape[-1])
    grad_tiles = gradient.reshape(row_tiles, row_size, col_tiles, col_size).transpose(0, 2, 1, 3)
    left_new = 0.5 * left_stat + 0.5 * jnp.einsum(
        "abij,abkj->abik", grad_tiles, grad_tiles, precision=lax.Precision.HIGH
    )
    right_new = 0.5 * right_stat + 0.5 * jnp.einsum(
        "abji,abjk->abik", grad_tiles, grad_tiles, precision=lax.Precision.HIGH
    )
    shaped = jnp.einsum("abij,abjk->abik", left_root, grad_tiles, precision=lax.Precision.HIGH)
    shaped = jnp.einsum("abij,abjk->abik", shaped, right_root, precision=lax.Precision.HIGH)
    update = (-LR * shaped).transpose(0, 2, 1, 3).reshape(gradient.shape)
    return (update, left_new, right_new)


def swapped(v, axis, size, offset):
    return lax.ppermute(v, axis, [(i, (i + offset) % size) for i in range(size)])


def pick(v, index):
    return lax.dynamic_index_in_dim(v, index, 0, keepdims=False)


def scatter_stage(v, axis, kind=BF):
    size = lax.axis_size(axis)
    here = lax.axis_index(axis)
    total = pick(v, here)
    for offset in range(1, size):
        sent = pick(v, lax.rem(here + offset, size)).astype(kind)
        total = total + swapped(sent, axis, size, offset).astype(F32)
    return total


def gather_stage(v, axis):
    size = lax.axis_size(axis)
    here = lax.axis_index(axis)
    out = jnp.zeros((size,) + v.shape, v.dtype)
    out = lax.dynamic_update_index_in_dim(out, v, here, 0)
    for offset in range(1, size):
        got = swapped(v, axis, size, offset)
        out = lax.dynamic_update_index_in_dim(out, got, lax.rem(here - offset + size, size), 0)
    return out


def core_sum(partial):
    z, x, core = (lax.axis_size(a) for a in ("z", "x", "core"))
    rows, cols = partial.shape
    blocks = partial.reshape(z, x, core, rows // (z * x * core), cols)
    return scatter_stage(jnp.moveaxis(blocks, 2, 0), "core", F32)


def across(v):
    return scatter_stage(scatter_stage(jnp.moveaxis(v, 1, 0), "x"), "z")


def reduce_plain(v):
    owned = across(v)
    total = owned
    size = lax.axis_size("seq")
    if size > 2:
        return lax.psum(owned, "seq")
    for offset in range(1, size):
        total = total + swapped(owned, "seq", size, offset)
    return total


def reduce_split(v):
    size = lax.axis_size("seq")
    z, x, rows, cols = v.shape
    if cols % (128 * size):
        return reduce_plain(v)
    v = jnp.moveaxis(v.reshape(z, x, rows, size, cols // size), 3, 0)
    owned = across(scatter_stage(v, "seq"))
    return jnp.moveaxis(gather_stage(owned, "seq"), 0, 1).reshape(rows, cols)


def xor_sum(v, axis):
    size = lax.axis_size(axis)
    bit = 1
    while bit < size:
        v = v + lax.ppermute(v, axis, [(i, i ^ bit) for i in range(size)])
        bit *= 2
    return v


STEP_OWNERS = 4


def chip_kernel(idx, *refs):
    send_ref, own_ref = refs[-2:]
    width = own_ref.shape[1]
    for owner in range(STEP_OWNERS):
        mine = pl.program_id(0) * STEP_OWNERS + owner == idx[0] * 2 + idx[1]
        row, col = 0, 0
        for part_ref, got_ref in zip(refs[:-2:2], refs[1:-2:2]):
            total = part_ref[owner, 0] + got_ref[owner]
            rows = total.shape[0] * total.shape[1] // width
            for low in range(0, total.shape[0], rows):
                piece = total[low : low + rows]
                at = (slice(row, row + rows), slice(col, col + piece.shape[1]))
                send_ref[(owner,) + at] = piece.astype(BF)

                @pl.when(mine)
                def _(at=at, piece=piece):
                    own_ref[at] = piece

                col += piece.shape[1]
                if col == width:
                    row, col = row + rows, 0


def chip_sum(idx, pairs):
    in_specs, ins, total, width = [], [], 0, 0
    for blocks, got in pairs:
        _, _, rows, cols = blocks.shape
        width = max(width, cols)
        total += rows * cols
        ins += [blocks, got]
        in_specs += [
            pl.BlockSpec((STEP_OWNERS, 1, rows, cols), lambda i, idx: (i, idx[2], 0, 0)),
            pl.BlockSpec((STEP_OWNERS, rows, cols), lambda i, idx: (i, 0, 0)),
        ]
    rows = total // width
    return pl.pallas_call(
        chip_kernel,
        grid_spec=pltpu.PrefetchScalarGridSpec(
            num_scalar_prefetch=1,
            grid=(8 // STEP_OWNERS,),
            in_specs=in_specs,
            out_specs=[
                pl.BlockSpec((STEP_OWNERS, rows, width), lambda i, idx: (i, 0, 0)),
                pl.BlockSpec((rows, width), lambda i, idx: (0, 0)),
            ],
        ),
        out_shape=[
            jax.ShapeDtypeStruct((8, rows, width), BF),
            jax.ShapeDtypeStruct((rows, width), F32),
        ],
        compiler_params=pltpu.CompilerParams(**PARAMS),
        name="chip_sum",
    )(idx, *ins)


def owner_kernel(idx, own_ref, got_ref, out_ref):
    mine = idx[0] * 2 + idx[1]
    total = own_ref[...]
    for i in range(8):
        total = total + jnp.where(mine == i, 0.0, got_ref[i].astype(F32))
    out_ref[...] = total


def owner_sum(idx, own, got):
    rows, width = own.shape
    tile = 48
    return pl.pallas_call(
        owner_kernel,
        grid_spec=pltpu.PrefetchScalarGridSpec(
            num_scalar_prefetch=1,
            grid=(rows // tile,),
            in_specs=[
                pl.BlockSpec((tile, width), lambda i, idx: (i, 0)),
                pl.BlockSpec((8, tile, width), lambda i, idx: (0, i, 0)),
            ],
            out_specs=pl.BlockSpec((tile, width), lambda i, idx: (i, 0)),
        ),
        out_shape=jax.ShapeDtypeStruct((rows, width), F32),
        name="owner_sum",
    )(idx, own, got)


def core_exchange(partial, core):
    rows, cols = partial.shape
    blocks = partial.reshape(8, 2, rows // 16, cols)
    sent = lax.dynamic_index_in_dim(blocks, 1 - core, 1, keepdims=False)
    return blocks, swapped(sent, "core", 2, 1)


def around(v, axis):
    size = lax.axis_size(axis)
    return jnp.stack([v] + [swapped(v, axis, size, offset) for offset in range(1, size)])


def assemble_kernel(idx, *refs, order):
    out_ref = refs[-1]
    sizes = {"z": 4, "x": 2}
    here = {"z": idx[0], "x": idx[1]}
    spots = ((idx[2], idx[3]), (idx[2], 1 - idx[3]), (1 - idx[2], idx[3]), (1 - idx[2], 1 - idx[3]))
    for ref, (core, seq) in zip(refs[:-1], spots):
        for a in range(ref.shape[0]):
            for b in range(ref.shape[1]):
                at = dict(
                    (axis, lax.rem(here[axis] - back + sizes[axis], sizes[axis]))
                    for axis, back in zip(order[::-1], (a, b))
                )
                out_ref[((at["z"] * 2 + at["x"]) * 2 + core) * 2 + seq] = ref[a, b]


def assemble(idx, pieces, order):
    shape = pieces[0].shape
    rows, cols = shape[-2:]
    out = pl.pallas_call(
        functools.partial(assemble_kernel, order=order),
        grid_spec=pltpu.PrefetchScalarGridSpec(
            num_scalar_prefetch=1,
            grid=(1,),
            in_specs=[pl.BlockSpec(shape, lambda i, idx: (0,) * 4)] * 4,
            out_specs=pl.BlockSpec((32, rows, cols), lambda i, idx: (0, 0, 0)),
        ),
        out_shape=jax.ShapeDtypeStruct((32, rows, cols), pieces[0].dtype),
        compiler_params=pltpu.CompilerParams(**PARAMS),
        name="assemble",
    )(idx, *pieces)
    return out.reshape(32 * rows, cols)


def row8(v, width=None):
    v = v.reshape(1, -1)
    if width is not None:
        v = jnp.pad(v, ((0, 0), (0, width - v.shape[1])))
    return jnp.broadcast_to(v, (8, v.shape[1]))


def body(
    block_input,
    cotangent,
    in_weight,
    dt_weight,
    out_weight,
    norm_gain,
    conv_weight,
    conv_bias,
    dt_bias,
    decay_log,
    skip_gain,
    gate_gain,
    in_left,
    in_right,
    in_left_root,
    in_right_root,
    dt_left,
    dt_right,
    dt_left_root,
    dt_right_root,
    out_left,
    out_right,
    out_left_root,
    out_right_root,
    vector_moment,
):
    seq_count, local_len, _ = block_input.shape
    seq_devices = lax.axis_size("seq")
    row_count = seq_count * local_len
    up = [(i, i + 1) for i in range(seq_devices - 1)]
    down = [(i + 1, i) for i in range(seq_devices - 1)]

    in_low = in_weight.astype(BF)
    dt_low = jnp.pad(dt_weight.astype(BF), ((0, 0), (0, 128 - HEADS)))
    main = lax.all_gather(
        jnp.concatenate([in_low[:, DI:], dt_low], axis=1), AXES, axis=0, tiled=True
    )
    part = jnp.arange(128)
    channel = jnp.arange(DI)
    emat = (
        ((part[:, None] % 32) == (channel[None, :] // HEADDIM)) & (part[:, None] < 96)
    ).astype(BF)
    gmat = ((channel[:, None] // HEADDIM) == part[None, :]).astype(BF)
    skip_wide = row8(jnp.repeat(skip_gain, HEADDIM))
    alog = row8(decay_log, 128)
    dtb = row8(jnp.concatenate([dt_bias, jnp.full((128 - HEADS,), -1e4, F32)]))
    cw8 = jnp.pad(conv_weight, ((0, 4), (0, 0)))
    gain8, cb8 = row8(norm_gain), row8(conv_bias)
    ggain8 = row8(gate_gain)
    tables = (emat, gmat, skip_wide, alog, dtb, cw8, gain8, cb8, ggain8)
    torus_sizes = tuple(lax.axis_size(a) for a in ("z", "x", "core", "seq"))
    direct = torus_sizes == (4, 2, 2, 2)
    idx = jnp.stack([lax.axis_index(a) for a in ("z", "x", "core", "seq")]).astype(jnp.int32)
    gate_low, out_low = in_low[:, :DI], out_weight.astype(BF)
    if direct:
        order = ("z", "x")
        gate_near = pick(gate_low.reshape(2, -1, DI), idx[3])
        out_near = pick(out_low.reshape(2, -1, D), idx[3])
        gate_near = around(around(gate_near, "z"), "x")
        out_near = around(around(out_near, "z"), "x")
        main = lax.optimization_barrier((main, gate_near, out_near) + tables)[0]
        gate_got = swapped(gate_near, "seq", 2, 1)
        out_got = swapped(out_near, "seq", 2, 1)
        gate_far = swapped(gate_near, "core", 2, 1)
        out_far = swapped(out_near, "core", 2, 1)
    else:
        wg = lax.all_gather(gate_low, AXES, axis=0, tiled=True)
        wo = lax.all_gather(out_low, AXES, axis=0, tiled=True)
    halo = lax.ppermute(block_input[:, local_len - 8 :, :], "seq", up)

    normed, mixed, pre, z, local_state, total = run_first(
        block_input, halo, gain8, main, cw8, cb8, dtb, alog, emat
    )
    span = jnp.repeat(jnp.exp(total[:, 0:1, :HEADS]), HEADDIM, axis=2)
    enter = lax.ppermute(local_state, "seq", up)
    for _ in range(seq_devices - 2):
        enter = lax.ppermute(local_state + span * enter, "seq", up)

    if direct:
        out_far_got = swapped(out_got, "core", 2, 1)
        gate_far_got = swapped(gate_got, "core", 2, 1)
        wo = assemble(idx, (out_near, out_got, out_far, out_far_got), order)
        wg = assemble(idx, (gate_near, gate_got, gate_far, gate_far_got), order)
    normed_rows = normed.reshape(row_count, D)
    upstream = cotangent.reshape(row_count, D)
    gate_part = dot(normed_rows, wg)
    branch_grad = dot(upstream, wo, NT)
    (
        block_output, branch, states_grad, gate_grad, states, rdot, local_dstate, row_sums,
    ) = run_second(
        pre, z, gate_part, branch_grad, block_input, enter, wo, skip_wide, ggain8, alog,
        gmat,
    )
    leave = lax.ppermute(local_dstate, "seq", down)
    for _ in range(seq_devices - 2):
        leave = lax.ppermute(local_dstate + span * leave, "seq", down)

    out_partial = dot(branch, upstream, TN)
    gate_partial = dot(normed_rows, gate_grad, TN)
    if direct:
        gate_pair = core_exchange(gate_partial, idx[2])
        out_pair = core_exchange(out_partial, idx[2])
        early, early_own = chip_sum(idx, [gate_pair, out_pair])
        states_grad, early = lax.optimization_barrier((states_grad, early))
        early = lax.all_to_all(early, ("z", "x"), split_axis=0, concat_axis=0, tiled=True)

    mgrad, last8, first8, column_sums = run_third(
        pre, mixed, z, states_grad, states, rdot, leave, cw8, skip_wide, alog, gmat
    )
    near = lax.ppermute(first8, "seq", down)
    mgrad, extra = run_patch(mgrad, mixed, last8, near, cw8)
    conv_weight_grad = (column_sums + extra)[:KCONV]
    conv_bias_grad = column_sums[KCONV]

    mgrad_rows = mgrad.reshape(row_count, WIDE)
    mixed_local = dot(normed_rows, mgrad_rows, TN)
    normed_grad = (
        dot(gate_grad, wg, NT) + dot(mgrad_rows, main, NT)
    )
    incoming = block_input.reshape(row_count, D).astype(F32)
    _, norm_back = jax.vjp(norm_piece, incoming, norm_gain)
    input_part, norm_gain_grad = norm_back(normed_grad)
    input_grad = (input_part + upstream.astype(F32)).reshape(block_input.shape)

    vector_local = jnp.concatenate(
        [
            norm_gain_grad,
            row_sums[0],
            conv_weight_grad.reshape(-1),
            conv_bias_grad,
            column_sums[5, :HEADS],
            -jnp.exp(decay_log) * column_sums[6, :HEADS],
            row_sums[1].reshape(HEADS, HEADDIM).sum(1),
        ]
    )
    if direct:
        late, late_own = chip_sum(idx, [core_exchange(mixed_local, idx[2])])
        vector_local, early, late = lax.optimization_barrier((vector_local, early, late))
        late = lax.all_to_all(late, ("z", "x"), split_axis=0, concat_axis=0, tiled=True)
        early_own = owner_sum(idx, early_own, early)
        early_own = early_own + swapped(early_own, "seq", 2, 1)
        share = D // 16
        gate_sum = early_own[:share]
        out_grad = jnp.concatenate([early_own[share:, :D], early_own[share:, D:]], axis=0)
        late_own = owner_sum(idx, late_own, late)
        mixed_sum = late_own + swapped(late_own, "seq", 2, 1)
    else:
        gate_sum = reduce_plain(core_sum(gate_partial))
        out_grad = reduce_split(core_sum(out_partial))
        mixed_sum = reduce_plain(core_sum(mixed_local))
    vector_rows = jnp.pad(vector_local, (0, -vector_local.shape[0] % 1024)).reshape(-1, 128)
    for axis in ("core", "seq", "x", "z"):
        if direct and axis == "x":
            vector_rows = lax.optimization_barrier((late, vector_rows))[1]
        vector_rows = xor_sum(vector_rows, axis)
    vector_grad = vector_rows.reshape(-1)[: vector_local.shape[0]]

    in_grad = jnp.concatenate([gate_sum, mixed_sum[:, :CONVCH]], axis=1)
    dt_grad = mixed_sum[:, CONVCH : CONVCH + HEADS]

    in_update, in_left_new, in_right_new = kron_update(
        in_grad, in_left, in_right, in_left_root, in_right_root
    )
    dt_update, dt_left_wide, dt_right_wide = kron_update(
        dt_grad, dt_left[:, None], dt_right[:, None], dt_left_root[:, None], dt_right_root[:, None]
    )
    out_update, out_left_new, out_right_new = kron_update(
        out_grad, out_left, out_right, out_left_root, out_right_root
    )
    vector_moment_new = 0.5 * vector_moment + 0.5 * vector_grad * vector_grad
    vector_update = -LR_VEC * vector_grad * lax.rsqrt(vector_moment_new)
    return (
        block_output,
        input_grad,
        in_grad,
        dt_grad,
        out_grad,
        in_update,
        dt_update,
        out_update,
        in_left_new,
        in_right_new,
        dt_left_wide[:, 0],
        dt_right_wide[:, 0],
        out_left_new,
        out_right_new,
        vector_grad,
        vector_moment_new,
        vector_update,
    )


def solution(mesh):
    dp, seq = mesh.shape["dp"], mesh.shape["seq"]
    split = (4, dp // 8, 2)
    torus = jax.sharding.Mesh(mesh.devices.reshape(split + (seq,)), AXES + ("seq",))
    tokens = P(AXES, "seq", None)
    rows = P(AXES, None)
    tri = P(AXES, None, None)
    quad = P(AXES, None, None, None)
    placed = (
        (tokens, tokens, rows, rows, rows) + (P(),) * 7 + (quad,) * 4 + (tri,) * 4 + (quad,) * 4 + (P(),)
    )

    return jax.shard_map(
        body,
        mesh=torus,
        in_specs=placed,
        out_specs=(tokens, tokens)
        + (rows,) * 6
        + (quad, quad, tri, tri, quad, quad)
        + (P(), P(), P()),
        check_vma=False,
    )
```

```python
import functools

import jax
import jax.numpy as jnp
from jax import lax
from jax.experimental import pallas as pl
from jax.experimental.pallas import tpu as pltpu
from jax.sharding import PartitionSpec as P


D = 768
HEADS = 24
HEADDIM = 64
DSTATE = 128
KCONV = 4
DI = 1536
CONVCH = 1792
WIDE = CONVCH + 128
ROW_BLOCK = 24
COL_BLOCK = 128

BL = 128
PAIRS = HEADS // 2

AXES = ("z", "x", "core")

EPS = 1e-05
LR = 0.25
LR_VEC = 0.02
NEG = -1e30
LOG2E = 1.4426950408889634
BF = jnp.bfloat16
F32 = jnp.float32
NN = (((1,), (0,)), ((), ()))
NT = (((1,), (1,)), ((), ()))
TN = (((0,), (0,)), ((), ()))


def dot(a, b, dims=NN):
    return lax.dot_general(a, b, dims, preferred_element_type=F32)


def split2(v):
    high = v.astype(BF)
    return high, (v - high.astype(F32)).astype(BF)


def dot3(a, b, dims=NN):
    ah, al = split2(a)
    bh, bl = split2(b)
    return dot(ah, bh, dims) + dot(al, bh, dims) + dot(ah, bl, dims)


def pack(v):
    high = v.astype(BF).astype(F32)
    rest = v - high
    mid = rest.astype(BF).astype(F32)
    low = rest - mid
    return (high + pltpu.roll(mid, 32, 1) + pltpu.roll(low, 64, 1)).astype(BF)


def head_lanes(shape):
    return lax.broadcasted_iota(jnp.int32, shape, 1) < HEADS


def prefix(tri, v):
    parts = dot(tri, pack(v))
    total = parts + pltpu.roll(parts, 96, 1) + pltpu.roll(parts, 64, 1)
    return jnp.where(head_lanes(total.shape), total, 0.0)


def expand(v, emat):
    return dot(pack(v), emat)


def head_sum(v, gather):
    high, low = split2(v)
    return dot(high, gather) + dot(low, gather)


def tri_mask(lower):
    rows = lax.broadcasted_iota(jnp.int32, (BL, BL), 0)
    cols = lax.broadcasted_iota(jnp.int32, (BL, BL), 1)
    return (rows >= cols) if lower else (cols >= rows)


def softplus(v):
    return jnp.maximum(v, 0.0) + jnp.log1p(jnp.exp(-jnp.abs(v)))


def sigmoid(v):
    return 0.5 * jnp.tanh(0.5 * v) + 0.5


def silu(v):
    half = 0.5 * v
    return half * jnp.tanh(half) + half


def silu_parts(v):
    half = 0.5 * v
    curve = jnp.tanh(half)
    return half * curve + half, 0.5 * curve + 0.5


def rates(alog_ref):
    rate = -jnp.exp(alog_ref[0:1, :])
    return jnp.where(head_lanes(rate.shape), rate, 0.0)


def pair_masks():
    left = lax.broadcasted_iota(jnp.int32, (BL, BL), 1) < HEADDIM
    first = jnp.where(left, 1.0, 0.0)
    return first.astype(BF), (1.0 - first).astype(BF)


def pair_blocks(v, masks):
    return jnp.concatenate([v * masks[0], v * masks[1]], axis=0)


def norm_rows(u, gain):
    inv = lax.rsqrt(jnp.mean(u * u, axis=-1, keepdims=True) + EPS)
    return u * inv * gain


def first_kernel(
    u_ref, halo_ref, gain_ref, w_ref, cw_ref, cb_ref, dtb_ref, alog_ref, emat_ref,
    normed_ref, mixed_ref, pre_ref, z_ref, state_ref, total_ref,
    tail, full,
):
    step_index = pl.program_id(1)
    tile = u_ref.shape[1]
    gain = gain_ref[0:1, :]

    @pl.when(step_index == 0)
    def _():
        near = norm_rows(halo_ref[0].astype(F32), gain).astype(BF)
        tail[...] = dot(near, w_ref[:, :CONVCH]).astype(BF).astype(F32)
        state_ref[...] = jnp.zeros_like(state_ref)
        total_ref[...] = jnp.zeros_like(total_ref)

    normed = norm_rows(u_ref[0].astype(F32), gain).astype(BF)
    normed_ref[0] = normed
    projected = dot(normed, w_ref[...])
    mixed_low = projected[:, :CONVCH].astype(BF)
    mixed_ref[0] = mixed_low
    mixed = mixed_low.astype(F32)
    z = projected[:, CONVCH:].astype(BF).astype(F32) + dtb_ref[0:1, :]
    z_ref[0] = z
    for low in range(0, CONVCH, 256):
        cols = slice(low, low + 256)
        own = mixed[:, cols]
        joined = jnp.concatenate([tail[:, cols], own], axis=0)
        pre = cb_ref[0:1, cols] + cw_ref[KCONV - 1 : KCONV, cols] * own
        for tap in range(KCONV - 1):
            moved = pltpu.roll(joined, KCONV - 1 - tap, 0)[8:, :]
            pre = pre + cw_ref[tap : tap + 1, cols] * moved
        pre_ref[0, :, cols] = pre
        full[:, cols] = silu(pre)
    tail[...] = mixed[tile - 8 :, :]
    rate = rates(alog_ref)

    def block(part, carry):
        rows = pl.ds(pl.multiple_of(part * BL, BL), BL)
        tri = jnp.where(tri_mask(True), 1.0, 0.0).astype(BF)
        step = softplus(z_ref[0, rows, :])
        cum = prefix(tri, step * rate)
        last = cum[BL - 1 : BL, :]
        weights = expand(jnp.exp(last - cum) * step, emat_ref[...])
        decay = expand(
            jnp.where(head_lanes((8, 128)), jnp.broadcast_to(jnp.exp(last), (8, 128)), 0.0),
            emat_ref[...],
        )[0:1, :]
        fresh = dot3(full[rows, DI : DI + DSTATE].T, weights * full[rows, :DI])
        state_ref[0] = state_ref[0] * decay + fresh
        total_ref[0] = total_ref[0] + jnp.broadcast_to(last, (8, 128))
        return carry

    lax.fori_loop(0, tile // BL, block, 0)


def dot_wide(ahl, ah, bh, bl):
    return dot(ahl, jnp.concatenate([bh, bh], axis=0)) + dot(ah, bl)


def dot3_split(a, b, dims):
    (ah, al), (bh, bl) = a, b
    return dot(ah, bh, dims) + dot(al, bh, dims) + dot(ah, bl, dims)


def wide_split(v):
    high, low = split2(v)
    return jnp.concatenate([high, low], axis=1), high


def rows8(v):
    return jnp.sum(v.reshape(v.shape[0] // 8, 8, v.shape[1]), axis=0)


def pair_values(pair, cum, cum_t, step, mask, left, transposed):
    kernels, columns = [], []
    for h in (2 * pair, 2 * pair + 1):
        column = jnp.broadcast_to(cum[:, h : h + 1], (BL, BL))
        row = cum_t[h : h + 1, :]
        spread = (row - column) if transposed else (column - row)
        kernels.append(jnp.exp2(jnp.where(mask, spread, NEG)))
        columns.append(column)
    chosen = jnp.where(left, columns[0], columns[1])
    steps = jnp.where(left, step[:, 2 * pair : 2 * pair + 1], step[:, 2 * pair + 1 : 2 * pair + 2])
    return kernels, chosen, steps


def lane_sum(v):
    return jnp.sum(v, axis=1, keepdims=True)


def second_kernel(
    pre_ref, z_ref, normed_ref, up_ref, u_ref, enter_ref, wg_ref, wo_ref, skip_ref, ggain_ref, alog_ref,
    gmat_ref,
    out_ref, branch_ref, dy_ref, ggrad_ref, state_ref, rdot_ref, dstate_ref, sums_ref,
    gain_acc, skip_acc, state, running, ys, es, xs_ref, ss_ref, sl_ref, sg_ref, up_scratch,
):
    step_index = pl.program_id(1)
    tile = pre_ref.shape[1]

    @pl.when(step_index == 0)
    def _():
        state[...] = enter_ref[0]
        running[...] = jnp.ones_like(running)
        dstate_ref[...] = jnp.zeros_like(dstate_ref)

    @pl.when((step_index == 0) & (pl.program_id(0) == 0))
    def _():
        gain_acc[...] = jnp.zeros_like(gain_acc)
        skip_acc[...] = jnp.zeros_like(skip_acc)

    rate = rates(alog_ref)

    def block(part, carry):
        rows = pl.ds(pl.multiple_of(part * BL, BL), BL)
        mask = tri_mask(True)
        left = lax.broadcasted_iota(jnp.int32, (BL, BL), 1) < HEADDIM
        masks = pair_masks()
        tri = jnp.where(mask, 1.0, 0.0).astype(BF)
        conv = silu(pre_ref[0, rows, DI:])
        inputs_b, inputs_c = conv[:, :DSTATE], conv[:, DSTATE:]
        step = softplus(z_ref[0, rows, :])
        cum = prefix(tri, step * (rate * LOG2E))
        cum_t = cum.T
        scores = dot3(inputs_c, inputs_b, NT)
        c_wide, c_high = wide_split(inputs_c)
        bt_wide, bt_high = wide_split(inputs_b.T)
        ct_wide, ct_high = wide_split(inputs_c.T)
        squares = jnp.zeros((BL, 128), F32)
        products = jnp.zeros((BL, 128), F32)
        for quad in range(PAIRS // 2):
            cols = slice(quad * 256, (quad + 1) * 256)
            inner, grown, weighted, xs = [], [], [], []
            for pair in (2 * quad, 2 * quad + 1):
                kernels, chosen, steps = pair_values(pair, cum, cum_t, step, mask, left, False)
                x = silu(pre_ref[0, rows, pair * 128 : (pair + 1) * 128])
                scaled = steps * x
                mh, ml = split2(jnp.concatenate([scores * k for k in kernels], axis=1))
                rh, rl = (pair_blocks(v, masks) for v in split2(scaled))
                inner.append(dot(mh, rh) + dot(ml, rh) + dot(mh, rl))
                grown.append(jnp.exp2(chosen))
                weighted.append(jnp.exp2(chosen[BL - 1 : BL, :] - chosen) * scaled)
                xs.append(x)
            inner, grown, weighted, x = (
                jnp.concatenate(v, axis=1) for v in (inner, grown, weighted, xs)
            )
            held = state[:, cols]
            state_ref[0, part, :, cols] = held
            yhat = inner + grown * dot_wide(c_wide, c_high, *split2(held))
            state[:, cols] = held * grown[BL - 1 : BL, :] + dot_wide(
                bt_wide, bt_high, *split2(weighted)
            )
            ys[:, cols] = yhat
            es[:, cols] = grown
            states = (yhat + skip_ref[0:1, cols] * x).astype(BF).astype(F32)
            sl, sg = silu_parts(dot(normed_ref[0, rows, :], wg_ref[:, cols]))
            upstream = dot(up_ref[rows, :], wo_ref[cols, :], NT)
            up_scratch[:, cols] = upstream
            gated = states * sl
            xs_ref[:, cols] = x
            ss_ref[:, cols] = states
            sl_ref[:, cols] = sl
            sg_ref[:, cols] = sg
            product = gated * (upstream * ggain_ref[0:1, cols])
            squared = gated * gated
            squares = squares + squared[:, :128] + squared[:, 128:]
            products = products + product[:, :128] + product[:, 128:]
        inv = lax.rsqrt(lane_sum(squares) * (1.0 / DI) + EPS)
        pull = jnp.broadcast_to(inv * inv * lane_sum(products) * (1.0 / DI), (BL, 128))
        inv = jnp.broadcast_to(inv, (BL, 128))
        rdot = jnp.zeros((BL, 128), F32)
        for quad in range(PAIRS // 2):
            cols = slice(quad * 256, (quad + 1) * 256)
            scaled_dy, dot_terms = [], []
            for pair in (2 * quad, 2 * quad + 1):
                own_cols = slice(pair * 128, (pair + 1) * 128)
                x = xs_ref[:, own_cols]
                yhat = ys[:, own_cols]
                states = ss_ref[:, own_cols]
                sl, sg = sl_ref[:, own_cols], sg_ref[:, own_cols]
                gated = states * sl
                gain = ggain_ref[0:1, own_cols]
                upstream = up_scratch[:, own_cols]
                norm = gated * inv
                branch_ref[rows, own_cols] = (norm * gain).astype(BF)
                gain_acc[:, own_cols] += rows8(upstream * norm)
                dgated = inv * (upstream * gain - gated * pull)
                dy_low = (dgated * sl).astype(BF)
                dy_ref[rows, own_cols] = dy_low
                ggrad_ref[rows, own_cols] = (dgated * states * (sg + sl * (1.0 - sg))).astype(BF)
                dy = dy_low.astype(F32)
                skip_acc[:, own_cols] += rows8(dy * x)
                dot_terms.append(dy * yhat)
                scaled_dy.append(es[:, own_cols] * running[0:1, own_cols] * dy)
            rdot = rdot + head_sum(jnp.concatenate(dot_terms, axis=1), gmat_ref[cols, :])
            dstate_ref[0, :, cols] += dot_wide(
                ct_wide, ct_high, *split2(jnp.concatenate(scaled_dy, axis=1))
            )
            running[:, cols] = running[:, cols] * es[BL - 1 : BL, cols]
        rdot_ref[0, rows, :] = rdot
        return carry

    lax.fori_loop(0, tile // BL, block, 0)
    out_ref[0] = (u_ref[0].astype(F32) + dot(branch_ref[...], wo_ref[...])).astype(BF)

    @pl.when((step_index == pl.num_programs(1) - 1) & (pl.program_id(0) == pl.num_programs(0) - 1))
    def _():
        sums_ref[0:1, :] = jnp.sum(gain_acc[...], axis=0, keepdims=True)
        sums_ref[1:2, :] = jnp.sum(skip_acc[...], axis=0, keepdims=True)


def third_kernel(
    pre_ref, mixed_ref, z_ref, dy_ref, state_ref, rdot_ref, leave_ref, cw_ref, skip_ref, alog_ref,
    gmat_ref,
    mgrad_ref, last_ref, first_ref, sums_ref,
    cw_acc, cb_acc, dtb_acc, rate_acc, dstate, tail,
):
    step_index = pl.program_id(1)

    @pl.when(step_index == 0)
    def _():
        dstate[...] = leave_ref[0]
        tail[...] = jnp.zeros_like(tail)

    @pl.when((step_index == 0) & (pl.program_id(0) == 0))
    def _():
        for ref in (cw_acc, cb_acc, dtb_acc, rate_acc):
            ref[...] = jnp.zeros_like(ref)

    rate = rates(alog_ref)
    mask = tri_mask(False)
    left = lax.broadcasted_iota(jnp.int32, (BL, BL), 1) < HEADDIM
    masks = pair_masks()
    low_tri = jnp.where(tri_mask(True), 1.0, 0.0).astype(BF)
    high_tri = jnp.where(mask, 1.0, 0.0).astype(BF)
    wide_pre = pre_ref[0, :, DI:]
    conv, wide_sg = silu_parts(wide_pre)
    inputs_b, inputs_c = conv[:, :DSTATE], conv[:, DSTATE:]
    z = z_ref[0]
    step = softplus(z)
    cum = prefix(low_tri, step * (rate * LOG2E))
    cum_t = cum.T
    lanes = head_lanes(cum.shape)
    scores_t = dot3(inputs_b, inputs_c, NT)
    b_wide, b_high = wide_split(inputs_b)
    ct_wide, ct_high = wide_split(inputs_c.T)
    dscores_t = jnp.zeros((BL, BL), F32)
    db = jnp.zeros((BL, DSTATE), F32)
    dc = jnp.zeros((BL, DSTATE), F32)
    sums = jnp.zeros((BL + 8, 128), F32)

    def back_conv(cols, dpre):
        joined = jnp.concatenate([dpre, tail[:, cols]], axis=0)
        tail[:, cols] = dpre[0:8, :]
        mixed = mixed_ref[0, :, cols].astype(F32)
        cb_acc[:, cols] += rows8(dpre)
        mgrad = cw_ref[KCONV - 1 : KCONV, cols] * dpre
        cw_acc[KCONV - 1, :, cols] += rows8(dpre * mixed)
        for tap in range(KCONV - 1):
            moved = pltpu.roll(joined, BL + 8 - (KCONV - 1 - tap), 0)[:BL, :]
            mgrad = mgrad + cw_ref[tap : tap + 1, cols] * moved
            cw_acc[tap, :, cols] += rows8(moved * mixed)
        mgrad_ref[0, :, cols] = mgrad.astype(BF)
        last_ref[0, :, cols] = jnp.where(step_index == 0, mgrad[BL - 8 :, :], last_ref[0, :, cols])

    for quad in range(PAIRS // 2):
        cols = slice(quad * 256, (quad + 1) * 256)
        inner, grown, shrink, scaled, xs, steps_wide, slopes = [], [], [], [], [], [], []
        dy = dy_ref[:, cols].astype(F32)
        for pair in (2 * quad, 2 * quad + 1):
            kernels, chosen, steps = pair_values(pair, cum, cum_t, step, mask, left, True)
            own = pre_ref[0, :, pair * 128 : (pair + 1) * 128]
            x, sg = silu_parts(own)
            slopes.append(sg + x * (1.0 - sg))
            xd = steps * x
            mh, ml = split2(jnp.concatenate([scores_t * k for k in kernels], axis=1))
            dyb = pair_blocks(dy_ref[:, pair * 128 : (pair + 1) * 128], masks)
            inner.append(dot(mh, dyb) + dot(ml, dyb))
            sh, sl = split2(xd)
            dmix = dot(sh, dyb, NT) + dot(sl, dyb, NT)
            dscores_t = dscores_t + dmix[:, :BL] * kernels[0] + dmix[:, BL:] * kernels[1]
            grown.append(jnp.exp2(chosen))
            shrink.append(jnp.exp2(chosen[BL - 1 : BL, :] - chosen))
            scaled.append(xd)
            xs.append(x)
            steps_wide.append(steps)
        inner, grown, shrink, scaled, x, steps_wide, slopes = (
            jnp.concatenate(v, axis=1) for v in (inner, grown, shrink, scaled, xs, steps_wide, slopes)
        )
        held = state_ref[0, 0, :, cols]
        ds = dstate[:, cols]
        held_parts, ds_parts = split2(held), split2(ds)
        decay = grown[BL - 1 : BL, :]
        dscaled_state = shrink * dot_wide(b_wide, b_high, *ds_parts)
        dscaled = inner + dscaled_state
        ends = jnp.sum(scaled * dscaled_state, axis=0, keepdims=True) + decay * jnp.sum(
            held * ds, axis=0, keepdims=True
        )
        sums = sums + head_sum(
            jnp.concatenate([x * dscaled, jnp.broadcast_to(ends, (8, 256))], axis=0),
            gmat_ref[cols, :],
        )
        grown_parts = split2(grown * dy)
        dc = dc + dot3_split(grown_parts, held_parts, NT)
        db = db + dot3_split(split2(shrink * scaled), ds_parts, NT)
        dstate[:, cols] = decay * ds + dot_wide(ct_wide, ct_high, *grown_parts)
        back_conv(cols, (steps_wide * dscaled + skip_ref[0:1, cols] * dy) * slopes)

    direct = sums[:BL]
    is_last = lax.broadcasted_iota(jnp.int32, (BL, 128), 0) == BL - 1
    dcum = rdot_ref[0] - step * direct + jnp.where(is_last, sums[BL : BL + 1, :], 0.0)
    dcum = jnp.where(lanes, dcum, 0.0)
    drate = prefix(high_tri, dcum)
    dz = (rate * drate + direct) * sigmoid(z)
    mgrad_ref[0, :, CONVCH:] = dz.astype(BF)
    dtb_acc[...] += rows8(dz)
    rate_acc[...] += rows8(step * drate)
    db = db + dot3(dscores_t, inputs_c)
    dc = dc + dot3(dscores_t.T, inputs_b)
    back_conv(
        slice(DI, CONVCH),
        jnp.concatenate([db, dc], axis=1) * (wide_sg + conv * (1.0 - wide_sg)),
    )
    first_ref[0] = tail[...]

    @pl.when((step_index == pl.num_programs(1) - 1) & (pl.program_id(0) == pl.num_programs(0) - 1))
    def _():
        for tap in range(KCONV):
            sums_ref[tap : tap + 1, :] = jnp.sum(cw_acc[tap], axis=0, keepdims=True)
        sums_ref[4:5, :] = jnp.sum(cb_acc[...], axis=0, keepdims=True)
        sums_ref[5:6, :128] = jnp.sum(dtb_acc[...], axis=0, keepdims=True)
        sums_ref[6:7, :128] = jnp.sum(rate_acc[...], axis=0, keepdims=True)


def patch_kernel(mgrad_ref, mixed_ref, last_ref, near_ref, cw_ref, out_ref, extra_ref):
    @pl.when(pl.program_id(0) == 0)
    def _():
        extra_ref[...] = jnp.zeros_like(extra_ref)

    rows = [last_ref[0, i : i + 1, :] for i in range(8)]
    near = [near_ref[0, i : i + 1, :] for i in range(KCONV - 1)]
    held = mixed_ref[0].astype(F32)
    first = 8 - (KCONV - 1)
    for k in range(KCONV - 1):
        for j in range(k, KCONV - 1):
            rows[first + j] = rows[first + j] + cw_ref[k : k + 1, :] * near[j - k]
            extra_ref[k : k + 1, :] += near[j - k] * held[8 + first + j : 9 + first + j, :]
    old = mgrad_ref[0].astype(F32)
    patched = jnp.concatenate([old[:8, :CONVCH], jnp.concatenate(rows, axis=0)], axis=0)
    out_ref[0, :, :CONVCH] = patched.astype(BF)
    out_ref[0, :, CONVCH:] = mgrad_ref[0, :, CONVCH:]


PARAMS = dict(vmem_limit_bytes=60 * 1024 * 1024)


def whole(shape):
    zeros = (0,) * len(shape)
    return pl.BlockSpec(shape, lambda b, i: zeros)


def run_first(u, halo, gain, w, cw, cb, dtb, alog, emat):
    seqs, length, _ = u.shape
    tile = min(256, length)
    grid = (seqs, length // tile)
    tok = lambda width: pl.BlockSpec((1, tile, width), lambda b, i: (b, i, 0))
    per = lambda *shape: pl.BlockSpec((1,) + shape, lambda b, i: (b,) + (0,) * len(shape))
    return pl.pallas_call(
        first_kernel,
        grid=grid,
        in_specs=[
            tok(D), per(8, D), whole(gain.shape), whole(w.shape),
            whole(cw.shape), whole(cb.shape), whole(dtb.shape), whole(alog.shape), whole(emat.shape),
        ],
        out_specs=[
            tok(D), tok(CONVCH), tok(CONVCH), tok(128), per(DSTATE, DI), per(8, 128),
        ],
        out_shape=[
            jax.ShapeDtypeStruct((seqs, length, D), BF),
            jax.ShapeDtypeStruct((seqs, length, CONVCH), BF),
            jax.ShapeDtypeStruct((seqs, length, CONVCH), F32),
            jax.ShapeDtypeStruct((seqs, length, 128), F32),
            jax.ShapeDtypeStruct((seqs, DSTATE, DI), F32),
            jax.ShapeDtypeStruct((seqs, 8, 128), F32),
        ],
        scratch_shapes=[pltpu.VMEM((8, CONVCH), F32), pltpu.VMEM((tile, CONVCH), F32)],
        compiler_params=pltpu.CompilerParams(**PARAMS),
        name="first",
    )(u, halo, gain, w, cw, cb, dtb, alog, emat)


def run_second(pre, z, normed, up, u, enter, wg, wo, skip, ggain, alog, gmat):
    seqs, length, _ = u.shape
    tile = min(256, length)
    steps = length // tile
    parts = tile // BL
    grid = (seqs, steps)
    tok = lambda width: pl.BlockSpec((1, tile, width), lambda b, i: (b, i, 0))
    flat = lambda width: pl.BlockSpec((tile, width), lambda b, i: (b * steps + i, 0))
    per = lambda *shape: pl.BlockSpec((1,) + shape, lambda b, i: (b,) + (0,) * len(shape))
    rows = seqs * length
    return pl.pallas_call(
        second_kernel,
        grid=grid,
        in_specs=[
            tok(CONVCH), tok(128), tok(D), flat(D), tok(D), per(DSTATE, DI), whole(wg.shape),
            whole(wo.shape),
            whole(skip.shape), whole(ggain.shape), whole(alog.shape), whole(gmat.shape),
        ],
        out_specs=[
            tok(D), flat(DI), flat(DI), flat(DI),
            pl.BlockSpec((1, parts, DSTATE, DI), lambda b, i: (b, i, 0, 0)),
            tok(128), per(DSTATE, DI), whole((8, DI)),
        ],
        out_shape=[
            jax.ShapeDtypeStruct((seqs, length, D), BF),
            jax.ShapeDtypeStruct((rows, DI), BF),
            jax.ShapeDtypeStruct((rows, DI), BF),
            jax.ShapeDtypeStruct((rows, DI), BF),
            jax.ShapeDtypeStruct((seqs, length // BL, DSTATE, DI), F32),
            jax.ShapeDtypeStruct((seqs, length, 128), F32),
            jax.ShapeDtypeStruct((seqs, DSTATE, DI), F32),
            jax.ShapeDtypeStruct((8, DI), F32),
        ],
        scratch_shapes=[
            pltpu.VMEM((8, DI), F32), pltpu.VMEM((8, DI), F32), pltpu.VMEM((DSTATE, DI), F32),
            pltpu.VMEM((8, DI), F32), *[pltpu.VMEM((BL, DI), F32)] * 7,
        ],
        compiler_params=pltpu.CompilerParams(**PARAMS),
        name="second",
    )(pre, z, normed, up, u, enter, wg, wo, skip, ggain, alog, gmat)


def run_third(pre, mixed, z, dy, states, rdot, leave, cw, skip, alog, gmat):
    seqs, length, _ = pre.shape
    steps = length // BL
    grid = (seqs, steps)
    tok = lambda width: pl.BlockSpec((1, BL, width), lambda b, i: (b, steps - 1 - i, 0))
    per = lambda *shape: pl.BlockSpec((1,) + shape, lambda b, i: (b,) + (0,) * len(shape))
    return pl.pallas_call(
        third_kernel,
        grid=grid,
        in_specs=[
            tok(CONVCH), tok(CONVCH), tok(128),
            pl.BlockSpec((BL, DI), lambda b, i: (b * steps + steps - 1 - i, 0)),
            pl.BlockSpec((1, 1, DSTATE, DI), lambda b, i: (b, steps - 1 - i, 0, 0)),
            tok(128), per(DSTATE, DI), whole(cw.shape), whole(skip.shape), whole(alog.shape),
            whole(gmat.shape),
        ],
        out_specs=[
            tok(WIDE), per(8, CONVCH), per(8, CONVCH), whole((8, CONVCH)),
        ],
        out_shape=[
            jax.ShapeDtypeStruct((seqs, length, WIDE), BF),
            jax.ShapeDtypeStruct((seqs, 8, CONVCH), F32),
            jax.ShapeDtypeStruct((seqs, 8, CONVCH), F32),
            jax.ShapeDtypeStruct((8, CONVCH), F32),
        ],
        scratch_shapes=[
            pltpu.VMEM((KCONV, 8, CONVCH), F32), pltpu.VMEM((8, CONVCH), F32),
            pltpu.VMEM((8, 128), F32), pltpu.VMEM((8, 128), F32),
            pltpu.VMEM((DSTATE, DI), F32), pltpu.VMEM((8, CONVCH), F32),
        ],
        compiler_params=pltpu.CompilerParams(**PARAMS),
        name="third",
    )(pre, mixed, z, dy, states, rdot, leave, cw, skip, alog, gmat)


def run_patch(mgrad, mixed, last8, near, cw):
    seqs, length, _ = mgrad.shape
    end = length // 16 - 1
    tok = lambda width: pl.BlockSpec((1, 16, width), lambda b: (b, end, 0))
    per = pl.BlockSpec((1, 8, CONVCH), lambda b: (b, 0, 0))
    row = pl.BlockSpec((8, CONVCH), lambda b: (0, 0))
    return pl.pallas_call(
        patch_kernel,
        grid=(seqs,),
        in_specs=[tok(WIDE), tok(CONVCH), per, per, row],
        out_specs=[tok(WIDE), row],
        out_shape=[
            jax.ShapeDtypeStruct(mgrad.shape, BF),
            jax.ShapeDtypeStruct((8, CONVCH), F32),
        ],
        input_output_aliases={0: 0},
        name="patch",
    )(mgrad, mixed, last8, near, cw)


def kron_update(gradient, left_stat, right_stat, left_root, right_root):
    row_tiles, col_tiles = (left_stat.shape[0], left_stat.shape[1])
    row_size, col_size = (left_stat.shape[-1], right_stat.shape[-1])
    grad_tiles = gradient.reshape(row_tiles, row_size, col_tiles, col_size).transpose(0, 2, 1, 3)
    left_new = 0.5 * left_stat + 0.5 * jnp.einsum(
        "abij,abkj->abik", grad_tiles, grad_tiles, precision=lax.Precision.HIGH
    )
    right_new = 0.5 * right_stat + 0.5 * jnp.einsum(
        "abji,abjk->abik", grad_tiles, grad_tiles, precision=lax.Precision.HIGH
    )
    shaped = jnp.einsum("abij,abjk->abik", left_root, grad_tiles, precision=lax.Precision.HIGH)
    shaped = jnp.einsum("abij,abjk->abik", shaped, right_root, precision=lax.Precision.HIGH)
    update = (-LR * shaped).transpose(0, 2, 1, 3).reshape(gradient.shape)
    return (update, left_new, right_new)


def kron_kernel(*refs):
    grad_ref, left_ref, right_ref, left_root_ref, right_root_ref = refs[:5]
    update_ref, left_new_ref, right_new_ref = refs[-3:]
    for r in range(left_ref.shape[0]):
        rows = slice(r * ROW_BLOCK, (r + 1) * ROW_BLOCK)
        for c in range(left_ref.shape[1]):
            cols = slice(c * COL_BLOCK, (c + 1) * COL_BLOCK)
            grad = grad_ref[rows, cols]
            left_new_ref[r, c] = 0.5 * left_ref[r, c] + 0.5 * dot3(grad, grad, NT)
            right_new_ref[r, c] = 0.5 * right_ref[r, c] + 0.5 * dot3(grad.T, grad)
            shaped = dot3(dot3(left_root_ref[r, c], grad), right_root_ref[r, c])
            update_ref[rows, cols] = -LR * shaped


def kron_tiles(grad, left, right, left_root, right_root, first, step, earlier=None):
    row_tiles = left.shape[0]
    rows, cols = grad.shape
    base = first // step
    stat = lambda size: pl.BlockSpec(
        (row_tiles, step, size, size), lambda i: (0, base + i, 0, 0)
    )
    wide = step * COL_BLOCK
    ins = [grad, left, right, left_root, right_root]
    in_specs = [pl.BlockSpec((rows, wide), lambda i: (0, i))] + [stat(ROW_BLOCK), stat(COL_BLOCK)] * 2
    aliases = {}
    if earlier is not None:
        ins += list(earlier)
        in_specs += [pl.BlockSpec(memory_space=pl.ANY)] * 3
        aliases = {5: 0, 6: 1, 7: 2}
    total = left.shape[1] * COL_BLOCK
    return pl.pallas_call(
        kron_kernel,
        grid=(cols // wide,),
        in_specs=in_specs,
        out_specs=[
            pl.BlockSpec((rows, wide), lambda i: (0, base + i)), stat(ROW_BLOCK), stat(COL_BLOCK),
        ],
        out_shape=[
            jax.ShapeDtypeStruct((rows, total), F32),
            jax.ShapeDtypeStruct(left.shape, F32),
            jax.ShapeDtypeStruct(right.shape, F32),
        ],
        input_output_aliases=aliases,
        compiler_params=pltpu.CompilerParams(**PARAMS),
        name="kron",
    )(*ins)


def back_kernel(
    ggrad_ref, mgrad_ref, wg_ref, main_ref, u_ref, up_ref, gain_ref, out_ref, gain_grad_ref
):
    @pl.when(pl.program_id(0) == 0)
    def _():
        gain_grad_ref[...] = jnp.zeros_like(gain_grad_ref)

    grad = dot(ggrad_ref[...], wg_ref[...], NT) + dot(mgrad_ref[...], main_ref[...], NT)
    u = u_ref[...].astype(F32)
    inv = lax.rsqrt(jnp.mean(u * u, axis=-1, keepdims=True) + EPS)
    norm = u * inv
    gain_grad_ref[...] += rows8(grad * norm)
    scaled = grad * gain_ref[0:1, :]
    pull = jnp.mean(scaled * norm, axis=-1, keepdims=True)
    out_ref[...] = up_ref[...].astype(F32) + inv * (scaled - norm * pull)


def run_back(ggrad, mgrad, wg, main, u, up, gain):
    rows = u.shape[0]
    tile = min(256, rows)
    tok = lambda width: pl.BlockSpec((tile, width), lambda i: (i, 0))
    return pl.pallas_call(
        back_kernel,
        grid=(rows // tile,),
        in_specs=[
            tok(DI), tok(WIDE), pl.BlockSpec(wg.shape, lambda i: (0, 0)),
            pl.BlockSpec(main.shape, lambda i: (0, 0)), tok(D), tok(D),
            pl.BlockSpec(gain.shape, lambda i: (0, 0)),
        ],
        out_specs=[tok(D), pl.BlockSpec((8, D), lambda i: (0, 0))],
        out_shape=[jax.ShapeDtypeStruct((rows, D), F32), jax.ShapeDtypeStruct((8, D), F32)],
        compiler_params=pltpu.CompilerParams(**PARAMS),
        name="back",
    )(ggrad, mgrad, wg, main, u, up, gain)


def swapped(v, axis, size, offset):
    return lax.ppermute(v, axis, [(i, (i + offset) % size) for i in range(size)])


def pick(v, index):
    return lax.dynamic_index_in_dim(v, index, 0, keepdims=False)


def scatter_stage(v, axis, kind=BF):
    size = lax.axis_size(axis)
    here = lax.axis_index(axis)
    total = pick(v, here)
    for offset in range(1, size):
        sent = pick(v, lax.rem(here + offset, size)).astype(kind)
        total = total + swapped(sent, axis, size, offset).astype(F32)
    return total


def gather_stage(v, axis):
    size = lax.axis_size(axis)
    here = lax.axis_index(axis)
    out = jnp.zeros((size,) + v.shape, v.dtype)
    out = lax.dynamic_update_index_in_dim(out, v, here, 0)
    for offset in range(1, size):
        got = swapped(v, axis, size, offset)
        out = lax.dynamic_update_index_in_dim(out, got, lax.rem(here - offset + size, size), 0)
    return out


def core_sum(partial):
    z, x, core = (lax.axis_size(a) for a in ("z", "x", "core"))
    rows, cols = partial.shape
    blocks = partial.reshape(z, x, core, rows // (z * x * core), cols)
    return scatter_stage(jnp.moveaxis(blocks, 2, 0), "core", F32)


def across(v):
    return scatter_stage(scatter_stage(jnp.moveaxis(v, 1, 0), "x"), "z")


def reduce_plain(v):
    owned = across(v)
    total = owned
    size = lax.axis_size("seq")
    if size > 2:
        return lax.psum(owned, "seq")
    for offset in range(1, size):
        total = total + swapped(owned, "seq", size, offset)
    return total


def reduce_split(v):
    size = lax.axis_size("seq")
    z, x, rows, cols = v.shape
    if cols % (128 * size):
        return reduce_plain(v)
    v = jnp.moveaxis(v.reshape(z, x, rows, size, cols // size), 3, 0)
    owned = across(scatter_stage(v, "seq"))
    return jnp.moveaxis(gather_stage(owned, "seq"), 0, 1).reshape(rows, cols)


def xor_sum(v, axis):
    size = lax.axis_size(axis)
    bit = 1
    while bit < size:
        v = v + lax.ppermute(v, axis, [(i, i ^ bit) for i in range(size)])
        bit *= 2
    return v


STEP_OWNERS = 4


def chip_kernel(idx, *refs):
    send_ref, own_ref = refs[-2:]
    width = own_ref.shape[1]
    for owner in range(STEP_OWNERS):
        mine = pl.program_id(0) * STEP_OWNERS + owner == idx[0] * 2 + idx[1]
        row, col = 0, 0
        for part_ref, got_ref in zip(refs[:-2:2], refs[1:-2:2]):
            total = part_ref[owner, 0] + got_ref[owner]
            rows = total.shape[0] * total.shape[1] // width
            for low in range(0, total.shape[0], rows):
                piece = total[low : low + rows]
                at = (slice(row, row + rows), slice(col, col + piece.shape[1]))
                send_ref[(owner,) + at] = piece.astype(BF)

                @pl.when(mine)
                def _(at=at, piece=piece):
                    own_ref[at] = piece

                col += piece.shape[1]
                if col == width:
                    row, col = row + rows, 0


def chip_sum(idx, pairs):
    in_specs, ins, total, width = [], [], 0, 0
    for blocks, got in pairs:
        _, _, rows, cols = blocks.shape
        width = max(width, cols)
        total += rows * cols
        ins += [blocks, got]
        in_specs += [
            pl.BlockSpec((STEP_OWNERS, 1, rows, cols), lambda i, idx: (i, idx[2], 0, 0)),
            pl.BlockSpec((STEP_OWNERS, rows, cols), lambda i, idx: (i, 0, 0)),
        ]
    rows = total // width
    return pl.pallas_call(
        chip_kernel,
        grid_spec=pltpu.PrefetchScalarGridSpec(
            num_scalar_prefetch=1,
            grid=(8 // STEP_OWNERS,),
            in_specs=in_specs,
            out_specs=[
                pl.BlockSpec((STEP_OWNERS, rows, width), lambda i, idx: (i, 0, 0)),
                pl.BlockSpec((rows, width), lambda i, idx: (0, 0)),
            ],
        ),
        out_shape=[
            jax.ShapeDtypeStruct((8, rows, width), BF),
            jax.ShapeDtypeStruct((rows, width), F32),
        ],
        compiler_params=pltpu.CompilerParams(**PARAMS),
        name="chip_sum",
    )(idx, *ins)


def owner_kernel(idx, own_ref, got_ref, out_ref):
    mine = idx[0] * 2 + idx[1]
    total = own_ref[...]
    for i in range(8):
        total = total + jnp.where(mine == i, 0.0, got_ref[i].astype(F32))
    out_ref[...] = total


def owner_sum(idx, own, got):
    rows, width = own.shape
    tile = 48
    return pl.pallas_call(
        owner_kernel,
        grid_spec=pltpu.PrefetchScalarGridSpec(
            num_scalar_prefetch=1,
            grid=(rows // tile,),
            in_specs=[
                pl.BlockSpec((tile, width), lambda i, idx: (i, 0)),
                pl.BlockSpec((8, tile, width), lambda i, idx: (0, i, 0)),
            ],
            out_specs=pl.BlockSpec((tile, width), lambda i, idx: (i, 0)),
        ),
        out_shape=jax.ShapeDtypeStruct((rows, width), F32),
        name="owner_sum",
    )(idx, own, got)


def core_exchange(partial, core):
    rows, cols = partial.shape
    blocks = partial.reshape(8, 2, rows // 16, cols)
    sent = lax.dynamic_index_in_dim(blocks, 1 - core, 1, keepdims=False)
    return blocks, swapped(sent, "core", 2, 1)


def around(v, axis):
    size = lax.axis_size(axis)
    return jnp.stack([v] + [swapped(v, axis, size, offset) for offset in range(1, size)])


def assemble_kernel(idx, *refs, order):
    out_ref = refs[-1]
    sizes = {"z": 4, "x": 2}
    here = {"z": idx[0], "x": idx[1]}
    spots = ((idx[2], idx[3]), (idx[2], 1 - idx[3]), (1 - idx[2], idx[3]), (1 - idx[2], 1 - idx[3]))
    for ref, (core, seq) in zip(refs[:-1], spots):
        for a in range(ref.shape[0]):
            for b in range(ref.shape[1]):
                at = dict(
                    (axis, lax.rem(here[axis] - back + sizes[axis], sizes[axis]))
                    for axis, back in zip(order[::-1], (a, b))
                )
                out_ref[((at["z"] * 2 + at["x"]) * 2 + core) * 2 + seq] = ref[a, b]


def assemble(idx, pieces, order):
    shape = pieces[0].shape
    rows, cols = shape[-2:]
    out = pl.pallas_call(
        functools.partial(assemble_kernel, order=order),
        grid_spec=pltpu.PrefetchScalarGridSpec(
            num_scalar_prefetch=1,
            grid=(1,),
            in_specs=[pl.BlockSpec(shape, lambda i, idx: (0,) * 4)] * 4,
            out_specs=pl.BlockSpec((32, rows, cols), lambda i, idx: (0, 0, 0)),
        ),
        out_shape=jax.ShapeDtypeStruct((32, rows, cols), pieces[0].dtype),
        compiler_params=pltpu.CompilerParams(**PARAMS),
        name="assemble",
    )(idx, *pieces)
    return out.reshape(32 * rows, cols)


def row8(v, width=None):
    v = v.reshape(1, -1)
    if width is not None:
        v = jnp.pad(v, ((0, 0), (0, width - v.shape[1])))
    return jnp.broadcast_to(v, (8, v.shape[1]))


def body(
    block_input,
    cotangent,
    in_weight,
    dt_weight,
    out_weight,
    norm_gain,
    conv_weight,
    conv_bias,
    dt_bias,
    decay_log,
    skip_gain,
    gate_gain,
    in_left,
    in_right,
    in_left_root,
    in_right_root,
    dt_left,
    dt_right,
    dt_left_root,
    dt_right_root,
    out_left,
    out_right,
    out_left_root,
    out_right_root,
    vector_moment,
):
    seq_count, local_len, _ = block_input.shape
    seq_devices = lax.axis_size("seq")
    row_count = seq_count * local_len
    up = [(i, i + 1) for i in range(seq_devices - 1)]
    down = [(i + 1, i) for i in range(seq_devices - 1)]

    in_low = in_weight.astype(BF)
    dt_low = jnp.pad(dt_weight.astype(BF), ((0, 0), (0, 128 - HEADS)))
    main = lax.all_gather(
        jnp.concatenate([in_low[:, DI:], dt_low], axis=1), AXES, axis=0, tiled=True
    )
    part = jnp.arange(128)
    channel = jnp.arange(DI)
    emat = (
        ((part[:, None] % 32) == (channel[None, :] // HEADDIM)) & (part[:, None] < 96)
    ).astype(BF)
    gmat = ((channel[:, None] // HEADDIM) == part[None, :]).astype(BF)
    skip_wide = row8(jnp.repeat(skip_gain, HEADDIM))
    alog = row8(decay_log, 128)
    dtb = row8(jnp.concatenate([dt_bias, jnp.full((128 - HEADS,), -1e4, F32)]))
    cw8 = jnp.pad(conv_weight, ((0, 4), (0, 0)))
    gain8, cb8 = row8(norm_gain), row8(conv_bias)
    ggain8 = row8(gate_gain)
    tables = (emat, gmat, skip_wide, alog, dtb, cw8, gain8, cb8, ggain8)
    torus_sizes = tuple(lax.axis_size(a) for a in ("z", "x", "core", "seq"))
    direct = torus_sizes == (4, 2, 2, 2)
    idx = jnp.stack([lax.axis_index(a) for a in ("z", "x", "core", "seq")]).astype(jnp.int32)
    gate_low, out_low = in_low[:, :DI], out_weight.astype(BF)
    if direct:
        order = ("z", "x")
        gate_near = pick(gate_low.reshape(2, -1, DI), idx[3])
        out_near = pick(out_low.reshape(2, -1, D), idx[3])
        gate_near = around(around(gate_near, "z"), "x")
        out_near = around(around(out_near, "z"), "x")
        main = lax.optimization_barrier((main, gate_near, out_near) + tables)[0]
        gate_got = swapped(gate_near, "seq", 2, 1)
        out_got = swapped(out_near, "seq", 2, 1)
        gate_far = swapped(gate_near, "core", 2, 1)
        out_far = swapped(out_near, "core", 2, 1)
    else:
        wg = lax.all_gather(gate_low, AXES, axis=0, tiled=True)
        wo = lax.all_gather(out_low, AXES, axis=0, tiled=True)
    halo = lax.ppermute(block_input[:, local_len - 8 :, :], "seq", up)

    normed, mixed, pre, z, local_state, total = run_first(
        block_input, halo, gain8, main, cw8, cb8, dtb, alog, emat
    )
    span = jnp.repeat(jnp.exp(total[:, 0:1, :HEADS]), HEADDIM, axis=2)
    enter = lax.ppermute(local_state, "seq", up)
    for _ in range(seq_devices - 2):
        enter = lax.ppermute(local_state + span * enter, "seq", up)

    if direct:
        out_far_got = swapped(out_got, "core", 2, 1)
        gate_far_got = swapped(gate_got, "core", 2, 1)
        wo = assemble(idx, (out_near, out_got, out_far, out_far_got), order)
        wg = assemble(idx, (gate_near, gate_got, gate_far, gate_far_got), order)
    normed_rows = normed.reshape(row_count, D)
    upstream = cotangent.reshape(row_count, D)
    (
        block_output, branch, states_grad, gate_grad, states, rdot, local_dstate, row_sums,
    ) = run_second(
        pre, z, normed, upstream, block_input, enter, wg, wo, skip_wide, ggain8, alog,
        gmat,
    )
    leave = lax.ppermute(local_dstate, "seq", down)
    for _ in range(seq_devices - 2):
        leave = lax.ppermute(local_dstate + span * leave, "seq", down)

    out_partial = dot(branch, upstream, TN)
    gate_partial = dot(normed_rows, gate_grad, TN)
    if direct:
        gate_pair = core_exchange(gate_partial, idx[2])
        out_pair = core_exchange(out_partial, idx[2])
        early, early_own = chip_sum(idx, [gate_pair, out_pair])
        states_grad, early = lax.optimization_barrier((states_grad, early))
        early = lax.all_to_all(early, ("z", "x"), split_axis=0, concat_axis=0, tiled=True)

    mgrad, last8, first8, column_sums = run_third(
        pre, mixed, z, states_grad, states, rdot, leave, cw8, skip_wide, alog, gmat
    )
    near = lax.ppermute(first8, "seq", down)
    mgrad, extra = run_patch(mgrad, mixed, last8, near, cw8)
    conv_weight_grad = (column_sums + extra)[:KCONV]
    conv_bias_grad = column_sums[KCONV]

    mgrad_rows = mgrad.reshape(row_count, WIDE)
    mixed_local = dot(normed_rows, mgrad_rows, TN)
    input_grad, gain_rows = run_back(
        gate_grad, mgrad_rows, wg, main, block_input.reshape(row_count, D), upstream, gain8
    )
    input_grad = input_grad.reshape(block_input.shape)

    vector_local = jnp.concatenate(
        [
            gain_rows.sum(0),
            row_sums[0],
            conv_weight_grad.reshape(-1),
            conv_bias_grad,
            column_sums[5, :HEADS],
            -jnp.exp(decay_log) * column_sums[6, :HEADS],
            row_sums[1].reshape(HEADS, HEADDIM).sum(1),
        ]
    )
    if direct:
        mixed_pair = core_exchange(mixed_local, idx[2])
        late, late_own = chip_sum(idx, [mixed_pair])
        late = lax.all_to_all(late, ("z", "x"), split_axis=0, concat_axis=0, tiled=True)
        early_own = owner_sum(idx, early_own, early)
        early_own = early_own + swapped(early_own, "seq", 2, 1)
        share = D // 16
        gate_sum = early_own[:share]
        out_grad = jnp.concatenate([early_own[share:, :D], early_own[share:, D:]], axis=0)
        late_own = owner_sum(idx, late_own, late)
        mixed_sum = late_own + swapped(late_own, "seq", 2, 1)
    else:
        gate_sum = reduce_plain(core_sum(gate_partial))
        out_grad = reduce_split(core_sum(out_partial))
        mixed_sum = reduce_plain(core_sum(mixed_local))
    vector_rows = jnp.pad(vector_local, (0, -vector_local.shape[0] % 1024)).reshape(-1, 128)
    for axis in ("core", "seq", "x", "z"):
        if direct and axis == "x":
            vector_rows = lax.optimization_barrier((late, vector_rows))[1]
        vector_rows = xor_sum(vector_rows, axis)
    vector_grad = vector_rows.reshape(-1)[: vector_local.shape[0]]

    in_grad = jnp.concatenate([gate_sum, mixed_sum[:, :CONVCH]], axis=1)
    dt_grad = mixed_sum[:, CONVCH : CONVCH + HEADS]

    gate_tiles = kron_tiles(gate_sum, in_left, in_right, in_left_root, in_right_root, 0, 2)
    in_update, in_left_new, in_right_new = kron_tiles(
        mixed_sum[:, :CONVCH], in_left, in_right, in_left_root, in_right_root, DI // COL_BLOCK, 2,
        gate_tiles,
    )
    dt_update, dt_left_wide, dt_right_wide = kron_update(
        dt_grad, dt_left[:, None], dt_right[:, None], dt_left_root[:, None], dt_right_root[:, None]
    )
    out_update, out_left_new, out_right_new = kron_tiles(
        out_grad, out_left, out_right, out_left_root, out_right_root, 0, 1
    )
    vector_moment_new = 0.5 * vector_moment + 0.5 * vector_grad * vector_grad
    vector_update = -LR_VEC * vector_grad * lax.rsqrt(vector_moment_new)
    return (
        block_output,
        input_grad,
        in_grad,
        dt_grad,
        out_grad,
        in_update,
        dt_update,
        out_update,
        in_left_new,
        in_right_new,
        dt_left_wide[:, 0],
        dt_right_wide[:, 0],
        out_left_new,
        out_right_new,
        vector_grad,
        vector_moment_new,
        vector_update,
    )


def solution(mesh):
    dp, seq = mesh.shape["dp"], mesh.shape["seq"]
    split = (4, dp // 8, 2)
    torus = jax.sharding.Mesh(mesh.devices.reshape(split + (seq,)), AXES + ("seq",))
    tokens = P(AXES, "seq", None)
    rows = P(AXES, None)
    tri = P(AXES, None, None)
    quad = P(AXES, None, None, None)
    placed = (
        (tokens, tokens, rows, rows, rows) + (P(),) * 7 + (quad,) * 4 + (tri,) * 4 + (quad,) * 4 + (P(),)
    )

    return jax.shard_map(
        body,
        mesh=torus,
        in_specs=placed,
        out_specs=(tokens, tokens)
        + (rows,) * 6
        + (quad, quad, tri, tri, quad, quad)
        + (P(), P(), P()),
        check_vma=False,
    )
```

```python
import functools

import jax
import jax.numpy as jnp
from jax import lax
from jax.experimental import pallas as pl
from jax.experimental.pallas import tpu as pltpu
from jax.sharding import PartitionSpec as P


D = 768
HEADS = 24
HEADDIM = 64
DSTATE = 128
KCONV = 4
DI = 1536
CONVCH = 1792
WIDE = CONVCH + 128
ROW_BLOCK = 24
COL_BLOCK = 128

BL = 128
PAIRS = HEADS // 2

AXES = ("z", "x", "core")

EPS = 1e-05
LR = 0.25
LR_VEC = 0.02
NEG = -1e30
LOG2E = 1.4426950408889634
BF = jnp.bfloat16
F32 = jnp.float32
NN = (((1,), (0,)), ((), ()))
NT = (((1,), (1,)), ((), ()))
TN = (((0,), (0,)), ((), ()))


def dot(a, b, dims=NN):
    return lax.dot_general(a, b, dims, preferred_element_type=F32)


def split2(v):
    high = v.astype(BF)
    return high, (v - high.astype(F32)).astype(BF)


def dot3(a, b, dims=NN):
    ah, al = split2(a)
    bh, bl = split2(b)
    return dot(ah, bh, dims) + dot(al, bh, dims) + dot(ah, bl, dims)


def pack(v):
    high = v.astype(BF).astype(F32)
    rest = v - high
    mid = rest.astype(BF).astype(F32)
    low = rest - mid
    return (high + pltpu.roll(mid, 32, 1) + pltpu.roll(low, 64, 1)).astype(BF)


def head_lanes(shape):
    return lax.broadcasted_iota(jnp.int32, shape, 1) < HEADS


def prefix(tri, v):
    parts = dot(tri, pack(v))
    total = parts + pltpu.roll(parts, 96, 1) + pltpu.roll(parts, 64, 1)
    return jnp.where(head_lanes(total.shape), total, 0.0)


def expand(v, emat):
    return dot(pack(v), emat)


def head_sum(v, gather):
    high, low = split2(v)
    return dot(high, gather) + dot(low, gather)


def tri_mask(lower):
    rows = lax.broadcasted_iota(jnp.int32, (BL, BL), 0)
    cols = lax.broadcasted_iota(jnp.int32, (BL, BL), 1)
    return (rows >= cols) if lower else (cols >= rows)


def softplus(v):
    return jnp.maximum(v, 0.0) + jnp.log1p(jnp.exp(-jnp.abs(v)))


def sigmoid(v):
    return 0.5 * jnp.tanh(0.5 * v) + 0.5


def silu(v):
    half = 0.5 * v
    return half * jnp.tanh(half) + half


def silu_parts(v):
    half = 0.5 * v
    curve = jnp.tanh(half)
    return half * curve + half, 0.5 * curve + 0.5


def rates(alog_ref):
    rate = -jnp.exp(alog_ref[0:1, :])
    return jnp.where(head_lanes(rate.shape), rate, 0.0)


def pair_masks():
    left = lax.broadcasted_iota(jnp.int32, (BL, BL), 1) < HEADDIM
    first = jnp.where(left, 1.0, 0.0)
    return first.astype(BF), (1.0 - first).astype(BF)


def pair_blocks(v, masks):
    return jnp.concatenate([v * masks[0], v * masks[1]], axis=0)


def norm_rows(u, gain):
    inv = lax.rsqrt(jnp.mean(u * u, axis=-1, keepdims=True) + EPS)
    return u * inv * gain


def first_kernel(
    u_ref, halo_ref, gain_ref, w_ref, cw_ref, cb_ref, dtb_ref, alog_ref, emat_ref,
    normed_ref, mixed_ref, pre_ref, z_ref, state_ref, total_ref,
    tail, full,
):
    step_index = pl.program_id(1)
    tile = u_ref.shape[1]
    gain = gain_ref[0:1, :]

    @pl.when(step_index == 0)
    def _():
        near = norm_rows(halo_ref[0].astype(F32), gain).astype(BF)
        tail[...] = dot(near, w_ref[:, :CONVCH]).astype(BF).astype(F32)
        state_ref[...] = jnp.zeros_like(state_ref)
        total_ref[...] = jnp.zeros_like(total_ref)

    normed = norm_rows(u_ref[0].astype(F32), gain).astype(BF)
    normed_ref[0] = normed
    projected = dot(normed, w_ref[...])
    mixed_low = projected[:, :CONVCH].astype(BF)
    mixed_ref[0] = mixed_low
    mixed = mixed_low.astype(F32)
    z = projected[:, CONVCH:].astype(BF).astype(F32) + dtb_ref[0:1, :]
    z_ref[0] = z
    for low in range(0, CONVCH, 256):
        cols = slice(low, low + 256)
        own = mixed[:, cols]
        joined = jnp.concatenate([tail[:, cols], own], axis=0)
        pre = cb_ref[0:1, cols] + cw_ref[KCONV - 1 : KCONV, cols] * own
        for tap in range(KCONV - 1):
            moved = pltpu.roll(joined, KCONV - 1 - tap, 0)[8:, :]
            pre = pre + cw_ref[tap : tap + 1, cols] * moved
        pre_ref[0, :, cols] = pre
        full[:, cols] = silu(pre)
    tail[...] = mixed[tile - 8 :, :]
    rate = rates(alog_ref)

    step_all = softplus(z)
    tri = jnp.where(tri_mask(True), 1.0, 0.0).astype(BF)
    emat = emat_ref[...]
    for part in range(tile // BL):
        rows = slice(part * BL, (part + 1) * BL)
        step = step_all[rows]
        cum = prefix(tri, step * rate)
        last = cum[BL - 1 : BL, :]
        weights = expand(jnp.exp(last - cum) * step, emat)
        decay = expand(
            jnp.where(head_lanes((8, 128)), jnp.broadcast_to(jnp.exp(last), (8, 128)), 0.0), emat
        )[0:1, :]
        fresh = dot3(full[rows, DI : DI + DSTATE].T, weights * full[rows, :DI])
        state_ref[0] = state_ref[0] * decay + fresh
        total_ref[0] = total_ref[0] + jnp.broadcast_to(last, (8, 128))


def dot_wide(ahl, ah, bh, bl):
    return dot(ahl, jnp.concatenate([bh, bh], axis=0)) + dot(ah, bl)


def dot3_split(a, b, dims):
    (ah, al), (bh, bl) = a, b
    return dot(ah, bh, dims) + dot(al, bh, dims) + dot(ah, bl, dims)


def wide_split(v):
    high, low = split2(v)
    return jnp.concatenate([high, low], axis=1), high


def rows8(v):
    return jnp.sum(v.reshape(v.shape[0] // 8, 8, v.shape[1]), axis=0)


def pair_values(pair, cum, cum_t, step, mask, left, transposed):
    kernels, columns = [], []
    for h in (2 * pair, 2 * pair + 1):
        column = jnp.broadcast_to(cum[:, h : h + 1], (BL, BL))
        row = cum_t[h : h + 1, :]
        spread = (row - column) if transposed else (column - row)
        kernels.append(jnp.exp2(jnp.where(mask, spread, NEG)))
        columns.append(column)
    chosen = jnp.where(left, columns[0], columns[1])
    steps = jnp.where(left, step[:, 2 * pair : 2 * pair + 1], step[:, 2 * pair + 1 : 2 * pair + 2])
    return kernels, chosen, steps


def lane_sum(v):
    return jnp.sum(v, axis=1, keepdims=True)


def second_kernel(
    pre_ref, z_ref, normed_ref, up_ref, u_ref, enter_ref, wg_ref, wo_ref, skip_ref, ggain_ref, alog_ref,
    gmat_ref,
    out_ref, branch_ref, dy_ref, ggrad_ref, state_ref, rdot_ref, dstate_ref, sums_ref,
    gain_acc, skip_acc, state, running, ys, es, xs_ref, ss_ref, sl_ref, sg_ref, up_scratch,
):
    step_index = pl.program_id(1)
    tile = pre_ref.shape[1]

    @pl.when(step_index == 0)
    def _():
        state[...] = enter_ref[0]
        running[...] = jnp.ones_like(running)
        dstate_ref[...] = jnp.zeros_like(dstate_ref)

    @pl.when((step_index == 0) & (pl.program_id(0) == 0))
    def _():
        gain_acc[...] = jnp.zeros_like(gain_acc)
        skip_acc[...] = jnp.zeros_like(skip_acc)

    rate = rates(alog_ref)

    def block(part, carry):
        rows = pl.ds(pl.multiple_of(part * BL, BL), BL)
        mask = tri_mask(True)
        left = lax.broadcasted_iota(jnp.int32, (BL, BL), 1) < HEADDIM
        masks = pair_masks()
        tri = jnp.where(mask, 1.0, 0.0).astype(BF)
        conv = silu(pre_ref[0, rows, DI:])
        inputs_b, inputs_c = conv[:, :DSTATE], conv[:, DSTATE:]
        step = softplus(z_ref[0, rows, :])
        cum = prefix(tri, step * (rate * LOG2E))
        cum_t = cum.T
        scores = dot3(inputs_c, inputs_b, NT)
        c_wide, c_high = wide_split(inputs_c)
        bt_wide, bt_high = wide_split(inputs_b.T)
        ct_wide, ct_high = wide_split(inputs_c.T)
        squares = jnp.zeros((BL, 128), F32)
        products = jnp.zeros((BL, 128), F32)
        for quad in range(PAIRS // 2):
            cols = slice(quad * 256, (quad + 1) * 256)
            inner, grown, weighted, xs = [], [], [], []
            for pair in (2 * quad, 2 * quad + 1):
                kernels, chosen, steps = pair_values(pair, cum, cum_t, step, mask, left, False)
                x = silu(pre_ref[0, rows, pair * 128 : (pair + 1) * 128])
                scaled = steps * x
                mh, ml = split2(jnp.concatenate([scores * k for k in kernels], axis=1))
                rh, rl = (pair_blocks(v, masks) for v in split2(scaled))
                inner.append(dot(mh, rh) + dot(ml, rh) + dot(mh, rl))
                grown.append(jnp.exp2(chosen))
                weighted.append(jnp.exp2(chosen[BL - 1 : BL, :] - chosen) * scaled)
                xs.append(x)
            inner, grown, weighted, x = (
                jnp.concatenate(v, axis=1) for v in (inner, grown, weighted, xs)
            )
            held = state[:, cols]
            state_ref[0, part, :, cols] = held
            yhat = inner + grown * dot_wide(c_wide, c_high, *split2(held))
            state[:, cols] = held * grown[BL - 1 : BL, :] + dot_wide(
                bt_wide, bt_high, *split2(weighted)
            )
            ys[:, cols] = yhat
            es[:, cols] = grown
            states = (yhat + skip_ref[0:1, cols] * x).astype(BF).astype(F32)
            sl, sg = silu_parts(dot(normed_ref[0, rows, :], wg_ref[:, cols]))
            upstream = dot(up_ref[rows, :], wo_ref[cols, :], NT)
            up_scratch[:, cols] = upstream
            gated = states * sl
            xs_ref[:, cols] = x
            ss_ref[:, cols] = states
            sl_ref[:, cols] = sl
            sg_ref[:, cols] = sg
            product = gated * (upstream * ggain_ref[0:1, cols])
            squared = gated * gated
            squares = squares + squared[:, :128] + squared[:, 128:]
            products = products + product[:, :128] + product[:, 128:]
        inv = lax.rsqrt(lane_sum(squares) * (1.0 / DI) + EPS)
        pull = jnp.broadcast_to(inv * inv * lane_sum(products) * (1.0 / DI), (BL, 128))
        inv = jnp.broadcast_to(inv, (BL, 128))
        rdot = jnp.zeros((BL, 128), F32)
        for quad in range(PAIRS // 2):
            cols = slice(quad * 256, (quad + 1) * 256)
            scaled_dy, dot_terms = [], []
            for pair in (2 * quad, 2 * quad + 1):
                own_cols = slice(pair * 128, (pair + 1) * 128)
                x = xs_ref[:, own_cols]
                yhat = ys[:, own_cols]
                states = ss_ref[:, own_cols]
                sl, sg = sl_ref[:, own_cols], sg_ref[:, own_cols]
                gated = states * sl
                gain = ggain_ref[0:1, own_cols]
                upstream = up_scratch[:, own_cols]
                norm = gated * inv
                branch_ref[rows, own_cols] = (norm * gain).astype(BF)
                gain_acc[:, own_cols] += rows8(upstream * norm)
                dgated = inv * (upstream * gain - gated * pull)
                dy_low = (dgated * sl).astype(BF)
                dy_ref[rows, own_cols] = dy_low
                ggrad_ref[rows, own_cols] = (dgated * states * (sg + sl * (1.0 - sg))).astype(BF)
                dy = dy_low.astype(F32)
                skip_acc[:, own_cols] += rows8(dy * x)
                dot_terms.append(dy * yhat)
                scaled_dy.append(es[:, own_cols] * running[0:1, own_cols] * dy)
            rdot = rdot + head_sum(jnp.concatenate(dot_terms, axis=1), gmat_ref[cols, :])
            dstate_ref[0, :, cols] += dot_wide(
                ct_wide, ct_high, *split2(jnp.concatenate(scaled_dy, axis=1))
            )
            running[:, cols] = running[:, cols] * es[BL - 1 : BL, cols]
        rdot_ref[0, rows, :] = rdot
        return carry

    lax.fori_loop(0, tile // BL, block, 0)
    out_ref[0] = (u_ref[0].astype(F32) + dot(branch_ref[...], wo_ref[...])).astype(BF)

    @pl.when((step_index == pl.num_programs(1) - 1) & (pl.program_id(0) == pl.num_programs(0) - 1))
    def _():
        sums_ref[0:1, :] = jnp.sum(gain_acc[...], axis=0, keepdims=True)
        sums_ref[1:2, :] = jnp.sum(skip_acc[...], axis=0, keepdims=True)


def third_kernel(
    pre_ref, mixed_ref, z_ref, dy_ref, state_ref, rdot_ref, leave_ref, cw_ref, skip_ref, alog_ref,
    gmat_ref,
    mgrad_ref, last_ref, first_ref, sums_ref,
    cw_acc, cb_acc, dtb_acc, rate_acc, dstate, tail,
):
    step_index = pl.program_id(1)

    @pl.when(step_index == 0)
    def _():
        dstate[...] = leave_ref[0]
        tail[...] = jnp.zeros_like(tail)

    @pl.when((step_index == 0) & (pl.program_id(0) == 0))
    def _():
        for ref in (cw_acc, cb_acc, dtb_acc, rate_acc):
            ref[...] = jnp.zeros_like(ref)

    rate = rates(alog_ref)
    mask = tri_mask(False)
    left = lax.broadcasted_iota(jnp.int32, (BL, BL), 1) < HEADDIM
    masks = pair_masks()
    low_tri = jnp.where(tri_mask(True), 1.0, 0.0).astype(BF)
    high_tri = jnp.where(mask, 1.0, 0.0).astype(BF)
    wide_pre = pre_ref[0, :, DI:]
    conv, wide_sg = silu_parts(wide_pre)
    inputs_b, inputs_c = conv[:, :DSTATE], conv[:, DSTATE:]
    z = z_ref[0]
    step = softplus(z)
    cum = prefix(low_tri, step * (rate * LOG2E))
    cum_t = cum.T
    lanes = head_lanes(cum.shape)
    scores_t = dot3(inputs_b, inputs_c, NT)
    b_wide, b_high = wide_split(inputs_b)
    ct_wide, ct_high = wide_split(inputs_c.T)
    dscores_t = jnp.zeros((BL, BL), F32)
    db = jnp.zeros((BL, DSTATE), F32)
    dc = jnp.zeros((BL, DSTATE), F32)
    sums = jnp.zeros((BL + 8, 128), F32)

    def back_conv(cols, dpre):
        joined = jnp.concatenate([dpre, tail[:, cols]], axis=0)
        tail[:, cols] = dpre[0:8, :]
        mixed = mixed_ref[0, :, cols].astype(F32)
        cb_acc[:, cols] += rows8(dpre)
        mgrad = cw_ref[KCONV - 1 : KCONV, cols] * dpre
        cw_acc[KCONV - 1, :, cols] += rows8(dpre * mixed)
        for tap in range(KCONV - 1):
            moved = pltpu.roll(joined, BL + 8 - (KCONV - 1 - tap), 0)[:BL, :]
            mgrad = mgrad + cw_ref[tap : tap + 1, cols] * moved
            cw_acc[tap, :, cols] += rows8(moved * mixed)
        mgrad_ref[0, :, cols] = mgrad.astype(BF)
        last_ref[0, :, cols] = jnp.where(step_index == 0, mgrad[BL - 8 :, :], last_ref[0, :, cols])

    for quad in range(PAIRS // 2):
        cols = slice(quad * 256, (quad + 1) * 256)
        inner, grown, shrink, scaled, xs, steps_wide, slopes = [], [], [], [], [], [], []
        dy = dy_ref[:, cols].astype(F32)
        for pair in (2 * quad, 2 * quad + 1):
            kernels, chosen, steps = pair_values(pair, cum, cum_t, step, mask, left, True)
            own = pre_ref[0, :, pair * 128 : (pair + 1) * 128]
            x, sg = silu_parts(own)
            slopes.append(sg + x * (1.0 - sg))
            xd = steps * x
            mh, ml = split2(jnp.concatenate([scores_t * k for k in kernels], axis=1))
            dyb = pair_blocks(dy_ref[:, pair * 128 : (pair + 1) * 128], masks)
            inner.append(dot(mh, dyb) + dot(ml, dyb))
            sh, sl = split2(xd)
            dmix = dot(sh, dyb, NT) + dot(sl, dyb, NT)
            dscores_t = dscores_t + dmix[:, :BL] * kernels[0] + dmix[:, BL:] * kernels[1]
            grown.append(jnp.exp2(chosen))
            shrink.append(jnp.exp2(chosen[BL - 1 : BL, :] - chosen))
            scaled.append(xd)
            xs.append(x)
            steps_wide.append(steps)
        inner, grown, shrink, scaled, x, steps_wide, slopes = (
            jnp.concatenate(v, axis=1) for v in (inner, grown, shrink, scaled, xs, steps_wide, slopes)
        )
        held = state_ref[0, 0, :, cols]
        ds = dstate[:, cols]
        held_parts, ds_parts = split2(held), split2(ds)
        decay = grown[BL - 1 : BL, :]
        dscaled_state = shrink * dot_wide(b_wide, b_high, *ds_parts)
        dscaled = inner + dscaled_state
        ends = jnp.sum(scaled * dscaled_state, axis=0, keepdims=True) + decay * jnp.sum(
            held * ds, axis=0, keepdims=True
        )
        sums = sums + head_sum(
            jnp.concatenate([x * dscaled, jnp.broadcast_to(ends, (8, 256))], axis=0),
            gmat_ref[cols, :],
        )
        grown_parts = split2(grown * dy)
        dc = dc + dot3_split(grown_parts, held_parts, NT)
        db = db + dot3_split(split2(shrink * scaled), ds_parts, NT)
        dstate[:, cols] = decay * ds + dot_wide(ct_wide, ct_high, *grown_parts)
        back_conv(cols, (steps_wide * dscaled + skip_ref[0:1, cols] * dy) * slopes)

    direct = sums[:BL]
    is_last = lax.broadcasted_iota(jnp.int32, (BL, 128), 0) == BL - 1
    dcum = rdot_ref[0] - step * direct + jnp.where(is_last, sums[BL : BL + 1, :], 0.0)
    dcum = jnp.where(lanes, dcum, 0.0)
    drate = prefix(high_tri, dcum)
    dz = (rate * drate + direct) * sigmoid(z)
    mgrad_ref[0, :, CONVCH:] = dz.astype(BF)
    dtb_acc[...] += rows8(dz)
    rate_acc[...] += rows8(step * drate)
    db = db + dot3(dscores_t, inputs_c)
    dc = dc + dot3(dscores_t.T, inputs_b)
    back_conv(
        slice(DI, CONVCH),
        jnp.concatenate([db, dc], axis=1) * (wide_sg + conv * (1.0 - wide_sg)),
    )
    first_ref[0] = tail[...]

    @pl.when((step_index == pl.num_programs(1) - 1) & (pl.program_id(0) == pl.num_programs(0) - 1))
    def _():
        for tap in range(KCONV):
            sums_ref[tap : tap + 1, :] = jnp.sum(cw_acc[tap], axis=0, keepdims=True)
        sums_ref[4:5, :] = jnp.sum(cb_acc[...], axis=0, keepdims=True)
        sums_ref[5:6, :128] = jnp.sum(dtb_acc[...], axis=0, keepdims=True)
        sums_ref[6:7, :128] = jnp.sum(rate_acc[...], axis=0, keepdims=True)


def patch_kernel(mgrad_ref, mixed_ref, last_ref, near_ref, cw_ref, out_ref, extra_ref):
    @pl.when(pl.program_id(0) == 0)
    def _():
        extra_ref[...] = jnp.zeros_like(extra_ref)

    rows = [last_ref[0, i : i + 1, :] for i in range(8)]
    near = [near_ref[0, i : i + 1, :] for i in range(KCONV - 1)]
    held = mixed_ref[0].astype(F32)
    first = 8 - (KCONV - 1)
    for k in range(KCONV - 1):
        for j in range(k, KCONV - 1):
            rows[first + j] = rows[first + j] + cw_ref[k : k + 1, :] * near[j - k]
            extra_ref[k : k + 1, :] += near[j - k] * held[8 + first + j : 9 + first + j, :]
    old = mgrad_ref[0].astype(F32)
    patched = jnp.concatenate([old[:8, :CONVCH], jnp.concatenate(rows, axis=0)], axis=0)
    out_ref[0, :, :CONVCH] = patched.astype(BF)
    out_ref[0, :, CONVCH:] = mgrad_ref[0, :, CONVCH:]


PARAMS = dict(vmem_limit_bytes=60 * 1024 * 1024)


def whole(shape):
    zeros = (0,) * len(shape)
    return pl.BlockSpec(shape, lambda b, i: zeros)


def run_first(u, halo, gain, w, cw, cb, dtb, alog, emat):
    seqs, length, _ = u.shape
    tile = min(256, length)
    grid = (seqs, length // tile)
    tok = lambda width: pl.BlockSpec((1, tile, width), lambda b, i: (b, i, 0))
    per = lambda *shape: pl.BlockSpec((1,) + shape, lambda b, i: (b,) + (0,) * len(shape))
    return pl.pallas_call(
        first_kernel,
        grid=grid,
        in_specs=[
            tok(D), per(8, D), whole(gain.shape), whole(w.shape),
            whole(cw.shape), whole(cb.shape), whole(dtb.shape), whole(alog.shape), whole(emat.shape),
        ],
        out_specs=[
            tok(D), tok(CONVCH), tok(CONVCH), tok(128), per(DSTATE, DI), per(8, 128),
        ],
        out_shape=[
            jax.ShapeDtypeStruct((seqs, length, D), BF),
            jax.ShapeDtypeStruct((seqs, length, CONVCH), BF),
            jax.ShapeDtypeStruct((seqs, length, CONVCH), F32),
            jax.ShapeDtypeStruct((seqs, length, 128), F32),
            jax.ShapeDtypeStruct((seqs, DSTATE, DI), F32),
            jax.ShapeDtypeStruct((seqs, 8, 128), F32),
        ],
        scratch_shapes=[pltpu.VMEM((8, CONVCH), F32), pltpu.VMEM((tile, CONVCH), F32)],
        compiler_params=pltpu.CompilerParams(**PARAMS),
        name="first",
    )(u, halo, gain, w, cw, cb, dtb, alog, emat)


def run_second(pre, z, normed, up, u, enter, wg, wo, skip, ggain, alog, gmat):
    seqs, length, _ = u.shape
    tile = min(256, length)
    steps = length // tile
    parts = tile // BL
    grid = (seqs, steps)
    tok = lambda width: pl.BlockSpec((1, tile, width), lambda b, i: (b, i, 0))
    flat = lambda width: pl.BlockSpec((tile, width), lambda b, i: (b * steps + i, 0))
    per = lambda *shape: pl.BlockSpec((1,) + shape, lambda b, i: (b,) + (0,) * len(shape))
    rows = seqs * length
    return pl.pallas_call(
        second_kernel,
        grid=grid,
        in_specs=[
            tok(CONVCH), tok(128), tok(D), flat(D), tok(D), per(DSTATE, DI), whole(wg.shape),
            whole(wo.shape),
            whole(skip.shape), whole(ggain.shape), whole(alog.shape), whole(gmat.shape),
        ],
        out_specs=[
            tok(D), flat(DI), flat(DI), flat(DI),
            pl.BlockSpec((1, parts, DSTATE, DI), lambda b, i: (b, i, 0, 0)),
            tok(128), per(DSTATE, DI), whole((8, DI)),
        ],
        out_shape=[
            jax.ShapeDtypeStruct((seqs, length, D), BF),
            jax.ShapeDtypeStruct((rows, DI), BF),
            jax.ShapeDtypeStruct((rows, DI), BF),
            jax.ShapeDtypeStruct((rows, DI), BF),
            jax.ShapeDtypeStruct((seqs, length // BL, DSTATE, DI), F32),
            jax.ShapeDtypeStruct((seqs, length, 128), F32),
            jax.ShapeDtypeStruct((seqs, DSTATE, DI), F32),
            jax.ShapeDtypeStruct((8, DI), F32),
        ],
        scratch_shapes=[
            pltpu.VMEM((8, DI), F32), pltpu.VMEM((8, DI), F32), pltpu.VMEM((DSTATE, DI), F32),
            pltpu.VMEM((8, DI), F32), *[pltpu.VMEM((BL, DI), F32)] * 7,
        ],
        compiler_params=pltpu.CompilerParams(**PARAMS),
        name="second",
    )(pre, z, normed, up, u, enter, wg, wo, skip, ggain, alog, gmat)


def run_third(pre, mixed, z, dy, states, rdot, leave, cw, skip, alog, gmat):
    seqs, length, _ = pre.shape
    steps = length // BL
    grid = (seqs, steps)
    tok = lambda width: pl.BlockSpec((1, BL, width), lambda b, i: (b, steps - 1 - i, 0))
    per = lambda *shape: pl.BlockSpec((1,) + shape, lambda b, i: (b,) + (0,) * len(shape))
    return pl.pallas_call(
        third_kernel,
        grid=grid,
        in_specs=[
            tok(CONVCH), tok(CONVCH), tok(128),
            pl.BlockSpec((BL, DI), lambda b, i: (b * steps + steps - 1 - i, 0)),
            pl.BlockSpec((1, 1, DSTATE, DI), lambda b, i: (b, steps - 1 - i, 0, 0)),
            tok(128), per(DSTATE, DI), whole(cw.shape), whole(skip.shape), whole(alog.shape),
            whole(gmat.shape),
        ],
        out_specs=[
            tok(WIDE), per(8, CONVCH), per(8, CONVCH), whole((8, CONVCH)),
        ],
        out_shape=[
            jax.ShapeDtypeStruct((seqs, length, WIDE), BF),
            jax.ShapeDtypeStruct((seqs, 8, CONVCH), F32),
            jax.ShapeDtypeStruct((seqs, 8, CONVCH), F32),
            jax.ShapeDtypeStruct((8, CONVCH), F32),
        ],
        scratch_shapes=[
            pltpu.VMEM((KCONV, 8, CONVCH), F32), pltpu.VMEM((8, CONVCH), F32),
            pltpu.VMEM((8, 128), F32), pltpu.VMEM((8, 128), F32),
            pltpu.VMEM((DSTATE, DI), F32), pltpu.VMEM((8, CONVCH), F32),
        ],
        compiler_params=pltpu.CompilerParams(**PARAMS),
        name="third",
    )(pre, mixed, z, dy, states, rdot, leave, cw, skip, alog, gmat)


def run_patch(mgrad, mixed, last8, near, cw):
    seqs, length, _ = mgrad.shape
    end = length // 16 - 1
    tok = lambda width: pl.BlockSpec((1, 16, width), lambda b: (b, end, 0))
    per = pl.BlockSpec((1, 8, CONVCH), lambda b: (b, 0, 0))
    row = pl.BlockSpec((8, CONVCH), lambda b: (0, 0))
    taps = pl.BlockSpec(cw.shape, lambda b: (0, 0))
    return pl.pallas_call(
        patch_kernel,
        grid=(seqs,),
        in_specs=[tok(WIDE), tok(CONVCH), per, per, taps],
        out_specs=[tok(WIDE), row],
        out_shape=[
            jax.ShapeDtypeStruct(mgrad.shape, BF),
            jax.ShapeDtypeStruct((8, CONVCH), F32),
        ],
        input_output_aliases={0: 0},
        name="patch",
    )(mgrad, mixed, last8, near, cw)


def kron_update(gradient, left_stat, right_stat, left_root, right_root):
    row_tiles, col_tiles = (left_stat.shape[0], left_stat.shape[1])
    row_size, col_size = (left_stat.shape[-1], right_stat.shape[-1])
    grad_tiles = gradient.reshape(row_tiles, row_size, col_tiles, col_size).transpose(0, 2, 1, 3)
    left_new = 0.5 * left_stat + 0.5 * jnp.einsum(
        "abij,abkj->abik", grad_tiles, grad_tiles, precision=lax.Precision.HIGH
    )
    right_new = 0.5 * right_stat + 0.5 * jnp.einsum(
        "abji,abjk->abik", grad_tiles, grad_tiles, precision=lax.Precision.HIGH
    )
    shaped = jnp.einsum("abij,abjk->abik", left_root, grad_tiles, precision=lax.Precision.HIGH)
    shaped = jnp.einsum("abij,abjk->abik", shaped, right_root, precision=lax.Precision.HIGH)
    update = (-LR * shaped).transpose(0, 2, 1, 3).reshape(gradient.shape)
    return (update, left_new, right_new)


def float_parts(v):
    high = v.astype(BF).astype(F32)
    return high, v - high


def kron_kernel(*refs):
    grad_ref, left_ref, right_ref, left_root_ref, right_root_ref = refs[:5]
    update_ref, left_new_ref, right_new_ref = refs[-3:]
    for r in range(left_ref.shape[0]):
        rows = slice(r * ROW_BLOCK, (r + 1) * ROW_BLOCK)
        for c in range(left_ref.shape[1]):
            cols = slice(c * COL_BLOCK, (c + 1) * COL_BLOCK)
            grad = grad_ref[rows, cols]
            high, low = float_parts(grad)
            root_high, root_low = float_parts(left_root_ref[r, c])
            below = jnp.concatenate([high, high, low], axis=0).astype(BF)
            right = dot(jnp.concatenate([high, low, high], axis=0).astype(BF), below, TN)
            rooted = dot(
                jnp.concatenate([root_high, root_low, root_high], axis=0).astype(BF), below, TN
            )
            high, low = high.astype(BF), low.astype(BF)
            left = dot(
                jnp.concatenate([high, low], axis=1), jnp.concatenate([high, high], axis=1), NT
            ) + dot(high, low, NT)
            left_new_ref[r, c] = 0.5 * left_ref[r, c] + 0.5 * left
            right_new_ref[r, c] = 0.5 * right_ref[r, c] + 0.5 * right
            shaped = dot_wide(*wide_split(rooted), *split2(right_root_ref[r, c]))
            update_ref[rows, cols] = -LR * shaped


def kron_tiles(grad, left, right, left_root, right_root, first, step, earlier=None):
    row_tiles = left.shape[0]
    rows, cols = grad.shape
    base = first // step
    stat = lambda size: pl.BlockSpec(
        (row_tiles, step, size, size), lambda i: (0, base + i, 0, 0)
    )
    wide = step * COL_BLOCK
    ins = [grad, left, right, left_root, right_root]
    in_specs = [pl.BlockSpec((rows, wide), lambda i: (0, i))] + [stat(ROW_BLOCK), stat(COL_BLOCK)] * 2
    aliases = {}
    if earlier is not None:
        ins += list(earlier)
        in_specs += [pl.BlockSpec(memory_space=pl.ANY)] * 3
        aliases = {5: 0, 6: 1, 7: 2}
    total = left.shape[1] * COL_BLOCK
    return pl.pallas_call(
        kron_kernel,
        grid=(cols // wide,),
        in_specs=in_specs,
        out_specs=[
            pl.BlockSpec((rows, wide), lambda i: (0, base + i)), stat(ROW_BLOCK), stat(COL_BLOCK),
        ],
        out_shape=[
            jax.ShapeDtypeStruct((rows, total), F32),
            jax.ShapeDtypeStruct(left.shape, F32),
            jax.ShapeDtypeStruct(right.shape, F32),
        ],
        input_output_aliases=aliases,
        compiler_params=pltpu.CompilerParams(**PARAMS),
        name="kron",
    )(*ins)


def back_kernel(
    ggrad_ref, mgrad_ref, wg_ref, main_ref, u_ref, up_ref, gain_ref, out_ref, gain_grad_ref
):
    @pl.when(pl.program_id(0) == 0)
    def _():
        gain_grad_ref[...] = jnp.zeros_like(gain_grad_ref)

    grad = dot(ggrad_ref[...], wg_ref[...], NT) + dot(mgrad_ref[...], main_ref[...], NT)
    u = u_ref[...].astype(F32)
    inv = lax.rsqrt(jnp.mean(u * u, axis=-1, keepdims=True) + EPS)
    norm = u * inv
    gain_grad_ref[...] += rows8(grad * norm)
    scaled = grad * gain_ref[0:1, :]
    pull = jnp.mean(scaled * norm, axis=-1, keepdims=True)
    out_ref[...] = up_ref[...].astype(F32) + inv * (scaled - norm * pull)


def run_back(ggrad, mgrad, wg, main, u, up, gain):
    rows = u.shape[0]
    tile = min(256, rows)
    tok = lambda width: pl.BlockSpec((tile, width), lambda i: (i, 0))
    return pl.pallas_call(
        back_kernel,
        grid=(rows // tile,),
        in_specs=[
            tok(DI), tok(WIDE), pl.BlockSpec(wg.shape, lambda i: (0, 0)),
            pl.BlockSpec(main.shape, lambda i: (0, 0)), tok(D), tok(D),
            pl.BlockSpec(gain.shape, lambda i: (0, 0)),
        ],
        out_specs=[tok(D), pl.BlockSpec((8, D), lambda i: (0, 0))],
        out_shape=[jax.ShapeDtypeStruct((rows, D), F32), jax.ShapeDtypeStruct((8, D), F32)],
        compiler_params=pltpu.CompilerParams(**PARAMS),
        name="back",
    )(ggrad, mgrad, wg, main, u, up, gain)


def swapped(v, axis, size, offset):
    return lax.ppermute(v, axis, [(i, (i + offset) % size) for i in range(size)])


def pick(v, index):
    return lax.dynamic_index_in_dim(v, index, 0, keepdims=False)


def scatter_stage(v, axis, kind=BF):
    size = lax.axis_size(axis)
    here = lax.axis_index(axis)
    total = pick(v, here)
    for offset in range(1, size):
        sent = pick(v, lax.rem(here + offset, size)).astype(kind)
        total = total + swapped(sent, axis, size, offset).astype(F32)
    return total


def gather_stage(v, axis):
    size = lax.axis_size(axis)
    here = lax.axis_index(axis)
    out = jnp.zeros((size,) + v.shape, v.dtype)
    out = lax.dynamic_update_index_in_dim(out, v, here, 0)
    for offset in range(1, size):
        got = swapped(v, axis, size, offset)
        out = lax.dynamic_update_index_in_dim(out, got, lax.rem(here - offset + size, size), 0)
    return out


def core_sum(partial):
    z, x, core = (lax.axis_size(a) for a in ("z", "x", "core"))
    rows, cols = partial.shape
    blocks = partial.reshape(z, x, core, rows // (z * x * core), cols)
    return scatter_stage(jnp.moveaxis(blocks, 2, 0), "core", F32)


def across(v):
    return scatter_stage(scatter_stage(jnp.moveaxis(v, 1, 0), "x"), "z")


def reduce_plain(v):
    owned = across(v)
    total = owned
    size = lax.axis_size("seq")
    if size > 2:
        return lax.psum(owned, "seq")
    for offset in range(1, size):
        total = total + swapped(owned, "seq", size, offset)
    return total


def reduce_split(v):
    size = lax.axis_size("seq")
    z, x, rows, cols = v.shape
    if cols % (128 * size):
        return reduce_plain(v)
    v = jnp.moveaxis(v.reshape(z, x, rows, size, cols // size), 3, 0)
    owned = across(scatter_stage(v, "seq"))
    return jnp.moveaxis(gather_stage(owned, "seq"), 0, 1).reshape(rows, cols)


def xor_sum(v, axis):
    size = lax.axis_size(axis)
    bit = 1
    while bit < size:
        v = v + lax.ppermute(v, axis, [(i, i ^ bit) for i in range(size)])
        bit *= 2
    return v


STEP_OWNERS = 4


def chip_kernel(idx, *refs):
    send_ref, own_ref = refs[-2:]
    width = own_ref.shape[1]
    for owner in range(STEP_OWNERS):
        mine = pl.program_id(0) * STEP_OWNERS + owner == idx[0] * 2 + idx[1]
        row, col = 0, 0
        for part_ref, got_ref in zip(refs[:-2:2], refs[1:-2:2]):
            total = part_ref[owner, 0] + got_ref[owner]
            rows = total.shape[0] * total.shape[1] // width
            for low in range(0, total.shape[0], rows):
                piece = total[low : low + rows]
                at = (slice(row, row + rows), slice(col, col + piece.shape[1]))
                send_ref[(owner,) + at] = piece.astype(BF)

                @pl.when(mine)
                def _(at=at, piece=piece):
                    own_ref[at] = piece

                col += piece.shape[1]
                if col == width:
                    row, col = row + rows, 0


def chip_sum(idx, pairs):
    in_specs, ins, total, width = [], [], 0, 0
    for blocks, got in pairs:
        _, _, rows, cols = blocks.shape
        width = max(width, cols)
        total += rows * cols
        ins += [blocks, got]
        in_specs += [
            pl.BlockSpec((STEP_OWNERS, 1, rows, cols), lambda i, idx: (i, idx[2], 0, 0)),
            pl.BlockSpec((STEP_OWNERS, rows, cols), lambda i, idx: (i, 0, 0)),
        ]
    rows = total // width
    return pl.pallas_call(
        chip_kernel,
        grid_spec=pltpu.PrefetchScalarGridSpec(
            num_scalar_prefetch=1,
            grid=(8 // STEP_OWNERS,),
            in_specs=in_specs,
            out_specs=[
                pl.BlockSpec((STEP_OWNERS, rows, width), lambda i, idx: (i, 0, 0)),
                pl.BlockSpec((rows, width), lambda i, idx: (0, 0)),
            ],
        ),
        out_shape=[
            jax.ShapeDtypeStruct((8, rows, width), BF),
            jax.ShapeDtypeStruct((rows, width), F32),
        ],
        compiler_params=pltpu.CompilerParams(**PARAMS),
        name="chip_sum",
    )(idx, *ins)


def owner_kernel(idx, own_ref, got_ref, out_ref):
    mine = idx[0] * 2 + idx[1]
    total = own_ref[...]
    for i in range(8):
        total = total + jnp.where(mine == i, 0.0, got_ref[i].astype(F32))
    out_ref[...] = total


def owner_sum(idx, own, got):
    rows, width = own.shape
    tile = 48
    return pl.pallas_call(
        owner_kernel,
        grid_spec=pltpu.PrefetchScalarGridSpec(
            num_scalar_prefetch=1,
            grid=(rows // tile,),
            in_specs=[
                pl.BlockSpec((tile, width), lambda i, idx: (i, 0)),
                pl.BlockSpec((8, tile, width), lambda i, idx: (0, i, 0)),
            ],
            out_specs=pl.BlockSpec((tile, width), lambda i, idx: (i, 0)),
        ),
        out_shape=jax.ShapeDtypeStruct((rows, width), F32),
        name="owner_sum",
    )(idx, own, got)


def core_exchange(partial, core):
    rows, cols = partial.shape
    blocks = partial.reshape(8, 2, rows // 16, cols)
    sent = lax.dynamic_index_in_dim(blocks, 1 - core, 1, keepdims=False)
    return blocks, swapped(sent, "core", 2, 1)


def around(v, axis):
    size = lax.axis_size(axis)
    return jnp.stack([v] + [swapped(v, axis, size, offset) for offset in range(1, size)])


def assemble_kernel(idx, *refs, order):
    out_ref = refs[-1]
    sizes = {"z": 4, "x": 2}
    here = {"z": idx[0], "x": idx[1]}
    spots = ((idx[2], idx[3]), (idx[2], 1 - idx[3]), (1 - idx[2], idx[3]), (1 - idx[2], 1 - idx[3]))
    for ref, (core, seq) in zip(refs[:-1], spots):
        for a in range(ref.shape[0]):
            for b in range(ref.shape[1]):
                at = dict(
                    (axis, lax.rem(here[axis] - back + sizes[axis], sizes[axis]))
                    for axis, back in zip(order[::-1], (a, b))
                )
                out_ref[((at["z"] * 2 + at["x"]) * 2 + core) * 2 + seq] = ref[a, b]


def assemble(idx, pieces, order):
    shape = pieces[0].shape
    rows, cols = shape[-2:]
    out = pl.pallas_call(
        functools.partial(assemble_kernel, order=order),
        grid_spec=pltpu.PrefetchScalarGridSpec(
            num_scalar_prefetch=1,
            grid=(1,),
            in_specs=[pl.BlockSpec(shape, lambda i, idx: (0,) * 4)] * 4,
            out_specs=pl.BlockSpec((32, rows, cols), lambda i, idx: (0, 0, 0)),
        ),
        out_shape=jax.ShapeDtypeStruct((32, rows, cols), pieces[0].dtype),
        compiler_params=pltpu.CompilerParams(**PARAMS),
        name="assemble",
    )(idx, *pieces)
    return out.reshape(32 * rows, cols)


def body(
    block_input,
    cotangent,
    in_weight,
    dt_weight,
    out_weight,
    norm_gain,
    conv_weight,
    conv_bias,
    dt_bias,
    decay_log,
    skip_gain,
    gate_gain,
    in_left,
    in_right,
    in_left_root,
    in_right_root,
    dt_left,
    dt_right,
    dt_left_root,
    dt_right_root,
    out_left,
    out_right,
    out_left_root,
    out_right_root,
    vector_moment,
):
    seq_count, local_len, _ = block_input.shape
    seq_devices = lax.axis_size("seq")
    row_count = seq_count * local_len
    up = [(i, i + 1) for i in range(seq_devices - 1)]
    down = [(i + 1, i) for i in range(seq_devices - 1)]

    in_low = in_weight.astype(BF)
    dt_low = jnp.pad(dt_weight.astype(BF), ((0, 0), (0, 128 - HEADS)))
    main = lax.all_gather(
        jnp.concatenate([in_low[:, DI:], dt_low], axis=1), AXES, axis=0, tiled=True
    )
    part = jnp.arange(128)
    channel = jnp.arange(DI)
    emat = (
        ((part[:, None] % 32) == (channel[None, :] // HEADDIM)) & (part[:, None] < 96)
    ).astype(BF)
    gmat = ((channel[:, None] // HEADDIM) == part[None, :]).astype(BF)
    skip_wide = jnp.repeat(skip_gain, HEADDIM).reshape(1, DI)
    alog = jnp.pad(decay_log, (0, 128 - HEADS)).reshape(1, 128)
    dtb = jnp.pad(dt_bias, (0, 128 - HEADS), constant_values=-1e4).reshape(1, 128)
    cw8 = conv_weight
    gain8, cb8 = norm_gain.reshape(1, D), conv_bias.reshape(1, CONVCH)
    ggain8 = gate_gain.reshape(1, DI)
    tables = (emat, gmat, skip_wide, alog, dtb, cw8, gain8, cb8, ggain8)
    torus_sizes = tuple(lax.axis_size(a) for a in ("z", "x", "core", "seq"))
    direct = torus_sizes == (4, 2, 2, 2)
    idx = jnp.stack([lax.axis_index(a) for a in ("z", "x", "core", "seq")]).astype(jnp.int32)
    gate_low, out_low = in_low[:, :DI], out_weight.astype(BF)
    if direct:
        order = ("z", "x")
        gate_near = pick(gate_low.reshape(2, -1, DI), idx[3])
        out_near = pick(out_low.reshape(2, -1, D), idx[3])
        gate_near = around(around(gate_near, "z"), "x")
        out_near = around(around(out_near, "z"), "x")
        main = lax.optimization_barrier((main, gate_near, out_near) + tables)[0]
        gate_got = swapped(gate_near, "seq", 2, 1)
        out_got = swapped(out_near, "seq", 2, 1)
        gate_far = swapped(gate_near, "core", 2, 1)
        out_far = swapped(out_near, "core", 2, 1)
    else:
        wg = lax.all_gather(gate_low, AXES, axis=0, tiled=True)
        wo = lax.all_gather(out_low, AXES, axis=0, tiled=True)
    halo = lax.ppermute(block_input[:, local_len - 8 :, :], "seq", up)

    normed, mixed, pre, z, local_state, total = run_first(
        block_input, halo, gain8, main, cw8, cb8, dtb, alog, emat
    )
    span = jnp.repeat(jnp.exp(total[:, 0:1, :HEADS]), HEADDIM, axis=2)
    enter = lax.ppermute(local_state, "seq", up)
    for _ in range(seq_devices - 2):
        enter = lax.ppermute(local_state + span * enter, "seq", up)

    if direct:
        out_far_got = swapped(out_got, "core", 2, 1)
        gate_far_got = swapped(gate_got, "core", 2, 1)
        wo = assemble(idx, (out_near, out_got, out_far, out_far_got), order)
        wg = assemble(idx, (gate_near, gate_got, gate_far, gate_far_got), order)
    normed_rows = normed.reshape(row_count, D)
    upstream = cotangent.reshape(row_count, D)
    (
        block_output, branch, states_grad, gate_grad, states, rdot, local_dstate, row_sums,
    ) = run_second(
        pre, z, normed, upstream, block_input, enter, wg, wo, skip_wide, ggain8, alog,
        gmat,
    )
    leave = lax.ppermute(local_dstate, "seq", down)
    for _ in range(seq_devices - 2):
        leave = lax.ppermute(local_dstate + span * leave, "seq", down)

    out_partial = dot(branch, upstream, TN)
    gate_partial = dot(normed_rows, gate_grad, TN)
    if direct:
        gate_pair = core_exchange(gate_partial, idx[2])
        out_pair = core_exchange(out_partial, idx[2])
        early, early_own = chip_sum(idx, [gate_pair, out_pair])
        states_grad, early = lax.optimization_barrier((states_grad, early))
        early = lax.all_to_all(early, ("z", "x"), split_axis=0, concat_axis=0, tiled=True)

    mgrad, last8, first8, column_sums = run_third(
        pre, mixed, z, states_grad, states, rdot, leave, cw8, skip_wide, alog, gmat
    )
    near = lax.ppermute(first8, "seq", down)
    mgrad, extra = run_patch(mgrad, mixed, last8, near, cw8)
    conv_weight_grad = (column_sums + extra)[:KCONV]
    conv_bias_grad = column_sums[KCONV]

    mgrad_rows = mgrad.reshape(row_count, WIDE)
    mixed_local = dot(normed_rows, mgrad_rows, TN)
    input_grad, gain_rows = run_back(
        gate_grad, mgrad_rows, wg, main, block_input.reshape(row_count, D), upstream, gain8
    )
    input_grad = input_grad.reshape(block_input.shape)

    vector_local = jnp.concatenate(
        [
            gain_rows.sum(0),
            row_sums[0],
            conv_weight_grad.reshape(-1),
            conv_bias_grad,
            column_sums[5, :HEADS],
            -jnp.exp(decay_log) * column_sums[6, :HEADS],
            row_sums[1].reshape(HEADS, HEADDIM).sum(1),
        ]
    )
    if direct:
        mixed_pair = core_exchange(mixed_local, idx[2])
        late, late_own = chip_sum(idx, [mixed_pair])
        late = lax.all_to_all(late, ("z", "x"), split_axis=0, concat_axis=0, tiled=True)
        early_own = owner_sum(idx, early_own, early)
        early_own = early_own + swapped(early_own, "seq", 2, 1)
        share = D // 16
        gate_sum = early_own[:share]
        out_grad = jnp.concatenate([early_own[share:, :D], early_own[share:, D:]], axis=0)
        late_own = owner_sum(idx, late_own, late)
        mixed_sum = late_own + swapped(late_own, "seq", 2, 1)
    else:
        gate_sum = reduce_plain(core_sum(gate_partial))
        out_grad = reduce_split(core_sum(out_partial))
        mixed_sum = reduce_plain(core_sum(mixed_local))
    vector_rows = jnp.pad(vector_local, (0, -vector_local.shape[0] % 1024)).reshape(-1, 128)
    for axis in ("core", "seq", "x", "z"):
        if direct and axis == "x":
            vector_rows = lax.optimization_barrier((late, vector_rows))[1]
        vector_rows = xor_sum(vector_rows, axis)
    vector_grad = vector_rows.reshape(-1)[: vector_local.shape[0]]

    in_grad = jnp.concatenate([gate_sum, mixed_sum[:, :CONVCH]], axis=1)
    dt_grad = mixed_sum[:, CONVCH : CONVCH + HEADS]

    gate_tiles = kron_tiles(gate_sum, in_left, in_right, in_left_root, in_right_root, 0, 2)
    in_update, in_left_new, in_right_new = kron_tiles(
        mixed_sum[:, :CONVCH], in_left, in_right, in_left_root, in_right_root, DI // COL_BLOCK, 2,
        gate_tiles,
    )
    dt_update, dt_left_wide, dt_right_wide = kron_update(
        dt_grad, dt_left[:, None], dt_right[:, None], dt_left_root[:, None], dt_right_root[:, None]
    )
    out_update, out_left_new, out_right_new = kron_tiles(
        out_grad, out_left, out_right, out_left_root, out_right_root, 0, 1
    )
    vector_moment_new = 0.5 * vector_moment + 0.5 * vector_grad * vector_grad
    vector_update = -LR_VEC * vector_grad * lax.rsqrt(vector_moment_new)
    return (
        block_output,
        input_grad,
        in_grad,
        dt_grad,
        out_grad,
        in_update,
        dt_update,
        out_update,
        in_left_new,
        in_right_new,
        dt_left_wide[:, 0],
        dt_right_wide[:, 0],
        out_left_new,
        out_right_new,
        vector_grad,
        vector_moment_new,
        vector_update,
    )


def solution(mesh):
    dp, seq = mesh.shape["dp"], mesh.shape["seq"]
    split = (4, dp // 8, 2)
    torus = jax.sharding.Mesh(mesh.devices.reshape(split + (seq,)), AXES + ("seq",))
    tokens = P(AXES, "seq", None)
    rows = P(AXES, None)
    tri = P(AXES, None, None)
    quad = P(AXES, None, None, None)
    placed = (
        (tokens, tokens, rows, rows, rows) + (P(),) * 7 + (quad,) * 4 + (tri,) * 4 + (quad,) * 4 + (P(),)
    )

    return jax.shard_map(
        body,
        mesh=torus,
        in_specs=placed,
        out_specs=(tokens, tokens)
        + (rows,) * 6
        + (quad, quad, tri, tri, quad, quad)
        + (P(), P(), P()),
        check_vma=False,
    )
```

```python
import functools

import jax
import jax.numpy as jnp
from jax import lax
from jax.experimental import pallas as pl
from jax.experimental.pallas import tpu as pltpu
from jax.sharding import PartitionSpec as P


D = 768
HEADS = 24
HEADDIM = 64
DSTATE = 128
KCONV = 4
DI = 1536
CONVCH = 1792
WIDE = CONVCH + 128
ROW_BLOCK = 24
COL_BLOCK = 128

BL = 128
PAIRS = HEADS // 2

AXES = ("z", "x", "core")

EPS = 1e-05
LR = 0.25
LR_VEC = 0.02
NEG = -1e30
LOG2E = 1.4426950408889634
BF = jnp.bfloat16
F32 = jnp.float32
NN = (((1,), (0,)), ((), ()))
NT = (((1,), (1,)), ((), ()))
TN = (((0,), (0,)), ((), ()))


def dot(a, b, dims=NN):
    return lax.dot_general(a, b, dims, preferred_element_type=F32)


def split2(v):
    high = v.astype(BF)
    return high, (v - high.astype(F32)).astype(BF)


def dot3(a, b, dims=NN):
    ah, al = split2(a)
    bh, bl = split2(b)
    return dot(ah, bh, dims) + dot(al, bh, dims) + dot(ah, bl, dims)


def pack(v):
    high = v.astype(BF).astype(F32)
    rest = v - high
    mid = rest.astype(BF).astype(F32)
    low = rest - mid
    return (high + pltpu.roll(mid, 32, 1) + pltpu.roll(low, 64, 1)).astype(BF)


def head_lanes(shape):
    return lax.broadcasted_iota(jnp.int32, shape, 1) < HEADS


def prefix(tri, v):
    parts = dot(tri, pack(v))
    total = parts + pltpu.roll(parts, 96, 1) + pltpu.roll(parts, 64, 1)
    return jnp.where(head_lanes(total.shape), total, 0.0)


def expand(v, emat):
    return dot(pack(v), emat)


def head_sum(v, gather):
    high, low = split2(v)
    return dot(high, gather) + dot(low, gather)


def tri_mask(lower):
    rows = lax.broadcasted_iota(jnp.int32, (BL, BL), 0)
    cols = lax.broadcasted_iota(jnp.int32, (BL, BL), 1)
    return (rows >= cols) if lower else (cols >= rows)


def softplus(v):
    return jnp.maximum(v, 0.0) + jnp.log1p(jnp.exp(-jnp.abs(v)))


def sigmoid(v):
    return 0.5 * jnp.tanh(0.5 * v) + 0.5


def silu(v):
    half = 0.5 * v
    return half * jnp.tanh(half) + half


def silu_parts(v):
    half = 0.5 * v
    curve = jnp.tanh(half)
    return half * curve + half, 0.5 * curve + 0.5


def rates(alog_ref):
    rate = -jnp.exp(alog_ref[0:1, :])
    return jnp.where(head_lanes(rate.shape), rate, 0.0)


def pair_masks():
    left = lax.broadcasted_iota(jnp.int32, (BL, BL), 1) < HEADDIM
    first = jnp.where(left, 1.0, 0.0)
    return first.astype(BF), (1.0 - first).astype(BF)


def pair_blocks(v, masks):
    return jnp.concatenate([v * masks[0], v * masks[1]], axis=0)


def norm_rows(u, gain):
    inv = lax.rsqrt(jnp.mean(u * u, axis=-1, keepdims=True) + EPS)
    return u * inv * gain


def first_kernel(
    u_ref, halo_ref, gain_ref, w_ref, side_ref, cw_ref, cb_ref, dtb_ref, alog_ref, emat_ref,
    normed_ref, mixed_ref, pre_ref, z_ref, state_ref, total_ref,
    tail, full,
):
    step_index = pl.program_id(1)
    tile = u_ref.shape[1]
    gain = gain_ref[0:1, :]

    @pl.when(step_index == 0)
    def _():
        near = norm_rows(halo_ref[0].astype(F32), gain).astype(BF)
        tail[:, :DI] = dot(near, w_ref[...]).astype(BF).astype(F32)
        tail[:, DI:] = dot(near, side_ref[...])[:, : CONVCH - DI].astype(BF).astype(F32)
        state_ref[...] = jnp.zeros_like(state_ref)
        total_ref[...] = jnp.zeros_like(total_ref)

    normed = norm_rows(u_ref[0].astype(F32), gain).astype(BF)
    normed_ref[0] = normed
    side = dot(normed, side_ref[...])
    mixed_low = jnp.concatenate(
        [dot(normed, w_ref[...]).astype(BF), side[:, : CONVCH - DI].astype(BF)], axis=1
    )
    mixed_ref[0] = mixed_low
    z = side[:, CONVCH - DI :].astype(BF).astype(F32) + dtb_ref[0:1, :]
    z_ref[0] = z

    def conv_columns(i, carry):
        cols = pl.ds(pl.multiple_of(i * 256, 256), 256)
        own = mixed_ref[0, :, cols].astype(F32)
        joined = jnp.concatenate([tail[:, cols], own], axis=0)
        pre = cb_ref[0:1, cols] + cw_ref[KCONV - 1 : KCONV, cols] * own
        for tap in range(KCONV - 1):
            moved = pltpu.roll(joined, KCONV - 1 - tap, 0)[8:, :]
            pre = pre + cw_ref[tap : tap + 1, cols] * moved
        pre_ref[0, :, cols] = pre
        full[:, cols] = silu(pre)
        return carry

    lax.fori_loop(0, CONVCH // 256, conv_columns, 0)
    tail[...] = mixed_low[tile - 8 :, :].astype(F32)
    rate = rates(alog_ref)

    step_all = softplus(z)
    tri = jnp.where(tri_mask(True), 1.0, 0.0).astype(BF)
    emat = emat_ref[...]
    for part in range(tile // BL):
        rows = slice(part * BL, (part + 1) * BL)
        step = step_all[rows]
        cum = prefix(tri, step * rate)
        last = cum[BL - 1 : BL, :]
        weights = expand(jnp.exp(last - cum) * step, emat)
        decay = expand(
            jnp.where(head_lanes((8, 128)), jnp.broadcast_to(jnp.exp(last), (8, 128)), 0.0), emat
        )[0:1, :]
        fresh = dot3(full[rows, DI : DI + DSTATE].T, weights * full[rows, :DI])
        state_ref[0] = state_ref[0] * decay + fresh
        total_ref[0] = total_ref[0] + jnp.broadcast_to(last, (8, 128))


def dot_wide(ahl, ah, bh, bl):
    return dot(ahl, jnp.concatenate([bh, bh], axis=0)) + dot(ah, bl)


def dot3_split(a, b, dims):
    (ah, al), (bh, bl) = a, b
    return dot(ah, bh, dims) + dot(al, bh, dims) + dot(ah, bl, dims)


def wide_split(v):
    high, low = split2(v)
    return jnp.concatenate([high, low], axis=1), high


def rows8(v):
    return jnp.sum(v.reshape(v.shape[0] // 8, 8, v.shape[1]), axis=0)


def pair_values(pair, cum, cum_t, step, mask, left, transposed):
    kernels, columns = [], []
    for h in (2 * pair, 2 * pair + 1):
        column = jnp.broadcast_to(cum[:, h : h + 1], (BL, BL))
        row = cum_t[h : h + 1, :]
        spread = (row - column) if transposed else (column - row)
        kernels.append(jnp.exp2(jnp.where(mask, spread, NEG)))
        columns.append(column)
    chosen = jnp.where(left, columns[0], columns[1])
    steps = jnp.where(left, step[:, 2 * pair : 2 * pair + 1], step[:, 2 * pair + 1 : 2 * pair + 2])
    return kernels, chosen, steps


def lane_sum(v):
    return jnp.sum(v, axis=1, keepdims=True)


def second_kernel(
    pre_ref, z_ref, normed_ref, up_ref, u_ref, enter_ref, wg_ref, wo_ref, skip_ref, ggain_ref, alog_ref,
    gmat_ref,
    out_ref, branch_ref, dy_ref, ggrad_ref, state_ref, rdot_ref, dstate_ref, sums_ref,
    gain_acc, skip_acc, state, running, ys, es, xs_ref, ss_ref, sl_ref, sg_ref, up_scratch,
):
    step_index = pl.program_id(1)
    tile = pre_ref.shape[1]

    @pl.when(step_index == 0)
    def _():
        state[...] = enter_ref[0]
        running[...] = jnp.ones_like(running)
        dstate_ref[...] = jnp.zeros_like(dstate_ref)

    @pl.when((step_index == 0) & (pl.program_id(0) == 0))
    def _():
        gain_acc[...] = jnp.zeros_like(gain_acc)
        skip_acc[...] = jnp.zeros_like(skip_acc)

    rate = rates(alog_ref)

    def block(part, carry):
        rows = pl.ds(pl.multiple_of(part * BL, BL), BL)
        mask = tri_mask(True)
        left = lax.broadcasted_iota(jnp.int32, (BL, BL), 1) < HEADDIM
        masks = pair_masks()
        tri = jnp.where(mask, 1.0, 0.0).astype(BF)
        conv = silu(pre_ref[0, rows, DI:])
        inputs_b, inputs_c = conv[:, :DSTATE], conv[:, DSTATE:]
        step = softplus(z_ref[0, rows, :])
        cum = prefix(tri, step * (rate * LOG2E))
        cum_t = cum.T
        scores = dot3(inputs_c, inputs_b, NT)
        c_wide, c_high = wide_split(inputs_c)
        bt_wide, bt_high = wide_split(inputs_b.T)
        ct_wide, ct_high = wide_split(inputs_c.T)
        squares = jnp.zeros((BL, 128), F32)
        products = jnp.zeros((BL, 128), F32)
        for quad in range(PAIRS // 2):
            cols = slice(quad * 256, (quad + 1) * 256)
            inner, grown, weighted, xs = [], [], [], []
            for pair in (2 * quad, 2 * quad + 1):
                kernels, chosen, steps = pair_values(pair, cum, cum_t, step, mask, left, False)
                x = silu(pre_ref[0, rows, pair * 128 : (pair + 1) * 128])
                scaled = steps * x
                mh, ml = split2(jnp.concatenate([scores * k for k in kernels], axis=1))
                rh, rl = (pair_blocks(v, masks) for v in split2(scaled))
                inner.append(dot(mh, rh) + dot(ml, rh) + dot(mh, rl))
                grown.append(jnp.exp2(chosen))
                weighted.append(jnp.exp2(chosen[BL - 1 : BL, :] - chosen) * scaled)
                xs.append(x)
            inner, grown, weighted, x = (
                jnp.concatenate(v, axis=1) for v in (inner, grown, weighted, xs)
            )
            held = state[:, cols]
            state_ref[0, part, :, cols] = held
            yhat = inner + grown * dot_wide(c_wide, c_high, *split2(held))
            state[:, cols] = held * grown[BL - 1 : BL, :] + dot_wide(
                bt_wide, bt_high, *split2(weighted)
            )
            ys[:, cols] = yhat
            es[:, cols] = grown
            states = (yhat + skip_ref[0:1, cols] * x).astype(BF).astype(F32)
            sl, sg = silu_parts(dot(normed_ref[0, rows, :], wg_ref[:, cols]))
            upstream = dot(up_ref[rows, :], wo_ref[cols, :], NT)
            up_scratch[:, cols] = upstream
            gated = states * sl
            xs_ref[:, cols] = x
            ss_ref[:, cols] = states
            sl_ref[:, cols] = sl
            sg_ref[:, cols] = sg
            product = gated * (upstream * ggain_ref[0:1, cols])
            squared = gated * gated
            squares = squares + squared[:, :128] + squared[:, 128:]
            products = products + product[:, :128] + product[:, 128:]
        inv = lax.rsqrt(lane_sum(squares) * (1.0 / DI) + EPS)
        pull = jnp.broadcast_to(inv * inv * lane_sum(products) * (1.0 / DI), (BL, 128))
        inv = jnp.broadcast_to(inv, (BL, 128))
        rdot = jnp.zeros((BL, 128), F32)
        for quad in range(PAIRS // 2):
            cols = slice(quad * 256, (quad + 1) * 256)
            scaled_dy, dot_terms = [], []
            for pair in (2 * quad, 2 * quad + 1):
                own_cols = slice(pair * 128, (pair + 1) * 128)
                x = xs_ref[:, own_cols]
                yhat = ys[:, own_cols]
                states = ss_ref[:, own_cols]
                sl, sg = sl_ref[:, own_cols], sg_ref[:, own_cols]
                gated = states * sl
                gain = ggain_ref[0:1, own_cols]
                upstream = up_scratch[:, own_cols]
                norm = gated * inv
                branch_ref[rows, own_cols] = (norm * gain).astype(BF)
                gain_acc[:, own_cols] += rows8(upstream * norm)
                dgated = inv * (upstream * gain - gated * pull)
                dy_low = (dgated * sl).astype(BF)
                dy_ref[rows, own_cols] = dy_low
                ggrad_ref[rows, own_cols] = (dgated * states * (sg + sl * (1.0 - sg))).astype(BF)
                dy = dy_low.astype(F32)
                skip_acc[:, own_cols] += rows8(dy * x)
                dot_terms.append(dy * yhat)
                scaled_dy.append(es[:, own_cols] * running[0:1, own_cols] * dy)
            rdot = rdot + head_sum(jnp.concatenate(dot_terms, axis=1), gmat_ref[cols, :])
            dstate_ref[0, :, cols] += dot_wide(
                ct_wide, ct_high, *split2(jnp.concatenate(scaled_dy, axis=1))
            )
            running[:, cols] = running[:, cols] * es[BL - 1 : BL, cols]
        rdot_ref[0, rows, :] = rdot
        return carry

    lax.fori_loop(0, tile // BL, block, 0)
    out_ref[0] = (u_ref[0].astype(F32) + dot(branch_ref[...], wo_ref[...])).astype(BF)

    @pl.when((step_index == pl.num_programs(1) - 1) & (pl.program_id(0) == pl.num_programs(0) - 1))
    def _():
        sums_ref[0:1, :] = jnp.sum(gain_acc[...], axis=0, keepdims=True)
        sums_ref[1:2, :] = jnp.sum(skip_acc[...], axis=0, keepdims=True)


def third_kernel(
    pre_ref, mixed_ref, z_ref, dy_ref, state_ref, rdot_ref, leave_ref, cw_ref, skip_ref, alog_ref,
    gmat_ref,
    mgrad_ref, last_ref, first_ref, sums_ref,
    cw_acc, cb_acc, dtb_acc, rate_acc, dstate, tail,
):
    step_index = pl.program_id(1)

    @pl.when(step_index == 0)
    def _():
        dstate[...] = leave_ref[0]
        tail[...] = jnp.zeros_like(tail)

    @pl.when((step_index == 0) & (pl.program_id(0) == 0))
    def _():
        for ref in (cw_acc, cb_acc, dtb_acc, rate_acc):
            ref[...] = jnp.zeros_like(ref)

    rate = rates(alog_ref)
    mask = tri_mask(False)
    left = lax.broadcasted_iota(jnp.int32, (BL, BL), 1) < HEADDIM
    masks = pair_masks()
    low_tri = jnp.where(tri_mask(True), 1.0, 0.0).astype(BF)
    high_tri = jnp.where(mask, 1.0, 0.0).astype(BF)
    wide_pre = pre_ref[0, :, DI:]
    conv, wide_sg = silu_parts(wide_pre)
    inputs_b, inputs_c = conv[:, :DSTATE], conv[:, DSTATE:]
    z = z_ref[0]
    step = softplus(z)
    cum = prefix(low_tri, step * (rate * LOG2E))
    cum_t = cum.T
    lanes = head_lanes(cum.shape)
    scores_t = dot3(inputs_b, inputs_c, NT)
    b_wide, b_high = wide_split(inputs_b)
    ct_wide, ct_high = wide_split(inputs_c.T)
    dscores_t = jnp.zeros((BL, BL), F32)
    db = jnp.zeros((BL, DSTATE), F32)
    dc = jnp.zeros((BL, DSTATE), F32)
    sums = jnp.zeros((BL + 8, 128), F32)

    def back_conv(cols, dpre):
        joined = jnp.concatenate([dpre, tail[:, cols]], axis=0)
        tail[:, cols] = dpre[0:8, :]
        mixed = mixed_ref[0, :, cols].astype(F32)
        cb_acc[:, cols] += rows8(dpre)
        mgrad = cw_ref[KCONV - 1 : KCONV, cols] * dpre
        cw_acc[KCONV - 1, :, cols] += rows8(dpre * mixed)
        for tap in range(KCONV - 1):
            moved = pltpu.roll(joined, BL + 8 - (KCONV - 1 - tap), 0)[:BL, :]
            mgrad = mgrad + cw_ref[tap : tap + 1, cols] * moved
            cw_acc[tap, :, cols] += rows8(moved * mixed)
        mgrad_ref[0, :, cols] = mgrad.astype(BF)
        last_ref[0, :, cols] = jnp.where(step_index == 0, mgrad[BL - 8 :, :], last_ref[0, :, cols])

    for quad in range(PAIRS // 2):
        cols = slice(quad * 256, (quad + 1) * 256)
        inner, grown, shrink, scaled, xs, steps_wide, slopes = [], [], [], [], [], [], []
        dy = dy_ref[:, cols].astype(F32)
        for pair in (2 * quad, 2 * quad + 1):
            kernels, chosen, steps = pair_values(pair, cum, cum_t, step, mask, left, True)
            own = pre_ref[0, :, pair * 128 : (pair + 1) * 128]
            x, sg = silu_parts(own)
            slopes.append(sg + x * (1.0 - sg))
            xd = steps * x
            mh, ml = split2(jnp.concatenate([scores_t * k for k in kernels], axis=1))
            dyb = pair_blocks(dy_ref[:, pair * 128 : (pair + 1) * 128], masks)
            inner.append(dot(mh, dyb) + dot(ml, dyb))
            sh, sl = split2(xd)
            dmix = dot(sh, dyb, NT) + dot(sl, dyb, NT)
            dscores_t = dscores_t + dmix[:, :BL] * kernels[0] + dmix[:, BL:] * kernels[1]
            grown.append(jnp.exp2(chosen))
            shrink.append(jnp.exp2(chosen[BL - 1 : BL, :] - chosen))
            scaled.append(xd)
            xs.append(x)
            steps_wide.append(steps)
        inner, grown, shrink, scaled, x, steps_wide, slopes = (
            jnp.concatenate(v, axis=1) for v in (inner, grown, shrink, scaled, xs, steps_wide, slopes)
        )
        held = state_ref[0, 0, :, cols]
        ds = dstate[:, cols]
        held_parts, ds_parts = split2(held), split2(ds)
        decay = grown[BL - 1 : BL, :]
        dscaled_state = shrink * dot_wide(b_wide, b_high, *ds_parts)
        dscaled = inner + dscaled_state
        ends = jnp.sum(scaled * dscaled_state, axis=0, keepdims=True) + decay * jnp.sum(
            held * ds, axis=0, keepdims=True
        )
        sums = sums + head_sum(
            jnp.concatenate([x * dscaled, jnp.broadcast_to(ends, (8, 256))], axis=0),
            gmat_ref[cols, :],
        )
        grown_parts = split2(grown * dy)
        dc = dc + dot3_split(grown_parts, held_parts, NT)
        db = db + dot3_split(split2(shrink * scaled), ds_parts, NT)
        dstate[:, cols] = decay * ds + dot_wide(ct_wide, ct_high, *grown_parts)
        back_conv(cols, (steps_wide * dscaled + skip_ref[0:1, cols] * dy) * slopes)

    direct = sums[:BL]
    is_last = lax.broadcasted_iota(jnp.int32, (BL, 128), 0) == BL - 1
    dcum = rdot_ref[0] - step * direct + jnp.where(is_last, sums[BL : BL + 1, :], 0.0)
    dcum = jnp.where(lanes, dcum, 0.0)
    drate = prefix(high_tri, dcum)
    dz = (rate * drate + direct) * sigmoid(z)
    mgrad_ref[0, :, CONVCH:] = dz.astype(BF)
    dtb_acc[...] += rows8(dz)
    rate_acc[...] += rows8(step * drate)
    db = db + dot3(dscores_t, inputs_c)
    dc = dc + dot3(dscores_t.T, inputs_b)
    back_conv(
        slice(DI, CONVCH),
        jnp.concatenate([db, dc], axis=1) * (wide_sg + conv * (1.0 - wide_sg)),
    )
    first_ref[0] = tail[...]

    @pl.when((step_index == pl.num_programs(1) - 1) & (pl.program_id(0) == pl.num_programs(0) - 1))
    def _():
        for tap in range(KCONV):
            sums_ref[tap : tap + 1, :] = jnp.sum(cw_acc[tap], axis=0, keepdims=True)
        sums_ref[4:5, :] = jnp.sum(cb_acc[...], axis=0, keepdims=True)
        sums_ref[5:6, :128] = jnp.sum(dtb_acc[...], axis=0, keepdims=True)
        sums_ref[6:7, :128] = jnp.sum(rate_acc[...], axis=0, keepdims=True)


def patch_kernel(mgrad_ref, mixed_ref, last_ref, near_ref, cw_ref, out_ref, extra_ref):
    @pl.when(pl.program_id(0) == 0)
    def _():
        extra_ref[...] = jnp.zeros_like(extra_ref)

    rows = [last_ref[0, i : i + 1, :] for i in range(8)]
    near = [near_ref[0, i : i + 1, :] for i in range(KCONV - 1)]
    held = mixed_ref[0].astype(F32)
    first = 8 - (KCONV - 1)
    for k in range(KCONV - 1):
        for j in range(k, KCONV - 1):
            rows[first + j] = rows[first + j] + cw_ref[k : k + 1, :] * near[j - k]
            extra_ref[k : k + 1, :] += near[j - k] * held[8 + first + j : 9 + first + j, :]
    old = mgrad_ref[0].astype(F32)
    patched = jnp.concatenate([old[:8, :CONVCH], jnp.concatenate(rows, axis=0)], axis=0)
    out_ref[0, :, :CONVCH] = patched.astype(BF)
    out_ref[0, :, CONVCH:] = mgrad_ref[0, :, CONVCH:]


PARAMS = dict(vmem_limit_bytes=60 * 1024 * 1024)


def whole(shape):
    zeros = (0,) * len(shape)
    return pl.BlockSpec(shape, lambda b, i: zeros)


def run_first(u, halo, gain, w, side, cw, cb, dtb, alog, emat):
    seqs, length, _ = u.shape
    tile = min(256, length)
    grid = (seqs, length // tile)
    tok = lambda width: pl.BlockSpec((1, tile, width), lambda b, i: (b, i, 0))
    per = lambda *shape: pl.BlockSpec((1,) + shape, lambda b, i: (b,) + (0,) * len(shape))
    return pl.pallas_call(
        first_kernel,
        grid=grid,
        in_specs=[
            tok(D), per(8, D), whole(gain.shape), whole(w.shape),
            whole(side.shape),
            whole(cw.shape), whole(cb.shape), whole(dtb.shape), whole(alog.shape), whole(emat.shape),
        ],
        out_specs=[
            tok(D), tok(CONVCH), tok(CONVCH), tok(128), per(DSTATE, DI), per(8, 128),
        ],
        out_shape=[
            jax.ShapeDtypeStruct((seqs, length, D), BF),
            jax.ShapeDtypeStruct((seqs, length, CONVCH), BF),
            jax.ShapeDtypeStruct((seqs, length, CONVCH), F32),
            jax.ShapeDtypeStruct((seqs, length, 128), F32),
            jax.ShapeDtypeStruct((seqs, DSTATE, DI), F32),
            jax.ShapeDtypeStruct((seqs, 8, 128), F32),
        ],
        scratch_shapes=[pltpu.VMEM((8, CONVCH), F32), pltpu.VMEM((tile, CONVCH), F32)],
        compiler_params=pltpu.CompilerParams(**PARAMS),
        name="first",
    )(u, halo, gain, w, side, cw, cb, dtb, alog, emat)


def run_second(pre, z, normed, up, u, enter, wg, wo, skip, ggain, alog, gmat):
    seqs, length, _ = u.shape
    tile = min(256, length)
    steps = length // tile
    parts = tile // BL
    grid = (seqs, steps)
    tok = lambda width: pl.BlockSpec((1, tile, width), lambda b, i: (b, i, 0))
    flat = lambda width: pl.BlockSpec((tile, width), lambda b, i: (b * steps + i, 0))
    per = lambda *shape: pl.BlockSpec((1,) + shape, lambda b, i: (b,) + (0,) * len(shape))
    rows = seqs * length
    return pl.pallas_call(
        second_kernel,
        grid=grid,
        in_specs=[
            tok(CONVCH), tok(128), tok(D), flat(D), tok(D), per(DSTATE, DI), whole(wg.shape),
            whole(wo.shape),
            whole(skip.shape), whole(ggain.shape), whole(alog.shape), whole(gmat.shape),
        ],
        out_specs=[
            tok(D), flat(DI), flat(DI), flat(DI),
            pl.BlockSpec((1, parts, DSTATE, DI), lambda b, i: (b, i, 0, 0)),
            tok(128), per(DSTATE, DI), whole((8, DI)),
        ],
        out_shape=[
            jax.ShapeDtypeStruct((seqs, length, D), BF),
            jax.ShapeDtypeStruct((rows, DI), BF),
            jax.ShapeDtypeStruct((rows, DI), BF),
            jax.ShapeDtypeStruct((rows, DI), BF),
            jax.ShapeDtypeStruct((seqs, length // BL, DSTATE, DI), F32),
            jax.ShapeDtypeStruct((seqs, length, 128), F32),
            jax.ShapeDtypeStruct((seqs, DSTATE, DI), F32),
            jax.ShapeDtypeStruct((8, DI), F32),
        ],
        scratch_shapes=[
            pltpu.VMEM((8, DI), F32), pltpu.VMEM((8, DI), F32), pltpu.VMEM((DSTATE, DI), F32),
            pltpu.VMEM((8, DI), F32), *[pltpu.VMEM((BL, DI), F32)] * 7,
        ],
        compiler_params=pltpu.CompilerParams(**PARAMS),
        name="second",
    )(pre, z, normed, up, u, enter, wg, wo, skip, ggain, alog, gmat)


def run_third(pre, mixed, z, dy, states, rdot, leave, cw, skip, alog, gmat):
    seqs, length, _ = pre.shape
    steps = length // BL
    grid = (seqs, steps)
    tok = lambda width: pl.BlockSpec((1, BL, width), lambda b, i: (b, steps - 1 - i, 0))
    per = lambda *shape: pl.BlockSpec((1,) + shape, lambda b, i: (b,) + (0,) * len(shape))
    return pl.pallas_call(
        third_kernel,
        grid=grid,
        in_specs=[
            tok(CONVCH), tok(CONVCH), tok(128),
            pl.BlockSpec((BL, DI), lambda b, i: (b * steps + steps - 1 - i, 0)),
            pl.BlockSpec((1, 1, DSTATE, DI), lambda b, i: (b, steps - 1 - i, 0, 0)),
            tok(128), per(DSTATE, DI), whole(cw.shape), whole(skip.shape), whole(alog.shape),
            whole(gmat.shape),
        ],
        out_specs=[
            tok(WIDE), per(8, CONVCH), per(8, CONVCH), whole((8, CONVCH)),
        ],
        out_shape=[
            jax.ShapeDtypeStruct((seqs, length, WIDE), BF),
            jax.ShapeDtypeStruct((seqs, 8, CONVCH), F32),
            jax.ShapeDtypeStruct((seqs, 8, CONVCH), F32),
            jax.ShapeDtypeStruct((8, CONVCH), F32),
        ],
        scratch_shapes=[
            pltpu.VMEM((KCONV, 8, CONVCH), F32), pltpu.VMEM((8, CONVCH), F32),
            pltpu.VMEM((8, 128), F32), pltpu.VMEM((8, 128), F32),
            pltpu.VMEM((DSTATE, DI), F32), pltpu.VMEM((8, CONVCH), F32),
        ],
        compiler_params=pltpu.CompilerParams(**PARAMS),
        name="third",
    )(pre, mixed, z, dy, states, rdot, leave, cw, skip, alog, gmat)


def run_patch(mgrad, mixed, last8, near, cw):
    seqs, length, _ = mgrad.shape
    end = length // 16 - 1
    tok = lambda width: pl.BlockSpec((1, 16, width), lambda b: (b, end, 0))
    per = pl.BlockSpec((1, 8, CONVCH), lambda b: (b, 0, 0))
    row = pl.BlockSpec((8, CONVCH), lambda b: (0, 0))
    taps = pl.BlockSpec(cw.shape, lambda b: (0, 0))
    return pl.pallas_call(
        patch_kernel,
        grid=(seqs,),
        in_specs=[tok(WIDE), tok(CONVCH), per, per, taps],
        out_specs=[tok(WIDE), row],
        out_shape=[
            jax.ShapeDtypeStruct(mgrad.shape, BF),
            jax.ShapeDtypeStruct((8, CONVCH), F32),
        ],
        input_output_aliases={0: 0},
        name="patch",
    )(mgrad, mixed, last8, near, cw)


def kron_update(gradient, left_stat, right_stat, left_root, right_root):
    row_tiles, col_tiles = (left_stat.shape[0], left_stat.shape[1])
    row_size, col_size = (left_stat.shape[-1], right_stat.shape[-1])
    grad_tiles = gradient.reshape(row_tiles, row_size, col_tiles, col_size).transpose(0, 2, 1, 3)
    left_new = 0.5 * left_stat + 0.5 * jnp.einsum(
        "abij,abkj->abik", grad_tiles, grad_tiles, precision=lax.Precision.HIGH
    )
    right_new = 0.5 * right_stat + 0.5 * jnp.einsum(
        "abji,abjk->abik", grad_tiles, grad_tiles, precision=lax.Precision.HIGH
    )
    shaped = jnp.einsum("abij,abjk->abik", left_root, grad_tiles, precision=lax.Precision.HIGH)
    shaped = jnp.einsum("abij,abjk->abik", shaped, right_root, precision=lax.Precision.HIGH)
    update = (-LR * shaped).transpose(0, 2, 1, 3).reshape(gradient.shape)
    return (update, left_new, right_new)


def float_parts(v):
    high = v.astype(BF).astype(F32)
    return high, v - high


def kron_kernel(*refs, unroll):
    grad_ref, left_ref, right_ref, left_root_ref, right_root_ref = refs[:5]
    update_ref, left_new_ref, right_new_ref = refs[-3:]

    def column(c, carry):
        cols = pl.ds(pl.multiple_of(c * COL_BLOCK, COL_BLOCK), COL_BLOCK)
        for r in range(left_ref.shape[0]):
            rows = slice(r * ROW_BLOCK, (r + 1) * ROW_BLOCK)
            grad = grad_ref[rows, cols]
            high, low = float_parts(grad)
            root_high, root_low = float_parts(left_root_ref[r, c])
            below = jnp.concatenate([high, high, low], axis=0).astype(BF)
            right = dot(jnp.concatenate([high, low, high], axis=0).astype(BF), below, TN)
            rooted = dot(
                jnp.concatenate([root_high, root_low, root_high], axis=0).astype(BF), below, TN
            )
            high, low = high.astype(BF), low.astype(BF)
            left = dot(
                jnp.concatenate([high, low], axis=1), jnp.concatenate([high, high], axis=1), NT
            ) + dot(high, low, NT)
            left_new_ref[r, c] = 0.5 * left_ref[r, c] + 0.5 * left
            right_new_ref[r, c] = 0.5 * right_ref[r, c] + 0.5 * right
            shaped = dot_wide(*wide_split(rooted), *split2(right_root_ref[r, c]))
            update_ref[rows, cols] = -LR * shaped
        return carry

    lax.fori_loop(0, left_ref.shape[1], column, 0, unroll=unroll)


def kron_tiles(grad, left, right, left_root, right_root, first, step, earlier=None):
    row_tiles = left.shape[0]
    rows, cols = grad.shape
    stat = lambda size: pl.BlockSpec(
        tuple(pl.Element(n) for n in (row_tiles, step, size, size)),
        lambda i: (0, first + step * i, 0, 0),
    )
    wide = step * COL_BLOCK
    ins = [grad, left, right, left_root, right_root]
    in_specs = [pl.BlockSpec((rows, wide), lambda i: (0, i))] + [stat(ROW_BLOCK), stat(COL_BLOCK)] * 2
    aliases = {}
    if earlier is not None:
        ins += list(earlier)
        in_specs += [pl.BlockSpec(memory_space=pl.ANY)] * 3
        aliases = {5: 0, 6: 1, 7: 2}
    total = left.shape[1] * COL_BLOCK
    return pl.pallas_call(
        functools.partial(kron_kernel, unroll=max(1, 4 // row_tiles)),
        grid=(cols // wide,),
        in_specs=in_specs,
        out_specs=[
            pl.BlockSpec(
                (pl.Element(rows), pl.Element(wide)),
                lambda i: (0, pl.multiple_of(first * COL_BLOCK + wide * i, COL_BLOCK)),
            ),
            stat(ROW_BLOCK), stat(COL_BLOCK),
        ],
        out_shape=[
            jax.ShapeDtypeStruct((rows, total), F32),
            jax.ShapeDtypeStruct(left.shape, F32),
            jax.ShapeDtypeStruct(right.shape, F32),
        ],
        input_output_aliases=aliases,
        compiler_params=pltpu.CompilerParams(**PARAMS),
        name="kron",
    )(*ins)


def back_kernel(
    ggrad_ref, mgrad_ref, wg_ref, main_ref, side_ref, u_ref, up_ref, gain_ref, out_ref, gain_grad_ref
):
    @pl.when(pl.program_id(0) == 0)
    def _():
        gain_grad_ref[...] = jnp.zeros_like(gain_grad_ref)

    grad = (
        dot(ggrad_ref[...], wg_ref[...], NT)
        + dot(mgrad_ref[:, :DI], main_ref[...], NT)
        + dot(mgrad_ref[:, DI:], side_ref[...], NT)
    )
    u = u_ref[...].astype(F32)
    inv = lax.rsqrt(jnp.mean(u * u, axis=-1, keepdims=True) + EPS)
    norm = u * inv
    gain_grad_ref[...] += rows8(grad * norm)
    scaled = grad * gain_ref[0:1, :]
    pull = jnp.mean(scaled * norm, axis=-1, keepdims=True)
    out_ref[...] = up_ref[...].astype(F32) + inv * (scaled - norm * pull)


def run_back(ggrad, mgrad, wg, main, side, u, up, gain):
    rows = u.shape[0]
    tile = min(256, rows)
    tok = lambda width: pl.BlockSpec((tile, width), lambda i: (i, 0))
    return pl.pallas_call(
        back_kernel,
        grid=(rows // tile,),
        in_specs=[
            tok(DI), tok(WIDE), pl.BlockSpec(wg.shape, lambda i: (0, 0)),
            pl.BlockSpec(main.shape, lambda i: (0, 0)), pl.BlockSpec(side.shape, lambda i: (0, 0)),
            tok(D), tok(D),
            pl.BlockSpec(gain.shape, lambda i: (0, 0)),
        ],
        out_specs=[tok(D), pl.BlockSpec((8, D), lambda i: (0, 0))],
        out_shape=[jax.ShapeDtypeStruct((rows, D), F32), jax.ShapeDtypeStruct((8, D), F32)],
        compiler_params=pltpu.CompilerParams(**PARAMS),
        name="back",
    )(ggrad, mgrad, wg, main, side, u, up, gain)


def swapped(v, axis, size, offset):
    return lax.ppermute(v, axis, [(i, (i + offset) % size) for i in range(size)])


def pick(v, index):
    return lax.dynamic_index_in_dim(v, index, 0, keepdims=False)


def scatter_stage(v, axis, kind=BF):
    size = lax.axis_size(axis)
    here = lax.axis_index(axis)
    total = pick(v, here)
    for offset in range(1, size):
        sent = pick(v, lax.rem(here + offset, size)).astype(kind)
        total = total + swapped(sent, axis, size, offset).astype(F32)
    return total


def gather_stage(v, axis):
    size = lax.axis_size(axis)
    here = lax.axis_index(axis)
    out = jnp.zeros((size,) + v.shape, v.dtype)
    out = lax.dynamic_update_index_in_dim(out, v, here, 0)
    for offset in range(1, size):
        got = swapped(v, axis, size, offset)
        out = lax.dynamic_update_index_in_dim(out, got, lax.rem(here - offset + size, size), 0)
    return out


def core_sum(partial):
    z, x, core = (lax.axis_size(a) for a in ("z", "x", "core"))
    rows, cols = partial.shape
    blocks = partial.reshape(z, x, core, rows // (z * x * core), cols)
    return scatter_stage(jnp.moveaxis(blocks, 2, 0), "core", F32)


def across(v):
    return scatter_stage(scatter_stage(jnp.moveaxis(v, 1, 0), "x"), "z")


def reduce_plain(v):
    owned = across(v)
    total = owned
    size = lax.axis_size("seq")
    if size > 2:
        return lax.psum(owned, "seq")
    for offset in range(1, size):
        total = total + swapped(owned, "seq", size, offset)
    return total


def reduce_split(v):
    size = lax.axis_size("seq")
    z, x, rows, cols = v.shape
    if cols % (128 * size):
        return reduce_plain(v)
    v = jnp.moveaxis(v.reshape(z, x, rows, size, cols // size), 3, 0)
    owned = across(scatter_stage(v, "seq"))
    return jnp.moveaxis(gather_stage(owned, "seq"), 0, 1).reshape(rows, cols)


def xor_sum(v, axis):
    size = lax.axis_size(axis)
    bit = 1
    while bit < size:
        v = v + lax.ppermute(v, axis, [(i, i ^ bit) for i in range(size)])
        bit *= 2
    return v


STEP_OWNERS = 4


def chip_kernel(idx, *refs):
    send_ref, own_ref = refs[-2:]
    width = own_ref.shape[1]

    def one_owner(owner, carry):
        mine = pl.program_id(0) * STEP_OWNERS + owner == idx[0] * 2 + idx[1]
        row, col = 0, 0
        for part_ref, got_ref in zip(refs[:-2:2], refs[1:-2:2]):
            total = part_ref[owner, 0] + got_ref[owner]
            rows = total.shape[0] * total.shape[1] // width
            for low in range(0, total.shape[0], rows):
                piece = total[low : low + rows]
                at = (slice(row, row + rows), slice(col, col + piece.shape[1]))
                send_ref[(owner,) + at] = piece.astype(BF)

                @pl.when(mine)
                def _(at=at, piece=piece):
                    own_ref[at] = piece

                col += piece.shape[1]
                if col == width:
                    row, col = row + rows, 0
        return carry

    lax.fori_loop(0, STEP_OWNERS, one_owner, 0)


def chip_sum(idx, pairs):
    in_specs, ins, total, width = [], [], 0, 0
    for blocks, got in pairs:
        _, _, rows, cols = blocks.shape
        width = max(width, cols)
        total += rows * cols
        ins += [blocks, got]
        in_specs += [
            pl.BlockSpec((STEP_OWNERS, 1, rows, cols), lambda i, idx: (i, idx[2], 0, 0)),
            pl.BlockSpec((STEP_OWNERS, rows, cols), lambda i, idx: (i, 0, 0)),
        ]
    rows = total // width
    return pl.pallas_call(
        chip_kernel,
        grid_spec=pltpu.PrefetchScalarGridSpec(
            num_scalar_prefetch=1,
            grid=(8 // STEP_OWNERS,),
            in_specs=in_specs,
            out_specs=[
                pl.BlockSpec((STEP_OWNERS, rows, width), lambda i, idx: (i, 0, 0)),
                pl.BlockSpec((rows, width), lambda i, idx: (0, 0)),
            ],
        ),
        out_shape=[
            jax.ShapeDtypeStruct((8, rows, width), BF),
            jax.ShapeDtypeStruct((rows, width), F32),
        ],
        compiler_params=pltpu.CompilerParams(**PARAMS),
        name="chip_sum",
    )(idx, *ins)


def owner_kernel(idx, own_ref, got_ref, out_ref):
    mine = idx[0] * 2 + idx[1]
    total = own_ref[...]
    for i in range(8):
        total = total + jnp.where(mine == i, 0.0, got_ref[i].astype(F32))
    out_ref[...] = total


def owner_sum(idx, own, got):
    rows, width = own.shape
    tile = 48
    return pl.pallas_call(
        owner_kernel,
        grid_spec=pltpu.PrefetchScalarGridSpec(
            num_scalar_prefetch=1,
            grid=(rows // tile,),
            in_specs=[
                pl.BlockSpec((tile, width), lambda i, idx: (i, 0)),
                pl.BlockSpec((8, tile, width), lambda i, idx: (0, i, 0)),
            ],
            out_specs=pl.BlockSpec((tile, width), lambda i, idx: (i, 0)),
        ),
        out_shape=jax.ShapeDtypeStruct((rows, width), F32),
        name="owner_sum",
    )(idx, own, got)


def core_exchange(partial, core):
    rows, cols = partial.shape
    blocks = partial.reshape(8, 2, rows // 16, cols)
    sent = lax.dynamic_index_in_dim(blocks, 1 - core, 1, keepdims=False)
    return blocks, swapped(sent, "core", 2, 1)


def around(v, axis):
    size = lax.axis_size(axis)
    return jnp.stack([v] + [swapped(v, axis, size, offset) for offset in range(1, size)])


def assemble_kernel(idx, *refs, order):
    out_ref = refs[-1]
    sizes = {"z": 4, "x": 2}
    here = {"z": idx[0], "x": idx[1]}
    spots = ((idx[2], idx[3]), (idx[2], 1 - idx[3]), (1 - idx[2], idx[3]), (1 - idx[2], 1 - idx[3]))
    for ref, (core, seq) in zip(refs[:-1], spots):
        for a in range(ref.shape[0]):
            for b in range(ref.shape[1]):
                at = dict(
                    (axis, lax.rem(here[axis] - back + sizes[axis], sizes[axis]))
                    for axis, back in zip(order[::-1], (a, b))
                )
                out_ref[((at["z"] * 2 + at["x"]) * 2 + core) * 2 + seq] = ref[a, b]


def assemble(idx, pieces, order):
    shape = pieces[0].shape
    rows, cols = shape[-2:]
    out = pl.pallas_call(
        functools.partial(assemble_kernel, order=order),
        grid_spec=pltpu.PrefetchScalarGridSpec(
            num_scalar_prefetch=1,
            grid=(1,),
            in_specs=[pl.BlockSpec(shape, lambda i, idx: (0,) * 4)] * 4,
            out_specs=pl.BlockSpec((32, rows, cols), lambda i, idx: (0, 0, 0)),
        ),
        out_shape=jax.ShapeDtypeStruct((32, rows, cols), pieces[0].dtype),
        compiler_params=pltpu.CompilerParams(**PARAMS),
        name="assemble",
    )(idx, *pieces)
    return out.reshape(32 * rows, cols)


def body(
    block_input,
    cotangent,
    in_weight,
    dt_weight,
    out_weight,
    norm_gain,
    conv_weight,
    conv_bias,
    dt_bias,
    decay_log,
    skip_gain,
    gate_gain,
    in_left,
    in_right,
    in_left_root,
    in_right_root,
    dt_left,
    dt_right,
    dt_left_root,
    dt_right_root,
    out_left,
    out_right,
    out_left_root,
    out_right_root,
    vector_moment,
):
    seq_count, local_len, _ = block_input.shape
    seq_devices = lax.axis_size("seq")
    row_count = seq_count * local_len
    up = [(i, i + 1) for i in range(seq_devices - 1)]
    down = [(i + 1, i) for i in range(seq_devices - 1)]

    in_low = in_weight.astype(BF)
    dt_low = jnp.pad(dt_weight.astype(BF), ((0, 0), (0, 128 - HEADS)))
    main = lax.all_gather(in_low[:, DI : 2 * DI], AXES, axis=0, tiled=True)
    side_low = jnp.concatenate([in_low[:, 2 * DI :], dt_low], axis=1)
    part = jnp.arange(128)
    channel = jnp.arange(DI)
    emat = (
        ((part[:, None] % 32) == (channel[None, :] // HEADDIM)) & (part[:, None] < 96)
    ).astype(BF)
    gmat = ((channel[:, None] // HEADDIM) == part[None, :]).astype(BF)
    skip_wide = jnp.repeat(skip_gain, HEADDIM).reshape(1, DI)
    alog = jnp.pad(decay_log, (0, 128 - HEADS)).reshape(1, 128)
    dtb = jnp.pad(dt_bias, (0, 128 - HEADS), constant_values=-1e4).reshape(1, 128)
    cw8 = conv_weight
    gain8, cb8 = norm_gain.reshape(1, D), conv_bias.reshape(1, CONVCH)
    ggain8 = gate_gain.reshape(1, DI)
    tables = (emat, gmat, skip_wide, alog, dtb, cw8, gain8, cb8, ggain8)
    torus_sizes = tuple(lax.axis_size(a) for a in ("z", "x", "core", "seq"))
    direct = torus_sizes == (4, 2, 2, 2)
    idx = jnp.stack([lax.axis_index(a) for a in ("z", "x", "core", "seq")]).astype(jnp.int32)
    gate_low, out_low = in_low[:, :DI], out_weight.astype(BF)
    if direct:
        order = ("z", "x")
        side_near = pick(side_low.reshape(2, -1, WIDE - DI), idx[3])
        side_near = around(around(side_near, "z"), "x")
        side_far = swapped(side_near, "core", 2, 1)
        side_got = swapped(side_near, "seq", 2, 1)
        side = assemble(
            idx, (side_near, side_got, side_far, swapped(side_got, "core", 2, 1)), order
        )
        gate_near = pick(gate_low.reshape(2, -1, DI), idx[3])
        out_near = pick(out_low.reshape(2, -1, D), idx[3])
        gate_near = around(around(gate_near, "z"), "x")
        out_near = around(around(out_near, "z"), "x")
        main = lax.optimization_barrier((main, side, gate_near, out_near) + tables)[0]
        gate_got = swapped(gate_near, "seq", 2, 1)
        out_got = swapped(out_near, "seq", 2, 1)
        gate_far = swapped(gate_near, "core", 2, 1)
        out_far = swapped(out_near, "core", 2, 1)
    else:
        side = lax.all_gather(side_low, AXES, axis=0, tiled=True)
        wg = lax.all_gather(gate_low, AXES, axis=0, tiled=True)
        wo = lax.all_gather(out_low, AXES, axis=0, tiled=True)
    halo = lax.ppermute(block_input[:, local_len - 8 :, :], "seq", up)

    normed, mixed, pre, z, local_state, total = run_first(
        block_input, halo, gain8, main, side, cw8, cb8, dtb, alog, emat
    )
    span = jnp.repeat(jnp.exp(total[:, 0:1, :HEADS]), HEADDIM, axis=2)
    enter = lax.ppermute(local_state, "seq", up)
    for _ in range(seq_devices - 2):
        enter = lax.ppermute(local_state + span * enter, "seq", up)

    if direct:
        out_far_got = swapped(out_got, "core", 2, 1)
        gate_far_got = swapped(gate_got, "core", 2, 1)
        wo = assemble(idx, (out_near, out_got, out_far, out_far_got), order)
        wg = assemble(idx, (gate_near, gate_got, gate_far, gate_far_got), order)
    normed_rows = normed.reshape(row_count, D)
    upstream = cotangent.reshape(row_count, D)
    (
        block_output, branch, states_grad, gate_grad, states, rdot, local_dstate, row_sums,
    ) = run_second(
        pre, z, normed, upstream, block_input, enter, wg, wo, skip_wide, ggain8, alog,
        gmat,
    )
    leave = lax.ppermute(local_dstate, "seq", down)
    for _ in range(seq_devices - 2):
        leave = lax.ppermute(local_dstate + span * leave, "seq", down)

    out_partial = dot(branch, upstream, TN)
    gate_partial = dot(normed_rows, gate_grad, TN)
    if direct:
        gate_pair = core_exchange(gate_partial, idx[2])
        out_pair = core_exchange(out_partial, idx[2])
        early, early_own = chip_sum(idx, [gate_pair, out_pair])
        states_grad, early = lax.optimization_barrier((states_grad, early))
        early = lax.all_to_all(early, ("z", "x"), split_axis=0, concat_axis=0, tiled=True)

    mgrad, last8, first8, column_sums = run_third(
        pre, mixed, z, states_grad, states, rdot, leave, cw8, skip_wide, alog, gmat
    )
    near = lax.ppermute(first8, "seq", down)
    mgrad, extra = run_patch(mgrad, mixed, last8, near, cw8)
    conv_weight_grad = (column_sums + extra)[:KCONV]
    conv_bias_grad = column_sums[KCONV]

    mgrad_rows = mgrad.reshape(row_count, WIDE)
    mixed_local = dot(normed_rows, mgrad_rows, TN)
    input_grad, gain_rows = run_back(
        gate_grad, mgrad_rows, wg, main, side, block_input.reshape(row_count, D), upstream, gain8
    )
    input_grad = input_grad.reshape(block_input.shape)

    vector_local = jnp.concatenate(
        [
            gain_rows.sum(0),
            row_sums[0],
            conv_weight_grad.reshape(-1),
            conv_bias_grad,
            column_sums[5, :HEADS],
            -jnp.exp(decay_log) * column_sums[6, :HEADS],
            row_sums[1].reshape(HEADS, HEADDIM).sum(1),
        ]
    )
    if direct:
        mixed_pair = core_exchange(mixed_local, idx[2])
        late, late_own = chip_sum(idx, [mixed_pair])
        late = lax.all_to_all(late, ("z", "x"), split_axis=0, concat_axis=0, tiled=True)
        early_own = owner_sum(idx, early_own, early)
        early_own = early_own + swapped(early_own, "seq", 2, 1)
        share = D // 16
        gate_sum = early_own[:share]
        out_grad = jnp.concatenate([early_own[share:, :D], early_own[share:, D:]], axis=0)
        late_own = owner_sum(idx, late_own, late)
        mixed_sum = late_own + swapped(late_own, "seq", 2, 1)
    else:
        gate_sum = reduce_plain(core_sum(gate_partial))
        out_grad = reduce_split(core_sum(out_partial))
        mixed_sum = reduce_plain(core_sum(mixed_local))
    vector_rows = jnp.pad(vector_local, (0, -vector_local.shape[0] % 1024)).reshape(-1, 128)
    for axis in ("core", "seq", "x", "z"):
        if direct and axis == "x":
            vector_rows = lax.optimization_barrier((late, vector_rows))[1]
        vector_rows = xor_sum(vector_rows, axis)
    vector_grad = vector_rows.reshape(-1)[: vector_local.shape[0]]

    in_grad = jnp.concatenate([gate_sum, mixed_sum[:, :CONVCH]], axis=1)
    dt_grad = mixed_sum[:, CONVCH : CONVCH + HEADS]

    gate_tiles = kron_tiles(gate_sum, in_left, in_right, in_left_root, in_right_root, 0, 6)
    in_update, in_left_new, in_right_new = kron_tiles(
        mixed_sum[:, :CONVCH], in_left, in_right, in_left_root, in_right_root, DI // COL_BLOCK, 7,
        gate_tiles,
    )
    dt_update, dt_left_wide, dt_right_wide = kron_update(
        dt_grad, dt_left[:, None], dt_right[:, None], dt_left_root[:, None], dt_right_root[:, None]
    )
    out_update, out_left_new, out_right_new = kron_tiles(
        out_grad, out_left, out_right, out_left_root, out_right_root, 0, 3
    )
    vector_moment_new = 0.5 * vector_moment + 0.5 * vector_grad * vector_grad
    vector_update = -LR_VEC * vector_grad * lax.rsqrt(vector_moment_new)
    return (
        block_output,
        input_grad,
        in_grad,
        dt_grad,
        out_grad,
        in_update,
        dt_update,
        out_update,
        in_left_new,
        in_right_new,
        dt_left_wide[:, 0],
        dt_right_wide[:, 0],
        out_left_new,
        out_right_new,
        vector_grad,
        vector_moment_new,
        vector_update,
    )


def solution(mesh):
    dp, seq = mesh.shape["dp"], mesh.shape["seq"]
    split = (4, dp // 8, 2)
    torus = jax.sharding.Mesh(mesh.devices.reshape(split + (seq,)), AXES + ("seq",))
    tokens = P(AXES, "seq", None)
    rows = P(AXES, None)
    tri = P(AXES, None, None)
    quad = P(AXES, None, None, None)
    placed = (
        (tokens, tokens, rows, rows, rows) + (P(),) * 7 + (quad,) * 4 + (tri,) * 4 + (quad,) * 4 + (P(),)
    )

    return jax.shard_map(
        body,
        mesh=torus,
        in_specs=placed,
        out_specs=(tokens, tokens)
        + (rows,) * 6
        + (quad, quad, tri, tri, quad, quad)
        + (P(), P(), P()),
        check_vma=False,
    )
```

```python
import functools

import jax
import jax.numpy as jnp
from jax import lax
from jax.experimental import pallas as pl
from jax.experimental.pallas import tpu as pltpu
from jax.sharding import PartitionSpec as P


D = 768
HEADS = 24
HEADDIM = 64
DSTATE = 128
KCONV = 4
DI = 1536
CONVCH = 1792
WIDE = CONVCH + 128
ROW_BLOCK = 24
COL_BLOCK = 128

BL = 128
PAIRS = HEADS // 2

AXES = ("z", "x", "core")

EPS = 1e-05
LR = 0.25
LR_VEC = 0.02
NEG = -1e30
LOG2E = 1.4426950408889634
BF = jnp.bfloat16
F32 = jnp.float32
NN = (((1,), (0,)), ((), ()))
NT = (((1,), (1,)), ((), ()))
TN = (((0,), (0,)), ((), ()))


def dot(a, b, dims=NN):
    return lax.dot_general(a, b, dims, preferred_element_type=F32)


def split2(v):
    high = v.astype(BF)
    return high, (v - high.astype(F32)).astype(BF)


def dot3(a, b, dims=NN):
    ah, al = split2(a)
    bh, bl = split2(b)
    return dot(ah, bh, dims) + dot(al, bh, dims) + dot(ah, bl, dims)


def pack(v):
    high = v.astype(BF).astype(F32)
    rest = v - high
    mid = rest.astype(BF).astype(F32)
    low = rest - mid
    return (high + pltpu.roll(mid, 32, 1) + pltpu.roll(low, 64, 1)).astype(BF)


def head_lanes(shape):
    return lax.broadcasted_iota(jnp.int32, shape, 1) < HEADS


def prefix(tri, v):
    parts = dot(tri, pack(v))
    total = parts + pltpu.roll(parts, 96, 1) + pltpu.roll(parts, 64, 1)
    return jnp.where(head_lanes(total.shape), total, 0.0)


def expand(v, emat):
    return dot(pack(v), emat)


def head_sum(v, gather):
    high, low = split2(v)
    return dot(high, gather) + dot(low, gather)


def tri_mask(lower):
    rows = lax.broadcasted_iota(jnp.int32, (BL, BL), 0)
    cols = lax.broadcasted_iota(jnp.int32, (BL, BL), 1)
    return (rows >= cols) if lower else (cols >= rows)


def softplus(v):
    return jnp.maximum(v, 0.0) + jnp.log1p(jnp.exp(-jnp.abs(v)))


def sigmoid(v):
    return 0.5 * jnp.tanh(0.5 * v) + 0.5


def silu(v):
    half = 0.5 * v
    return half * jnp.tanh(half) + half


def silu_parts(v):
    half = 0.5 * v
    curve = jnp.tanh(half)
    return half * curve + half, 0.5 * curve + 0.5


def rates(alog_ref):
    rate = -jnp.exp(alog_ref[0:1, :])
    return jnp.where(head_lanes(rate.shape), rate, 0.0)


def pair_masks():
    left = lax.broadcasted_iota(jnp.int32, (BL, BL), 1) < HEADDIM
    first = jnp.where(left, 1.0, 0.0)
    return first.astype(BF), (1.0 - first).astype(BF)


def pair_blocks(v, masks):
    return jnp.concatenate([v * masks[0], v * masks[1]], axis=0)


def norm_rows(u, gain):
    inv = lax.rsqrt(jnp.mean(u * u, axis=-1, keepdims=True) + EPS)
    return u * inv * gain


def first_kernel(
    u_ref, halo_ref, gain_ref, w_ref, cw_ref, cb_ref, dtb_ref, alog_ref, emat_ref,
    normed_ref, mixed_ref, pre_ref, z_ref, state_ref, total_ref,
    tail, full,
):
    step_index = pl.program_id(1)
    tile = u_ref.shape[1]
    gain = gain_ref[0:1, :]

    @pl.when(step_index == 0)
    def _():
        near = norm_rows(halo_ref[0].astype(F32), gain).astype(BF)
        tail[...] = dot(near, w_ref[:, :CONVCH]).astype(BF).astype(F32)
        state_ref[...] = jnp.zeros_like(state_ref)
        total_ref[...] = jnp.zeros_like(total_ref)

    normed = norm_rows(u_ref[0].astype(F32), gain).astype(BF)
    normed_ref[0] = normed
    projected = dot(normed, w_ref[...])
    mixed_low = projected[:, :CONVCH].astype(BF)
    mixed_ref[0] = mixed_low
    mixed = mixed_low.astype(F32)
    z = projected[:, CONVCH:].astype(BF).astype(F32) + dtb_ref[0:1, :]
    z_ref[0] = z
    for low in range(0, CONVCH, 256):
        cols = slice(low, low + 256)
        own = mixed[:, cols]
        joined = jnp.concatenate([tail[:, cols], own], axis=0)
        pre = cb_ref[0:1, cols] + cw_ref[KCONV - 1 : KCONV, cols] * own
        for tap in range(KCONV - 1):
            moved = pltpu.roll(joined, KCONV - 1 - tap, 0)[8:, :]
            pre = pre + cw_ref[tap : tap + 1, cols] * moved
        pre_ref[0, :, cols] = pre
        full[:, cols] = silu(pre)
    tail[...] = mixed[tile - 8 :, :]
    rate = rates(alog_ref)

    step_all = softplus(z)
    tri = jnp.where(tri_mask(True), 1.0, 0.0).astype(BF)
    emat = emat_ref[...]
    for part in range(tile // BL):
        rows = slice(part * BL, (part + 1) * BL)
        step = step_all[rows]
        cum = prefix(tri, step * rate)
        last = cum[BL - 1 : BL, :]
        weights = expand(jnp.exp(last - cum) * step, emat)
        decay = expand(
            jnp.where(head_lanes((8, 128)), jnp.broadcast_to(jnp.exp(last), (8, 128)), 0.0), emat
        )[0:1, :]
        fresh = dot3(full[rows, DI : DI + DSTATE].T, weights * full[rows, :DI])
        state_ref[0] = state_ref[0] * decay + fresh
        total_ref[0] = total_ref[0] + jnp.broadcast_to(last, (8, 128))


def dot_wide(ahl, ah, bh, bl):
    return dot(ahl, jnp.concatenate([bh, bh], axis=0)) + dot(ah, bl)


def dot3_split(a, b, dims):
    (ah, al), (bh, bl) = a, b
    return dot(ah, bh, dims) + dot(al, bh, dims) + dot(ah, bl, dims)


def wide_split(v):
    high, low = split2(v)
    return jnp.concatenate([high, low], axis=1), high


def rows8(v):
    return jnp.sum(v.reshape(v.shape[0] // 8, 8, v.shape[1]), axis=0)


def pair_values(pair, cum, cum_t, step, mask, left, transposed):
    kernels, columns = [], []
    for h in (2 * pair, 2 * pair + 1):
        column = jnp.broadcast_to(cum[:, h : h + 1], (BL, BL))
        row = cum_t[h : h + 1, :]
        spread = (row - column) if transposed else (column - row)
        kernels.append(jnp.exp2(jnp.where(mask, spread, NEG)))
        columns.append(column)
    chosen = jnp.where(left, columns[0], columns[1])
    steps = jnp.where(left, step[:, 2 * pair : 2 * pair + 1], step[:, 2 * pair + 1 : 2 * pair + 2])
    return kernels, chosen, steps


def lane_sum(v):
    return jnp.sum(v, axis=1, keepdims=True)


def second_kernel(
    pre_ref, z_ref, normed_ref, up_ref, u_ref, enter_ref, wg_ref, wo_ref, skip_ref, ggain_ref, alog_ref,
    gmat_ref,
    out_ref, branch_ref, dy_ref, ggrad_ref, state_ref, rdot_ref, dstate_ref, sums_ref,
    gain_acc, skip_acc, state, running, ys, es, xs_ref, ss_ref, sl_ref, sg_ref, up_scratch,
):
    step_index = pl.program_id(1)
    tile = pre_ref.shape[1]

    @pl.when(step_index == 0)
    def _():
        state[...] = enter_ref[0]
        running[...] = jnp.ones_like(running)
        dstate_ref[...] = jnp.zeros_like(dstate_ref)

    @pl.when((step_index == 0) & (pl.program_id(0) == 0))
    def _():
        gain_acc[...] = jnp.zeros_like(gain_acc)
        skip_acc[...] = jnp.zeros_like(skip_acc)

    rate = rates(alog_ref)

    def block(part, carry):
        rows = pl.ds(pl.multiple_of(part * BL, BL), BL)
        mask = tri_mask(True)
        left = lax.broadcasted_iota(jnp.int32, (BL, BL), 1) < HEADDIM
        masks = pair_masks()
        tri = jnp.where(mask, 1.0, 0.0).astype(BF)
        conv = silu(pre_ref[0, rows, DI:])
        inputs_b, inputs_c = conv[:, :DSTATE], conv[:, DSTATE:]
        step = softplus(z_ref[0, rows, :])
        cum = prefix(tri, step * (rate * LOG2E))
        cum_t = cum.T
        scores = dot3(inputs_c, inputs_b, NT)
        c_wide, c_high = wide_split(inputs_c)
        bt_wide, bt_high = wide_split(inputs_b.T)
        ct_wide, ct_high = wide_split(inputs_c.T)
        squares = jnp.zeros((BL, 128), F32)
        products = jnp.zeros((BL, 128), F32)
        for quad in range(PAIRS // 2):
            cols = slice(quad * 256, (quad + 1) * 256)
            inner, grown, weighted, xs = [], [], [], []
            for pair in (2 * quad, 2 * quad + 1):
                kernels, chosen, steps = pair_values(pair, cum, cum_t, step, mask, left, False)
                x = silu(pre_ref[0, rows, pair * 128 : (pair + 1) * 128])
                scaled = steps * x
                mh, ml = split2(jnp.concatenate([scores * k for k in kernels], axis=1))
                rh, rl = (pair_blocks(v, masks) for v in split2(scaled))
                inner.append(dot(mh, rh) + dot(ml, rh) + dot(mh, rl))
                grown.append(jnp.exp2(chosen))
                weighted.append(jnp.exp2(chosen[BL - 1 : BL, :] - chosen) * scaled)
                xs.append(x)
            inner, grown, weighted, x = (
                jnp.concatenate(v, axis=1) for v in (inner, grown, weighted, xs)
            )
            held = state[:, cols]
            state_ref[0, part, :, cols] = held
            yhat = inner + grown * dot_wide(c_wide, c_high, *split2(held))
            state[:, cols] = held * grown[BL - 1 : BL, :] + dot_wide(
                bt_wide, bt_high, *split2(weighted)
            )
            ys[:, cols] = yhat
            es[:, cols] = grown
            states = (yhat + skip_ref[0:1, cols] * x).astype(BF).astype(F32)
            sl, sg = silu_parts(dot(normed_ref[0, rows, :], wg_ref[:, cols]))
            upstream = dot(up_ref[rows, :], wo_ref[cols, :], NT)
            up_scratch[:, cols] = upstream
            gated = states * sl
            xs_ref[:, cols] = x
            ss_ref[:, cols] = states
            sl_ref[:, cols] = sl
            sg_ref[:, cols] = sg
            product = gated * (upstream * ggain_ref[0:1, cols])
            squared = gated * gated
            squares = squares + squared[:, :128] + squared[:, 128:]
            products = products + product[:, :128] + product[:, 128:]
        inv = lax.rsqrt(lane_sum(squares) * (1.0 / DI) + EPS)
        pull = jnp.broadcast_to(inv * inv * lane_sum(products) * (1.0 / DI), (BL, 128))
        inv = jnp.broadcast_to(inv, (BL, 128))
        rdot = jnp.zeros((BL, 128), F32)
        for quad in range(PAIRS // 2):
            cols = slice(quad * 256, (quad + 1) * 256)
            scaled_dy, dot_terms = [], []
            for pair in (2 * quad, 2 * quad + 1):
                own_cols = slice(pair * 128, (pair + 1) * 128)
                x = xs_ref[:, own_cols]
                yhat = ys[:, own_cols]
                states = ss_ref[:, own_cols]
                sl, sg = sl_ref[:, own_cols], sg_ref[:, own_cols]
                gated = states * sl
                gain = ggain_ref[0:1, own_cols]
                upstream = up_scratch[:, own_cols]
                norm = gated * inv
                branch_ref[rows, own_cols] = (norm * gain).astype(BF)
                gain_acc[:, own_cols] += rows8(upstream * norm)
                dgated = inv * (upstream * gain - gated * pull)
                dy_low = (dgated * sl).astype(BF)
                dy_ref[rows, own_cols] = dy_low
                ggrad_ref[rows, own_cols] = (dgated * states * (sg + sl * (1.0 - sg))).astype(BF)
                dy = dy_low.astype(F32)
                skip_acc[:, own_cols] += rows8(dy * x)
                dot_terms.append(dy * yhat)
                scaled_dy.append(es[:, own_cols] * running[0:1, own_cols] * dy)
            rdot = rdot + head_sum(jnp.concatenate(dot_terms, axis=1), gmat_ref[cols, :])
            dstate_ref[0, :, cols] += dot_wide(
                ct_wide, ct_high, *split2(jnp.concatenate(scaled_dy, axis=1))
            )
            running[:, cols] = running[:, cols] * es[BL - 1 : BL, cols]
        rdot_ref[0, rows, :] = rdot
        return carry

    lax.fori_loop(0, tile // BL, block, 0)
    out_ref[0] = (u_ref[0].astype(F32) + dot(branch_ref[...], wo_ref[...])).astype(BF)

    @pl.when((step_index == pl.num_programs(1) - 1) & (pl.program_id(0) == pl.num_programs(0) - 1))
    def _():
        sums_ref[0:1, :] = jnp.sum(gain_acc[...], axis=0, keepdims=True)
        sums_ref[1:2, :] = jnp.sum(skip_acc[...], axis=0, keepdims=True)


def third_kernel(
    pre_ref, mixed_ref, z_ref, dy_ref, state_ref, rdot_ref, leave_ref, cw_ref, skip_ref, alog_ref,
    gmat_ref,
    mgrad_ref, last_ref, first_ref, sums_ref,
    cw_acc, cb_acc, dtb_acc, rate_acc, dstate, tail,
):
    step_index = pl.program_id(1)

    @pl.when(step_index == 0)
    def _():
        dstate[...] = leave_ref[0]
        tail[...] = jnp.zeros_like(tail)

    @pl.when((step_index == 0) & (pl.program_id(0) == 0))
    def _():
        for ref in (cw_acc, cb_acc, dtb_acc, rate_acc):
            ref[...] = jnp.zeros_like(ref)

    rate = rates(alog_ref)
    mask = tri_mask(False)
    left = lax.broadcasted_iota(jnp.int32, (BL, BL), 1) < HEADDIM
    masks = pair_masks()
    low_tri = jnp.where(tri_mask(True), 1.0, 0.0).astype(BF)
    high_tri = jnp.where(mask, 1.0, 0.0).astype(BF)
    wide_pre = pre_ref[0, :, DI:]
    conv, wide_sg = silu_parts(wide_pre)
    inputs_b, inputs_c = conv[:, :DSTATE], conv[:, DSTATE:]
    z = z_ref[0]
    step = softplus(z)
    cum = prefix(low_tri, step * (rate * LOG2E))
    cum_t = cum.T
    lanes = head_lanes(cum.shape)
    scores_t = dot3(inputs_b, inputs_c, NT)
    b_wide, b_high = wide_split(inputs_b)
    ct_wide, ct_high = wide_split(inputs_c.T)
    dscores_t = jnp.zeros((BL, BL), F32)
    db = jnp.zeros((BL, DSTATE), F32)
    dc = jnp.zeros((BL, DSTATE), F32)
    sums = jnp.zeros((BL + 8, 128), F32)

    def back_conv(cols, dpre):
        joined = jnp.concatenate([dpre, tail[:, cols]], axis=0)
        tail[:, cols] = dpre[0:8, :]
        mixed = mixed_ref[0, :, cols].astype(F32)
        cb_acc[:, cols] += rows8(dpre)
        mgrad = cw_ref[KCONV - 1 : KCONV, cols] * dpre
        cw_acc[KCONV - 1, :, cols] += rows8(dpre * mixed)
        for tap in range(KCONV - 1):
            moved = pltpu.roll(joined, BL + 8 - (KCONV - 1 - tap), 0)[:BL, :]
            mgrad = mgrad + cw_ref[tap : tap + 1, cols] * moved
            cw_acc[tap, :, cols] += rows8(moved * mixed)
        mgrad_ref[0, :, cols] = mgrad.astype(BF)
        last_ref[0, :, cols] = jnp.where(step_index == 0, mgrad[BL - 8 :, :], last_ref[0, :, cols])

    for quad in range(PAIRS // 2):
        cols = slice(quad * 256, (quad + 1) * 256)
        inner, grown, shrink, scaled, xs, steps_wide, slopes = [], [], [], [], [], [], []
        dy = dy_ref[:, cols].astype(F32)
        for pair in (2 * quad, 2 * quad + 1):
            kernels, chosen, steps = pair_values(pair, cum, cum_t, step, mask, left, True)
            own = pre_ref[0, :, pair * 128 : (pair + 1) * 128]
            x, sg = silu_parts(own)
            slopes.append(sg + x * (1.0 - sg))
            xd = steps * x
            mh, ml = split2(jnp.concatenate([scores_t * k for k in kernels], axis=1))
            dyb = pair_blocks(dy_ref[:, pair * 128 : (pair + 1) * 128], masks)
            inner.append(dot(mh, dyb) + dot(ml, dyb))
            sh, sl = split2(xd)
            dmix = dot(sh, dyb, NT) + dot(sl, dyb, NT)
            dscores_t = dscores_t + dmix[:, :BL] * kernels[0] + dmix[:, BL:] * kernels[1]
            grown.append(jnp.exp2(chosen))
            shrink.append(jnp.exp2(chosen[BL - 1 : BL, :] - chosen))
            scaled.append(xd)
            xs.append(x)
            steps_wide.append(steps)
        inner, grown, shrink, scaled, x, steps_wide, slopes = (
            jnp.concatenate(v, axis=1) for v in (inner, grown, shrink, scaled, xs, steps_wide, slopes)
        )
        held = state_ref[0, 0, :, cols]
        ds = dstate[:, cols]
        held_parts, ds_parts = split2(held), split2(ds)
        decay = grown[BL - 1 : BL, :]
        dscaled_state = shrink * dot_wide(b_wide, b_high, *ds_parts)
        dscaled = inner + dscaled_state
        ends = jnp.sum(scaled * dscaled_state, axis=0, keepdims=True) + decay * jnp.sum(
            held * ds, axis=0, keepdims=True
        )
        sums = sums + head_sum(
            jnp.concatenate([x * dscaled, jnp.broadcast_to(ends, (8, 256))], axis=0),
            gmat_ref[cols, :],
        )
        grown_parts = split2(grown * dy)
        dc = dc + dot3_split(grown_parts, held_parts, NT)
        db = db + dot3_split(split2(shrink * scaled), ds_parts, NT)
        dstate[:, cols] = decay * ds + dot_wide(ct_wide, ct_high, *grown_parts)
        back_conv(cols, (steps_wide * dscaled + skip_ref[0:1, cols] * dy) * slopes)

    direct = sums[:BL]
    is_last = lax.broadcasted_iota(jnp.int32, (BL, 128), 0) == BL - 1
    dcum = rdot_ref[0] - step * direct + jnp.where(is_last, sums[BL : BL + 1, :], 0.0)
    dcum = jnp.where(lanes, dcum, 0.0)
    drate = prefix(high_tri, dcum)
    dz = (rate * drate + direct) * sigmoid(z)
    mgrad_ref[0, :, CONVCH:] = dz.astype(BF)
    dtb_acc[...] += rows8(dz)
    rate_acc[...] += rows8(step * drate)
    db = db + dot3(dscores_t, inputs_c)
    dc = dc + dot3(dscores_t.T, inputs_b)
    back_conv(
        slice(DI, CONVCH),
        jnp.concatenate([db, dc], axis=1) * (wide_sg + conv * (1.0 - wide_sg)),
    )
    first_ref[0] = tail[...]

    @pl.when((step_index == pl.num_programs(1) - 1) & (pl.program_id(0) == pl.num_programs(0) - 1))
    def _():
        for tap in range(KCONV):
            sums_ref[tap : tap + 1, :] = jnp.sum(cw_acc[tap], axis=0, keepdims=True)
        sums_ref[4:5, :] = jnp.sum(cb_acc[...], axis=0, keepdims=True)
        sums_ref[5:6, :128] = jnp.sum(dtb_acc[...], axis=0, keepdims=True)
        sums_ref[6:7, :128] = jnp.sum(rate_acc[...], axis=0, keepdims=True)


def patch_kernel(mgrad_ref, mixed_ref, last_ref, near_ref, cw_ref, out_ref, extra_ref):
    @pl.when(pl.program_id(0) == 0)
    def _():
        extra_ref[...] = jnp.zeros_like(extra_ref)

    rows = [last_ref[0, i : i + 1, :] for i in range(8)]
    near = [near_ref[0, i : i + 1, :] for i in range(KCONV - 1)]
    held = mixed_ref[0].astype(F32)
    first = 8 - (KCONV - 1)
    for k in range(KCONV - 1):
        for j in range(k, KCONV - 1):
            rows[first + j] = rows[first + j] + cw_ref[k : k + 1, :] * near[j - k]
            extra_ref[k : k + 1, :] += near[j - k] * held[8 + first + j : 9 + first + j, :]
    old = mgrad_ref[0].astype(F32)
    patched = jnp.concatenate([old[:8, :CONVCH], jnp.concatenate(rows, axis=0)], axis=0)
    out_ref[0, :, :CONVCH] = patched.astype(BF)
    out_ref[0, :, CONVCH:] = mgrad_ref[0, :, CONVCH:]


PARAMS = dict(vmem_limit_bytes=60 * 1024 * 1024)


def whole(shape):
    zeros = (0,) * len(shape)
    return pl.BlockSpec(shape, lambda b, i: zeros)


def run_first(u, halo, gain, w, cw, cb, dtb, alog, emat):
    seqs, length, _ = u.shape
    tile = min(256, length)
    grid = (seqs, length // tile)
    tok = lambda width: pl.BlockSpec((1, tile, width), lambda b, i: (b, i, 0))
    per = lambda *shape: pl.BlockSpec((1,) + shape, lambda b, i: (b,) + (0,) * len(shape))
    return pl.pallas_call(
        first_kernel,
        grid=grid,
        in_specs=[
            tok(D), per(8, D), whole(gain.shape), whole(w.shape),
            whole(cw.shape), whole(cb.shape), whole(dtb.shape), whole(alog.shape), whole(emat.shape),
        ],
        out_specs=[
            tok(D), tok(CONVCH), tok(CONVCH), tok(128), per(DSTATE, DI), per(8, 128),
        ],
        out_shape=[
            jax.ShapeDtypeStruct((seqs, length, D), BF),
            jax.ShapeDtypeStruct((seqs, length, CONVCH), BF),
            jax.ShapeDtypeStruct((seqs, length, CONVCH), F32),
            jax.ShapeDtypeStruct((seqs, length, 128), F32),
            jax.ShapeDtypeStruct((seqs, DSTATE, DI), F32),
            jax.ShapeDtypeStruct((seqs, 8, 128), F32),
        ],
        scratch_shapes=[pltpu.VMEM((8, CONVCH), F32), pltpu.VMEM((tile, CONVCH), F32)],
        compiler_params=pltpu.CompilerParams(**PARAMS),
        name="first",
    )(u, halo, gain, w, cw, cb, dtb, alog, emat)


def run_second(pre, z, normed, up, u, enter, wg, wo, skip, ggain, alog, gmat):
    seqs, length, _ = u.shape
    tile = min(256, length)
    steps = length // tile
    parts = tile // BL
    grid = (seqs, steps)
    tok = lambda width: pl.BlockSpec((1, tile, width), lambda b, i: (b, i, 0))
    flat = lambda width: pl.BlockSpec((tile, width), lambda b, i: (b * steps + i, 0))
    per = lambda *shape: pl.BlockSpec((1,) + shape, lambda b, i: (b,) + (0,) * len(shape))
    rows = seqs * length
    return pl.pallas_call(
        second_kernel,
        grid=grid,
        in_specs=[
            tok(CONVCH), tok(128), tok(D), flat(D), tok(D), per(DSTATE, DI), whole(wg.shape),
            whole(wo.shape),
            whole(skip.shape), whole(ggain.shape), whole(alog.shape), whole(gmat.shape),
        ],
        out_specs=[
            tok(D), flat(DI), flat(DI), flat(DI),
            pl.BlockSpec((1, parts, DSTATE, DI), lambda b, i: (b, i, 0, 0)),
            tok(128), per(DSTATE, DI), whole((8, DI)),
        ],
        out_shape=[
            jax.ShapeDtypeStruct((seqs, length, D), BF),
            jax.ShapeDtypeStruct((rows, DI), BF),
            jax.ShapeDtypeStruct((rows, DI), BF),
            jax.ShapeDtypeStruct((rows, DI), BF),
            jax.ShapeDtypeStruct((seqs, length // BL, DSTATE, DI), F32),
            jax.ShapeDtypeStruct((seqs, length, 128), F32),
            jax.ShapeDtypeStruct((seqs, DSTATE, DI), F32),
            jax.ShapeDtypeStruct((8, DI), F32),
        ],
        scratch_shapes=[
            pltpu.VMEM((8, DI), F32), pltpu.VMEM((8, DI), F32), pltpu.VMEM((DSTATE, DI), F32),
            pltpu.VMEM((8, DI), F32), *[pltpu.VMEM((BL, DI), F32)] * 7,
        ],
        compiler_params=pltpu.CompilerParams(**PARAMS),
        name="second",
    )(pre, z, normed, up, u, enter, wg, wo, skip, ggain, alog, gmat)


def run_third(pre, mixed, z, dy, states, rdot, leave, cw, skip, alog, gmat):
    seqs, length, _ = pre.shape
    steps = length // BL
    grid = (seqs, steps)
    tok = lambda width: pl.BlockSpec((1, BL, width), lambda b, i: (b, steps - 1 - i, 0))
    per = lambda *shape: pl.BlockSpec((1,) + shape, lambda b, i: (b,) + (0,) * len(shape))
    return pl.pallas_call(
        third_kernel,
        grid=grid,
        in_specs=[
            tok(CONVCH), tok(CONVCH), tok(128),
            pl.BlockSpec((BL, DI), lambda b, i: (b * steps + steps - 1 - i, 0)),
            pl.BlockSpec((1, 1, DSTATE, DI), lambda b, i: (b, steps - 1 - i, 0, 0)),
            tok(128), per(DSTATE, DI), whole(cw.shape), whole(skip.shape), whole(alog.shape),
            whole(gmat.shape),
        ],
        out_specs=[
            tok(WIDE), per(8, CONVCH), per(8, CONVCH), whole((8, CONVCH)),
        ],
        out_shape=[
            jax.ShapeDtypeStruct((seqs, length, WIDE), BF),
            jax.ShapeDtypeStruct((seqs, 8, CONVCH), F32),
            jax.ShapeDtypeStruct((seqs, 8, CONVCH), F32),
            jax.ShapeDtypeStruct((8, CONVCH), F32),
        ],
        scratch_shapes=[
            pltpu.VMEM((KCONV, 8, CONVCH), F32), pltpu.VMEM((8, CONVCH), F32),
            pltpu.VMEM((8, 128), F32), pltpu.VMEM((8, 128), F32),
            pltpu.VMEM((DSTATE, DI), F32), pltpu.VMEM((8, CONVCH), F32),
        ],
        compiler_params=pltpu.CompilerParams(**PARAMS),
        name="third",
    )(pre, mixed, z, dy, states, rdot, leave, cw, skip, alog, gmat)


def run_patch(mgrad, mixed, last8, near, cw):
    seqs, length, _ = mgrad.shape
    end = length // 16 - 1
    tok = lambda width: pl.BlockSpec((1, 16, width), lambda b: (b, end, 0))
    per = pl.BlockSpec((1, 8, CONVCH), lambda b: (b, 0, 0))
    row = pl.BlockSpec((8, CONVCH), lambda b: (0, 0))
    taps = pl.BlockSpec(cw.shape, lambda b: (0, 0))
    return pl.pallas_call(
        patch_kernel,
        grid=(seqs,),
        in_specs=[tok(WIDE), tok(CONVCH), per, per, taps],
        out_specs=[tok(WIDE), row],
        out_shape=[
            jax.ShapeDtypeStruct(mgrad.shape, BF),
            jax.ShapeDtypeStruct((8, CONVCH), F32),
        ],
        input_output_aliases={0: 0},
        name="patch",
    )(mgrad, mixed, last8, near, cw)


def kron_update(gradient, left_stat, right_stat, left_root, right_root):
    row_tiles, col_tiles = (left_stat.shape[0], left_stat.shape[1])
    row_size, col_size = (left_stat.shape[-1], right_stat.shape[-1])
    grad_tiles = gradient.reshape(row_tiles, row_size, col_tiles, col_size).transpose(0, 2, 1, 3)
    left_new = 0.5 * left_stat + 0.5 * jnp.einsum(
        "abij,abkj->abik", grad_tiles, grad_tiles, precision=lax.Precision.HIGH
    )
    right_new = 0.5 * right_stat + 0.5 * jnp.einsum(
        "abji,abjk->abik", grad_tiles, grad_tiles, precision=lax.Precision.HIGH
    )
    shaped = jnp.einsum("abij,abjk->abik", left_root, grad_tiles, precision=lax.Precision.HIGH)
    shaped = jnp.einsum("abij,abjk->abik", shaped, right_root, precision=lax.Precision.HIGH)
    update = (-LR * shaped).transpose(0, 2, 1, 3).reshape(gradient.shape)
    return (update, left_new, right_new)


def float_parts(v):
    high = v.astype(BF).astype(F32)
    return high, v - high


def kron_kernel(*refs, unroll):
    grad_ref, left_ref, right_ref, left_root_ref, right_root_ref = refs[:5]
    update_ref, left_new_ref, right_new_ref = refs[-3:]

    def column(c, carry):
        cols = pl.ds(pl.multiple_of(c * COL_BLOCK, COL_BLOCK), COL_BLOCK)
        for r in range(left_ref.shape[0]):
            rows = slice(r * ROW_BLOCK, (r + 1) * ROW_BLOCK)
            grad = grad_ref[rows, cols]
            high, low = float_parts(grad)
            root_high, root_low = float_parts(left_root_ref[r, c])
            below = jnp.concatenate([high, high, low], axis=0).astype(BF)
            right = dot(jnp.concatenate([high, low, high], axis=0).astype(BF), below, TN)
            rooted = dot(
                jnp.concatenate([root_high, root_low, root_high], axis=0).astype(BF), below, TN
            )
            high, low = high.astype(BF), low.astype(BF)
            left = dot(
                jnp.concatenate([high, low], axis=1), jnp.concatenate([high, high], axis=1), NT
            ) + dot(high, low, NT)
            left_new_ref[r, c] = 0.5 * left_ref[r, c] + 0.5 * left
            right_new_ref[r, c] = 0.5 * right_ref[r, c] + 0.5 * right
            shaped = dot_wide(*wide_split(rooted), *split2(right_root_ref[r, c]))
            update_ref[rows, cols] = -LR * shaped
        return carry

    lax.fori_loop(0, left_ref.shape[1], column, 0, unroll=unroll)


def kron_tiles(grad, left, right, left_root, right_root, first, step, earlier=None):
    row_tiles = left.shape[0]
    rows, cols = grad.shape
    stat = lambda size: pl.BlockSpec(
        tuple(pl.Element(n) for n in (row_tiles, step, size, size)),
        lambda i: (0, first + step * i, 0, 0),
    )
    wide = step * COL_BLOCK
    ins = [grad, left, right, left_root, right_root]
    in_specs = [pl.BlockSpec((rows, wide), lambda i: (0, i))] + [stat(ROW_BLOCK), stat(COL_BLOCK)] * 2
    aliases = {}
    if earlier is not None:
        ins += list(earlier)
        in_specs += [pl.BlockSpec(memory_space=pl.ANY)] * 3
        aliases = {5: 0, 6: 1, 7: 2}
    total = left.shape[1] * COL_BLOCK
    return pl.pallas_call(
        functools.partial(kron_kernel, unroll=max(1, 4 // row_tiles)),
        grid=(cols // wide,),
        in_specs=in_specs,
        out_specs=[
            pl.BlockSpec(
                (pl.Element(rows), pl.Element(wide)),
                lambda i: (0, pl.multiple_of(first * COL_BLOCK + wide * i, COL_BLOCK)),
            ),
            stat(ROW_BLOCK), stat(COL_BLOCK),
        ],
        out_shape=[
            jax.ShapeDtypeStruct((rows, total), F32),
            jax.ShapeDtypeStruct(left.shape, F32),
            jax.ShapeDtypeStruct(right.shape, F32),
        ],
        input_output_aliases=aliases,
        compiler_params=pltpu.CompilerParams(**PARAMS),
        name="kron",
    )(*ins)


def back_kernel(
    ggrad_ref, mgrad_ref, wg_ref, main_ref, u_ref, up_ref, gain_ref, out_ref, gain_grad_ref
):
    @pl.when(pl.program_id(0) == 0)
    def _():
        gain_grad_ref[...] = jnp.zeros_like(gain_grad_ref)

    grad = dot(ggrad_ref[...], wg_ref[...], NT) + dot(mgrad_ref[...], main_ref[...], NT)
    u = u_ref[...].astype(F32)
    inv = lax.rsqrt(jnp.mean(u * u, axis=-1, keepdims=True) + EPS)
    norm = u * inv
    gain_grad_ref[...] += rows8(grad * norm)
    scaled = grad * gain_ref[0:1, :]
    pull = jnp.mean(scaled * norm, axis=-1, keepdims=True)
    out_ref[...] = up_ref[...].astype(F32) + inv * (scaled - norm * pull)


def run_back(ggrad, mgrad, wg, main, u, up, gain):
    rows = u.shape[0]
    tile = min(256, rows)
    tok = lambda width: pl.BlockSpec((tile, width), lambda i: (i, 0))
    return pl.pallas_call(
        back_kernel,
        grid=(rows // tile,),
        in_specs=[
            tok(DI), tok(WIDE), pl.BlockSpec(wg.shape, lambda i: (0, 0)),
            pl.BlockSpec(main.shape, lambda i: (0, 0)), tok(D), tok(D),
            pl.BlockSpec(gain.shape, lambda i: (0, 0)),
        ],
        out_specs=[tok(D), pl.BlockSpec((8, D), lambda i: (0, 0))],
        out_shape=[jax.ShapeDtypeStruct((rows, D), F32), jax.ShapeDtypeStruct((8, D), F32)],
        compiler_params=pltpu.CompilerParams(**PARAMS),
        name="back",
    )(ggrad, mgrad, wg, main, u, up, gain)


def swapped(v, axis, size, offset):
    return lax.ppermute(v, axis, [(i, (i + offset) % size) for i in range(size)])


def pick(v, index):
    return lax.dynamic_index_in_dim(v, index, 0, keepdims=False)


def scatter_stage(v, axis, kind=BF):
    size = lax.axis_size(axis)
    here = lax.axis_index(axis)
    total = pick(v, here)
    for offset in range(1, size):
        sent = pick(v, lax.rem(here + offset, size)).astype(kind)
        total = total + swapped(sent, axis, size, offset).astype(F32)
    return total


def gather_stage(v, axis):
    size = lax.axis_size(axis)
    here = lax.axis_index(axis)
    out = jnp.zeros((size,) + v.shape, v.dtype)
    out = lax.dynamic_update_index_in_dim(out, v, here, 0)
    for offset in range(1, size):
        got = swapped(v, axis, size, offset)
        out = lax.dynamic_update_index_in_dim(out, got, lax.rem(here - offset + size, size), 0)
    return out


def core_sum(partial):
    z, x, core = (lax.axis_size(a) for a in ("z", "x", "core"))
    rows, cols = partial.shape
    blocks = partial.reshape(z, x, core, rows // (z * x * core), cols)
    return scatter_stage(jnp.moveaxis(blocks, 2, 0), "core", F32)


def across(v):
    return scatter_stage(scatter_stage(jnp.moveaxis(v, 1, 0), "x"), "z")


def reduce_plain(v):
    owned = across(v)
    total = owned
    size = lax.axis_size("seq")
    if size > 2:
        return lax.psum(owned, "seq")
    for offset in range(1, size):
        total = total + swapped(owned, "seq", size, offset)
    return total


def reduce_split(v):
    size = lax.axis_size("seq")
    z, x, rows, cols = v.shape
    if cols % (128 * size):
        return reduce_plain(v)
    v = jnp.moveaxis(v.reshape(z, x, rows, size, cols // size), 3, 0)
    owned = across(scatter_stage(v, "seq"))
    return jnp.moveaxis(gather_stage(owned, "seq"), 0, 1).reshape(rows, cols)


def xor_sum(v, axis):
    size = lax.axis_size(axis)
    bit = 1
    while bit < size:
        v = v + lax.ppermute(v, axis, [(i, i ^ bit) for i in range(size)])
        bit *= 2
    return v


STEP_OWNERS = 4


def chip_kernel(idx, *refs):
    send_ref, own_ref = refs[-2:]
    width = own_ref.shape[1]

    def one_owner(owner, carry):
        mine = pl.program_id(0) * STEP_OWNERS + owner == idx[0] * 2 + idx[1]
        row, col = 0, 0
        for part_ref, got_ref in zip(refs[:-2:2], refs[1:-2:2]):
            total = part_ref[owner, 0] + got_ref[owner]
            rows = total.shape[0] * total.shape[1] // width
            for low in range(0, total.shape[0], rows):
                piece = total[low : low + rows]
                at = (slice(row, row + rows), slice(col, col + piece.shape[1]))
                send_ref[(owner,) + at] = piece.astype(BF)

                @pl.when(mine)
                def _(at=at, piece=piece):
                    own_ref[at] = piece

                col += piece.shape[1]
                if col == width:
                    row, col = row + rows, 0
        return carry

    lax.fori_loop(0, STEP_OWNERS, one_owner, 0)


def chip_sum(idx, pairs):
    in_specs, ins, total, width = [], [], 0, 0
    for blocks, got in pairs:
        _, _, rows, cols = blocks.shape
        width = max(width, cols)
        total += rows * cols
        ins += [blocks, got]
        in_specs += [
            pl.BlockSpec((STEP_OWNERS, 1, rows, cols), lambda i, idx: (i, idx[2], 0, 0)),
            pl.BlockSpec((STEP_OWNERS, rows, cols), lambda i, idx: (i, 0, 0)),
        ]
    rows = total // width
    return pl.pallas_call(
        chip_kernel,
        grid_spec=pltpu.PrefetchScalarGridSpec(
            num_scalar_prefetch=1,
            grid=(8 // STEP_OWNERS,),
            in_specs=in_specs,
            out_specs=[
                pl.BlockSpec((STEP_OWNERS, rows, width), lambda i, idx: (i, 0, 0)),
                pl.BlockSpec((rows, width), lambda i, idx: (0, 0)),
            ],
        ),
        out_shape=[
            jax.ShapeDtypeStruct((8, rows, width), BF),
            jax.ShapeDtypeStruct((rows, width), F32),
        ],
        compiler_params=pltpu.CompilerParams(**PARAMS),
        name="chip_sum",
    )(idx, *ins)


def owner_kernel(idx, own_ref, got_ref, out_ref):
    mine = idx[0] * 2 + idx[1]
    total = own_ref[...]
    for i in range(8):
        total = total + jnp.where(mine == i, 0.0, got_ref[i].astype(F32))
    out_ref[...] = total


def owner_sum(idx, own, got):
    rows, width = own.shape
    tile = 48
    return pl.pallas_call(
        owner_kernel,
        grid_spec=pltpu.PrefetchScalarGridSpec(
            num_scalar_prefetch=1,
            grid=(rows // tile,),
            in_specs=[
                pl.BlockSpec((tile, width), lambda i, idx: (i, 0)),
                pl.BlockSpec((8, tile, width), lambda i, idx: (0, i, 0)),
            ],
            out_specs=pl.BlockSpec((tile, width), lambda i, idx: (i, 0)),
        ),
        out_shape=jax.ShapeDtypeStruct((rows, width), F32),
        name="owner_sum",
    )(idx, own, got)


def core_exchange(partial, core):
    rows, cols = partial.shape
    blocks = partial.reshape(8, 2, rows // 16, cols)
    sent = lax.dynamic_index_in_dim(blocks, 1 - core, 1, keepdims=False)
    return blocks, swapped(sent, "core", 2, 1)


def around(v, axis):
    size = lax.axis_size(axis)
    return jnp.stack([v] + [swapped(v, axis, size, offset) for offset in range(1, size)])


def assemble_kernel(idx, *refs, order):
    out_ref = refs[-1]
    sizes = {"z": 4, "x": 2}
    here = {"z": idx[0], "x": idx[1]}
    spots = ((idx[2], idx[3]), (idx[2], 1 - idx[3]), (1 - idx[2], idx[3]), (1 - idx[2], 1 - idx[3]))
    for ref, (core, seq) in zip(refs[:-1], spots):
        for a in range(ref.shape[0]):
            for b in range(ref.shape[1]):
                at = dict(
                    (axis, lax.rem(here[axis] - back + sizes[axis], sizes[axis]))
                    for axis, back in zip(order[::-1], (a, b))
                )
                out_ref[((at["z"] * 2 + at["x"]) * 2 + core) * 2 + seq] = ref[a, b]


def assemble(idx, pieces, order):
    shape = pieces[0].shape
    rows, cols = shape[-2:]
    out = pl.pallas_call(
        functools.partial(assemble_kernel, order=order),
        grid_spec=pltpu.PrefetchScalarGridSpec(
            num_scalar_prefetch=1,
            grid=(1,),
            in_specs=[pl.BlockSpec(shape, lambda i, idx: (0,) * 4)] * 4,
            out_specs=pl.BlockSpec((32, rows, cols), lambda i, idx: (0, 0, 0)),
        ),
        out_shape=jax.ShapeDtypeStruct((32, rows, cols), pieces[0].dtype),
        compiler_params=pltpu.CompilerParams(**PARAMS),
        name="assemble",
    )(idx, *pieces)
    return out.reshape(32 * rows, cols)


def body(
    block_input,
    cotangent,
    in_weight,
    dt_weight,
    out_weight,
    norm_gain,
    conv_weight,
    conv_bias,
    dt_bias,
    decay_log,
    skip_gain,
    gate_gain,
    in_left,
    in_right,
    in_left_root,
    in_right_root,
    dt_left,
    dt_right,
    dt_left_root,
    dt_right_root,
    out_left,
    out_right,
    out_left_root,
    out_right_root,
    vector_moment,
):
    seq_count, local_len, _ = block_input.shape
    seq_devices = lax.axis_size("seq")
    row_count = seq_count * local_len
    up = [(i, i + 1) for i in range(seq_devices - 1)]
    down = [(i + 1, i) for i in range(seq_devices - 1)]

    in_low = in_weight.astype(BF)
    dt_low = jnp.pad(dt_weight.astype(BF), ((0, 0), (0, 128 - HEADS)))
    main = lax.all_gather(
        jnp.concatenate([in_low[:, DI:], dt_low], axis=1), AXES, axis=0, tiled=True
    )
    part = jnp.arange(128)
    channel = jnp.arange(DI)
    emat = (
        ((part[:, None] % 32) == (channel[None, :] // HEADDIM)) & (part[:, None] < 96)
    ).astype(BF)
    gmat = ((channel[:, None] // HEADDIM) == part[None, :]).astype(BF)
    skip_wide = jnp.repeat(skip_gain, HEADDIM).reshape(1, DI)
    alog = jnp.pad(decay_log, (0, 128 - HEADS)).reshape(1, 128)
    dtb = jnp.pad(dt_bias, (0, 128 - HEADS), constant_values=-1e4).reshape(1, 128)
    cw8 = conv_weight
    gain8, cb8 = norm_gain.reshape(1, D), conv_bias.reshape(1, CONVCH)
    ggain8 = gate_gain.reshape(1, DI)
    tables = (emat, gmat, skip_wide, alog, dtb, cw8, gain8, cb8, ggain8)
    torus_sizes = tuple(lax.axis_size(a) for a in ("z", "x", "core", "seq"))
    direct = torus_sizes == (4, 2, 2, 2)
    idx = jnp.stack([lax.axis_index(a) for a in ("z", "x", "core", "seq")]).astype(jnp.int32)
    gate_low, out_low = in_low[:, :DI], out_weight.astype(BF)
    if direct:
        order = ("z", "x")
        gate_near = pick(gate_low.reshape(2, -1, DI), idx[3])
        out_near = pick(out_low.reshape(2, -1, D), idx[3])
        gate_near = around(around(gate_near, "z"), "x")
        out_near = around(around(out_near, "z"), "x")
        main = lax.optimization_barrier((main, gate_near, out_near) + tables)[0]
        gate_got = swapped(gate_near, "seq", 2, 1)
        out_got = swapped(out_near, "seq", 2, 1)
        gate_far = swapped(gate_near, "core", 2, 1)
        out_far = swapped(out_near, "core", 2, 1)
    else:
        wg = lax.all_gather(gate_low, AXES, axis=0, tiled=True)
        wo = lax.all_gather(out_low, AXES, axis=0, tiled=True)
    halo = lax.ppermute(block_input[:, local_len - 8 :, :], "seq", up)

    normed, mixed, pre, z, local_state, total = run_first(
        block_input, halo, gain8, main, cw8, cb8, dtb, alog, emat
    )
    span = jnp.repeat(jnp.exp(total[:, 0:1, :HEADS]), HEADDIM, axis=2)
    enter = lax.ppermute(local_state, "seq", up)
    for _ in range(seq_devices - 2):
        enter = lax.ppermute(local_state + span * enter, "seq", up)

    if direct:
        out_far_got = swapped(out_got, "core", 2, 1)
        gate_far_got = swapped(gate_got, "core", 2, 1)
        wo = assemble(idx, (out_near, out_got, out_far, out_far_got), order)
        wg = assemble(idx, (gate_near, gate_got, gate_far, gate_far_got), order)
    normed_rows = normed.reshape(row_count, D)
    upstream = cotangent.reshape(row_count, D)
    (
        block_output, branch, states_grad, gate_grad, states, rdot, local_dstate, row_sums,
    ) = run_second(
        pre, z, normed, upstream, block_input, enter, wg, wo, skip_wide, ggain8, alog,
        gmat,
    )
    leave = lax.ppermute(local_dstate, "seq", down)
    for _ in range(seq_devices - 2):
        leave = lax.ppermute(local_dstate + span * leave, "seq", down)

    out_partial = dot(branch, upstream, TN)
    gate_partial = dot(normed_rows, gate_grad, TN)
    if direct:
        gate_pair = core_exchange(gate_partial, idx[2])
        out_pair = core_exchange(out_partial, idx[2])
        early, early_own = chip_sum(idx, [gate_pair, out_pair])
        states_grad, early = lax.optimization_barrier((states_grad, early))
        early = lax.all_to_all(early, ("z", "x"), split_axis=0, concat_axis=0, tiled=True)

    mgrad, last8, first8, column_sums = run_third(
        pre, mixed, z, states_grad, states, rdot, leave, cw8, skip_wide, alog, gmat
    )
    near = lax.ppermute(first8, "seq", down)
    mgrad, extra = run_patch(mgrad, mixed, last8, near, cw8)
    conv_weight_grad = (column_sums + extra)[:KCONV]
    conv_bias_grad = column_sums[KCONV]

    mgrad_rows = mgrad.reshape(row_count, WIDE)
    mixed_local = dot(normed_rows, mgrad_rows, TN)
    input_grad, gain_rows = run_back(
        gate_grad, mgrad_rows, wg, main, block_input.reshape(row_count, D), upstream, gain8
    )
    input_grad = input_grad.reshape(block_input.shape)

    vector_local = jnp.concatenate(
        [
            gain_rows.sum(0),
            row_sums[0],
            conv_weight_grad.reshape(-1),
            conv_bias_grad,
            column_sums[5, :HEADS],
            -jnp.exp(decay_log) * column_sums[6, :HEADS],
            row_sums[1].reshape(HEADS, HEADDIM).sum(1),
        ]
    )
    if direct:
        mixed_pair = core_exchange(mixed_local, idx[2])
        late, late_own = chip_sum(idx, [mixed_pair])
        late = lax.all_to_all(late, ("z", "x"), split_axis=0, concat_axis=0, tiled=True)
        early_own = owner_sum(idx, early_own, early)
        early_own = early_own + swapped(early_own, "seq", 2, 1)
        share = D // 16
        gate_sum = early_own[:share]
        out_grad = jnp.concatenate([early_own[share:, :D], early_own[share:, D:]], axis=0)
        late_own = owner_sum(idx, late_own, late)
        mixed_sum = late_own + swapped(late_own, "seq", 2, 1)
    else:
        gate_sum = reduce_plain(core_sum(gate_partial))
        out_grad = reduce_split(core_sum(out_partial))
        mixed_sum = reduce_plain(core_sum(mixed_local))
    vector_rows = jnp.pad(vector_local, (0, -vector_local.shape[0] % 1024)).reshape(-1, 128)
    for axis in ("core", "seq", "x", "z"):
        if direct and axis == "x":
            vector_rows = lax.optimization_barrier((late, vector_rows))[1]
        vector_rows = xor_sum(vector_rows, axis)
    vector_grad = vector_rows.reshape(-1)[: vector_local.shape[0]]

    in_grad = jnp.concatenate([gate_sum, mixed_sum[:, :CONVCH]], axis=1)
    dt_grad = mixed_sum[:, CONVCH : CONVCH + HEADS]

    gate_tiles = kron_tiles(gate_sum, in_left, in_right, in_left_root, in_right_root, 0, 6)
    in_update, in_left_new, in_right_new = kron_tiles(
        mixed_sum[:, :CONVCH], in_left, in_right, in_left_root, in_right_root, DI // COL_BLOCK, 7,
        gate_tiles,
    )
    dt_update, dt_left_wide, dt_right_wide = kron_update(
        dt_grad, dt_left[:, None], dt_right[:, None], dt_left_root[:, None], dt_right_root[:, None]
    )
    out_update, out_left_new, out_right_new = kron_tiles(
        out_grad, out_left, out_right, out_left_root, out_right_root, 0, 3
    )
    vector_moment_new = 0.5 * vector_moment + 0.5 * vector_grad * vector_grad
    vector_update = -LR_VEC * vector_grad * lax.rsqrt(vector_moment_new)
    return (
        block_output,
        input_grad,
        in_grad,
        dt_grad,
        out_grad,
        in_update,
        dt_update,
        out_update,
        in_left_new,
        in_right_new,
        dt_left_wide[:, 0],
        dt_right_wide[:, 0],
        out_left_new,
        out_right_new,
        vector_grad,
        vector_moment_new,
        vector_update,
    )


def solution(mesh):
    dp, seq = mesh.shape["dp"], mesh.shape["seq"]
    split = (4, dp // 8, 2)
    torus = jax.sharding.Mesh(mesh.devices.reshape(split + (seq,)), AXES + ("seq",))
    tokens = P(AXES, "seq", None)
    rows = P(AXES, None)
    tri = P(AXES, None, None)
    quad = P(AXES, None, None, None)
    placed = (
        (tokens, tokens, rows, rows, rows) + (P(),) * 7 + (quad,) * 4 + (tri,) * 4 + (quad,) * 4 + (P(),)
    )

    return jax.shard_map(
        body,
        mesh=torus,
        in_specs=placed,
        out_specs=(tokens, tokens)
        + (rows,) * 6
        + (quad, quad, tri, tri, quad, quad)
        + (P(), P(), P()),
        check_vma=False,
    )
```
